128 devices in a mesh: req: 4 (over y), exp: 32 (over z, x, core).
Axes of the slice: x: 4, y: 4, z: 4, core: 2. Of those that a mesh axis runs over, the one named last changes fastest.
Arguments:
- queries: bfloat16 [16384, 2048], P(('req', 'exp')), may hold values from -128 to 128
- keys_then_values: bfloat16 [16384, 1024], P(('req', 'exp')), may hold values from -8 to 8
- residual: bfloat16 [16384, 2048], P(('req', 'exp')), may hold values from -6 to 6
- norm_gain: bfloat16 [2048], replicated, may hold values from 0.099609375 to 1.8984375
- prompt_lengths: int32 [4, 16], P('req'), may hold values from 1 to 3072, 4096 in all within a row
- expert_ids: int32 [16384, 6], P(('req', 'exp')), may hold values from 0 to 31, all different within a row; in each aligned block of 128 rows (0 to 127, 128 to 255, ...) at most 36 rows name the same one
- router_logits: float32 [16384, 6], P(('req', 'exp')), may hold values from -10 to 320
- w_gate: bfloat16 [32, 2048, 1408], P('exp'), may hold values from -0.125 to 0.125
- w_up: bfloat16 [32, 2048, 1408], P('exp'), may hold values from -0.125 to 0.125
- w_down: bfloat16 [32, 1408, 2048], P('exp'), may hold values from -0.15625 to 0.15625
- w_shared_gate: bfloat16 [2048, 2816], P('exp', 'req'), may hold values from -0.125 to 0.125
- w_shared_up: bfloat16 [2048, 2816], P('exp', 'req'), may hold values from -0.125 to 0.125
- w_shared_down: bfloat16 [2048, 2816], P('exp', 'req'), may hold values from -0.109375 to 0.109375
- page_table: int32 [4, 256], replicated, may hold values from 0 to 1023, as said below
Outputs:
- layer_out: bfloat16 [16384, 2048], P(('req', 'exp'))
- kv_cache: bfloat16 [1024, 16, 1024], P(('req', 'exp'))
- log_totals: float32 [16, 16384], P(None, ('req', 'exp'))
The draws below stay inside these ranges and needn't reach their ends.
Inputs may be any that keep to these rules, and one draw needn't show every extreme that they name: `expert_ids`: in the rows of one device no expert is named more than 36 times. `page_table`: the entries are a permutation of 0 to 1023. Entry [r, j] lies in the aligned block of 8 slots whose index modulo 256 // 8 equals j // 8; each aligned block of 8 entries of a row names exactly 2 slots in each aligned block of 256 slots.
All inputs are finite; a program needn't handle non-finite values.
Results may differ from the reference program's by a relative error of at most 0.0065.
Values may be sent and summed in bfloat16 or wider, within the bound.
A program may use at most 192 MiB of HBM per device.

```python
import math
import jax
import jax.numpy as jnp
import numpy as np
from jax import lax

D = 2048
QUERY_HEADS = 16
KEY_VALUE_HEADS = 4
HEAD_SIZE = 128
FF = 1408
TOPK = 6
PAGE = 16
NPROMPT = 16
TOK_DEV = 128
SFF = 2816
GROUPS = 4
EXPERTS = 32
G_TOK = 4096
TOKEN_TOTAL = 16384
MAXLEN = 3072
CAP = 36
PAGES_DEV = 8
PGROUP = 2
GPAGES = 256
N_EXP = 32


def value_offsets(key):
    phase_key = jax.random.fold_in(key, 53)
    phases = jax.random.uniform(phase_key, (1, KEY_VALUE_HEADS * HEAD_SIZE), jnp.float32, -3.14159, 3.14159)
    block_index = (jnp.arange(TOKEN_TOTAL) // 128).astype(jnp.float32)
    return 2.5 * jnp.cos(2.4 * block_index[:, None] + phases)


def attention_pair(key):
    base_key = jax.random.fold_in(key, 11)
    query_key, key_value_random = jax.random.split(base_key, 2)
    offsets = value_offsets(key)
    queries = jnp.clip(jax.random.normal(query_key, (TOKEN_TOTAL, QUERY_HEADS * HEAD_SIZE), jnp.float32), -6.0, 6.0)
    key_value_rows = jnp.clip(jax.random.normal(key_value_random, (TOKEN_TOTAL, 2 * KEY_VALUE_HEADS * HEAD_SIZE), jnp.float32), -6.0, 6.0)
    value_portion = key_value_rows[:, KEY_VALUE_HEADS * HEAD_SIZE:] + offsets
    key_value_rows = jnp.concatenate([key_value_rows[:, :KEY_VALUE_HEADS * HEAD_SIZE], value_portion], axis=1)
    key_value_rows = jnp.clip(key_value_rows, -8.0, 8.0)
    return (queries, key_value_rows)


def draw_queries(key, part):
    return attention_pair(key)[0].astype(jnp.bfloat16)


def draw_keys_then_values(key, part):
    return attention_pair(key)[1].astype(jnp.bfloat16)


def draw_router_logits(key, part):
    base_key = jax.random.fold_in(key, 23)
    first_key = jax.random.fold_in(base_key, 0)
    logits = jnp.clip(1.5 * jax.random.normal(first_key, (TOKEN_TOTAL, TOPK), jnp.float32), -9.0, 9.0)
    return logits


def draw_page_table(key, part):
    base_key = jax.random.fold_in(key, 37)
    source_key, dest_key = jax.random.split(base_key)
    columns = GPAGES // PAGES_DEV
    count_all = GROUPS * columns
    sigma = jax.vmap(lambda one_key: jax.random.permutation(one_key, PAGES_DEV))(jax.random.split(source_key, count_all))
    sigma = sigma.reshape(GROUPS, columns, PAGES_DEV)
    tau_perm = jax.vmap(lambda one_key: jax.random.permutation(one_key, PAGES_DEV))(jax.random.split(dest_key, count_all))
    tau_perm = tau_perm.reshape(GROUPS, columns, PAGES_DEV)
    dest_group = sigma % GROUPS
    order_in = sigma // GROUPS
    source_group = jnp.arange(GROUPS)[:, None, None]
    column_index = jnp.arange(columns)[None, :, None]
    incoming = source_group * PGROUP + order_in
    slot_in = tau_perm[dest_group, column_index, incoming]
    global_slot = dest_group * GPAGES + column_index * PAGES_DEV + slot_in
    return global_slot.reshape(GROUPS, GPAGES).astype(jnp.int32)


def steps_of(own_key, extent, cuts, low, largest):
    factor_of = 1.0
    for axis_at, shards_of in cuts:
        heights = jax.random.uniform(jax.random.fold_in(jax.random.fold_in(own_key, 6), axis_at), (shards_of,), jnp.float32, low / len(cuts), largest / len(cuts))
        factor_of = factor_of * jnp.repeat(jnp.exp(heights), extent[axis_at] // shards_of).reshape((-1,) + (1,) * (len(extent) - 1 - axis_at))
    return factor_of


def length_profile(number_of, total, bound, slope):
    loads = [(1 << 20) // math.isqrt(grade ** slope) + 1 for grade in range(2, number_of + 1)]
    rest, holding = total - bound - (number_of - 1), [1] * (number_of - 1)
    while rest > 0:
        free = [i for i in range(number_of - 1) if holding[i] < bound]
        whole, left = sum([loads[i] for i in free]), rest
        for i in free:
            extra = min(bound - holding[i], max(1, left * loads[i] // whole), rest)
            holding[i] = holding[i] + extra
            rest = rest - extra
    return np.array([bound] + holding)


def ragged(stream_key, count, total, limit, skew):
    if count == 2:
        one = jax.random.randint(stream_key, (), max(1, total - limit), min(limit, total - 1) + 1)
        return jnp.stack([one, total - one])
    sizes = jnp.asarray(length_profile(count, total, limit, skew), jnp.int32)
    couples = (count - 1) // 2
    source_of, receiver = sizes[1:1 + 2 * couples:2], sizes[2:2 + 2 * couples:2]
    margin = jnp.minimum(source_of - 1, limit - receiver)
    passed = jax.random.randint(jax.random.fold_in(stream_key, 1), (couples,), 0, 1 << 20) % (margin + 1)
    sizes = sizes.at[1:1 + 2 * couples:2].set(source_of - passed).at[2:2 + 2 * couples:2].set(receiver + passed)
    return sizes[jax.random.permutation(jax.random.fold_in(stream_key, 2), count)]


def deal_out(own_key, own, number, rows, count, top, reach, skew):
    sequence = jax.random.permutation(own_key, count)
    crowded, usual = portions_of(count, rows * top, reach, skew, True), portions_of(count, rows * top, reach, skew, False)
    places = jnp.arange(count)

    def named(sizes, rotation):
        used = int((sizes > 0).sum())
        fixed = max(1, used // 4)
        moved = fixed + (places - fixed + rotation * (used - fixed)) % max(1, count - fixed)
        return jnp.zeros((count,), jnp.int32).at[sequence[jnp.where(places < fixed, places, moved)]].set(jnp.asarray(sizes, jnp.int32))

    sizes = jnp.where(number % 4 == 0, named(crowded, number // 4), named(usual, number - number // 4 - 1))
    mixed = jax.random.permutation(jax.random.fold_in(own, 3), count)
    source_of, sink = mixed[0:count // 2 * 2:2], mixed[1:count // 2 * 2:2]
    slack = jnp.minimum(sizes[source_of] - 1, reach - sizes[sink]) // 2
    slack = jnp.where((source_of == sequence[0]) | (sink == sequence[0]) | (sizes[sink] == 0), 0, jnp.maximum(slack, 0))
    moved = jax.random.randint(jax.random.fold_in(own, 4), (count // 2,), 0, 1 << 20) % (slack + 1)
    sizes = sizes.at[source_of].add(-moved).at[sink].add(moved)
    items = jnp.searchsorted(jnp.cumsum(sizes), jnp.arange(rows * top), side="right").astype(jnp.int32)
    grid = items.reshape(top, rows).T
    grid = grid[jax.random.permutation(jax.random.fold_in(own, 1), rows)]
    rotation = jax.random.randint(jax.random.fold_in(own, 2), (rows, 1), 0, top)
    return jnp.take_along_axis(grid, (jnp.arange(top)[None, :] + rotation) % top, axis=1)


def portions_of(count, total, reach, slope, full):
    portions = [(1 << 20) // math.isqrt(standing ** slope) + 1 for standing in range(1, count + 1)]
    largest = reach if full else min(reach, max(-(-total // count), total * portions[0] // sum(portions)))
    least = 1 if total - largest >= count - 1 else 0
    given, spare = [largest] + [least] * (count - 1), total - largest - least * (count - 1)
    while spare > 0:
        movable = [i for i in range(1, count) if given[i] < largest] or [i for i in range(1, count) if given[i] < reach]
        mass, budget = sum([portions[i] for i in movable]), spare
        for i in movable:
            more = min(reach - given[i], max(1, budget * portions[i] // mass), spare)
            given[i] = given[i] + more
            spare = spare - more
    return np.array(given)


def scatter_about(own_key, shape, scale, limit, pieces=(), kind=jnp.bfloat16):
    values = jax.random.normal(own_key, shape, jnp.float32) * scale
    if len(pieces) > 0:
        values = steps_of(own_key, shape, pieces, -0.22, 0.18) * values
    return jnp.clip(values, min=-limit, max=limit).astype(kind)


def setup_inputs(seed: int = 0) -> dict:
    key_list = jax.random.split(jax.random.key(seed), 15)
    queries = draw_queries(jax.random.fold_in(key_list[14], 71), 0)
    keys_then_values = draw_keys_then_values(jax.random.fold_in(key_list[14], 71), 0)
    residual = scatter_about(key_list[2], (TOKEN_TOTAL, D), 1.0, 6.0, ((0, 128),))
    norm_gain = jnp.clip(1.0 + 0.18 * jax.random.normal(key_list[3], (D,), jnp.float32), 0.099609375, 1.8984375).astype(jnp.bfloat16)
    prompt_lengths = jax.vmap(lambda own: ragged(own, NPROMPT, G_TOK, MAXLEN, 2))(jax.random.split(key_list[4], GROUPS)).reshape((GROUPS, NPROMPT)).astype(jnp.int32)
    expert_ids_keys = jax.random.split(jax.random.fold_in(key_list[5], 1), TOKEN_TOTAL // TOK_DEV)
    expert_ids_turns = jax.random.permutation(jax.random.fold_in(key_list[5], 3), TOKEN_TOTAL // TOK_DEV)
    expert_ids = jax.vmap(lambda own, number: deal_out(jax.random.fold_in(key_list[5], 2), own, number, TOK_DEV, EXPERTS, TOPK, CAP, 2))(expert_ids_keys, expert_ids_turns).reshape((TOKEN_TOTAL, TOPK))
    router_logits = draw_router_logits(jax.random.fold_in(key_list[14], 71), 0)
    w_gate = scatter_about(key_list[7], (EXPERTS, D, FF), D ** -0.5, 0.125, ((0, 32),))
    w_up = scatter_about(key_list[8], (EXPERTS, D, FF), D ** -0.5, 0.125, ((0, 32),))
    w_down = scatter_about(key_list[9], (EXPERTS, FF, D), FF ** -0.5, 0.15625, ((0, 32),))
    w_shared_gate = scatter_about(key_list[10], (D, SFF), D ** -0.5, 0.125, ((0, 32), (1, 4)))
    w_shared_up = scatter_about(key_list[11], (D, SFF), D ** -0.5, 0.125, ((0, 32), (1, 4)))
    w_shared_down = scatter_about(key_list[12], (D, SFF), SFF ** -0.5, 0.109375, ((0, 32), (1, 4)))
    page_table = draw_page_table(jax.random.fold_in(key_list[14], 71), 0)
    return dict(queries=queries, keys_then_values=keys_then_values, residual=residual, norm_gain=norm_gain, prompt_lengths=prompt_lengths, expert_ids=expert_ids, router_logits=router_logits, w_gate=w_gate, w_up=w_up, w_down=w_down, w_shared_gate=w_shared_gate, w_shared_up=w_shared_up, w_shared_down=w_shared_down, page_table=page_table)


large_negative = -1e+30
eps_norm = 1e-06

def segment_ids(positions, prompt_ends):
    return lax.optimization_barrier(jnp.sum((positions[:, None] >= prompt_ends[None, :]).astype(jnp.int32), axis=1))

def group_attention(queries, keys_then_values, lengths):
    group_row_block = queries.shape[0]
    heads_per_group = QUERY_HEADS // KEY_VALUE_HEADS
    query_everything = queries.reshape(group_row_block, KEY_VALUE_HEADS, heads_per_group, HEAD_SIZE)
    key_row_block = keys_then_values[:, :KEY_VALUE_HEADS * HEAD_SIZE].reshape(group_row_block, KEY_VALUE_HEADS, HEAD_SIZE).astype(jnp.float32)
    value_row_block = keys_then_values[:, KEY_VALUE_HEADS * HEAD_SIZE:].reshape(group_row_block, KEY_VALUE_HEADS, HEAD_SIZE).astype(jnp.float32)
    prompt_ends = jnp.cumsum(lengths).astype(jnp.int32)
    key_pos = jnp.arange(group_row_block, dtype=jnp.int32)
    key_seg = segment_ids(key_pos, prompt_ends)
    block_rows = math.gcd(group_row_block, 512)

    def one_block(block_index):
        begin_at = (block_index * block_rows).astype(jnp.int32)
        query_block = lax.dynamic_slice_in_dim(query_everything, begin_at, block_rows, 0).astype(jnp.float32)
        query_pos = begin_at + jnp.arange(block_rows, dtype=jnp.int32)
        query_seg = segment_ids(query_pos, prompt_ends)
        scores = jnp.einsum('qhgd,khd->hgqk', query_block, key_row_block) * HEAD_SIZE ** (-0.5)
        visible = (key_pos[None, :] <= query_pos[:, None]) & (key_seg[None, :] == query_seg[:, None])
        scores = jnp.where(visible, scores, large_negative)
        row_max = lax.optimization_barrier(jnp.max(scores, axis=3, keepdims=True))
        exp_terms = jnp.where(visible, jnp.exp(scores - row_max), 0.0)
        row_total = lax.optimization_barrier(jnp.sum(exp_terms, axis=3))
        rounded = lax.optimization_barrier(exp_terms.astype(jnp.bfloat16)).astype(jnp.float32)
        mixed_heads = jnp.einsum('hgqk,khd->hgqd', rounded, value_row_block) / row_total[..., None]
        log_block = (row_max[..., 0] + jnp.log(row_total)).reshape(QUERY_HEADS, block_rows)
        return (jnp.transpose(mixed_heads, (2, 0, 1, 3)).reshape(block_rows, QUERY_HEADS * HEAD_SIZE).astype(jnp.bfloat16), log_block)
    blocks, log_blocks = lax.map(one_block, jnp.arange(group_row_block // block_rows, dtype=jnp.int32))
    log_group = jnp.transpose(log_blocks, (1, 0, 2)).reshape(QUERY_HEADS, group_row_block)
    return (blocks.reshape(group_row_block, QUERY_HEADS * HEAD_SIZE), log_group)

def reference(queries, keys_then_values, residual, norm_gain, prompt_lengths, expert_ids, router_logits, w_gate, w_up, w_down, w_shared_gate, w_shared_up, w_shared_down, page_table):
    group_row_block = TOK_DEV * N_EXP
    pieces_all = []
    log_pieces = []
    for group_index in range(GROUPS):
        lower = group_index * group_row_block
        upper = lower + group_row_block
        mixed_group, log_group = group_attention(queries[lower:upper], keys_then_values[lower:upper], prompt_lengths[group_index])
        pieces_all.append(mixed_group)
        log_pieces.append(log_group)
    attention = jnp.concatenate(pieces_all, axis=0)
    log_totals = jnp.concatenate(log_pieces, axis=1)
    hidden = residual.astype(jnp.float32) + attention.astype(jnp.float32)
    scale_rows = lax.rsqrt(lax.optimization_barrier(jnp.mean(hidden * hidden, axis=-1, keepdims=True)) + eps_norm)
    normed = (hidden * scale_rows * norm_gain.astype(jnp.float32)).astype(jnp.bfloat16)
    route_weights = jax.nn.softmax(router_logits.astype(jnp.float32), axis=-1)
    flat_ids = expert_ids.reshape(-1)
    flat_weights = jnp.concatenate([route_weights.reshape(-1), jnp.zeros((1,), jnp.float32)])
    normed_pad = jnp.concatenate([normed, jnp.zeros((1, D), jnp.bfloat16)], axis=0)
    most_rows = GROUPS * N_EXP * CAP

    def one_expert(mix_total, expert_index):
        pick_rows = jnp.nonzero(flat_ids == expert_index, size=most_rows, fill_value=TOKEN_TOTAL * TOPK)[0].astype(jnp.int32)
        token_index = pick_rows // TOPK
        inputs = normed_pad[token_index]
        gate_out = jnp.dot(inputs, w_gate[expert_index], preferred_element_type=jnp.float32)
        up_out = jnp.dot(inputs, w_up[expert_index], preferred_element_type=jnp.float32)
        activated = (jax.nn.silu(gate_out) * up_out).astype(jnp.bfloat16)
        expert_out = jnp.dot(activated, w_down[expert_index], preferred_element_type=jnp.float32).astype(jnp.bfloat16)
        mix_total = mix_total.at[token_index].add(flat_weights[pick_rows][:, None] * expert_out.astype(jnp.float32), mode='drop')
        return (mix_total, None)
    mix_total, _ = lax.scan(one_expert, jnp.zeros((TOKEN_TOTAL, D), jnp.float32), jnp.arange(EXPERTS, dtype=jnp.int32))
    shared_gate = jnp.dot(normed, w_shared_gate, preferred_element_type=jnp.float32)
    shared_up = jnp.dot(normed, w_shared_up, preferred_element_type=jnp.float32)
    shared_act = (jax.nn.silu(shared_gate) * shared_up).astype(jnp.bfloat16)
    shared_out = jnp.dot(shared_act, jnp.transpose(w_shared_down), preferred_element_type=jnp.float32).astype(jnp.bfloat16)
    layer_out = (hidden + mix_total + shared_out.astype(jnp.float32)).astype(jnp.bfloat16)
    key_value_width = 2 * KEY_VALUE_HEADS * HEAD_SIZE
    kv_pages = keys_then_values.reshape(GROUPS * GPAGES, PAGE, key_value_width)
    kv_cache = jnp.zeros((GROUPS * GPAGES, PAGE, key_value_width), jnp.bfloat16).at[page_table.reshape(-1)].set(kv_pages)
    return (layer_out, kv_cache, log_totals)
```

```python
import functools

import jax
import jax.numpy as jnp
from jax import lax
from jax.experimental import pallas as pl
from jax.experimental.pallas import tpu as pltpu
from jax.sharding import PartitionSpec as P

D = 2048
QUERY_HEADS = 16
KEY_VALUE_HEADS = 4
HEAD_SIZE = 128
FF = 1408
TOPK = 6
PAGE = 16
CAP = 36
TOK = 128
SPAD = 768
MAXLEN = 3072
eps_norm = 1e-06
MESH = pl.DeviceIdType.MESH
CODES = (0, 1, -1, 2)
ANY = pl.BlockSpec(memory_space=pl.ANY)
VM = pl.BlockSpec(memory_space=pltpu.VMEM)
SM = pl.BlockSpec(memory_space=pltpu.SMEM)
F32 = jnp.float32
BF16 = jnp.bfloat16
VMEM_LIMIT = 62 * 1024 * 1024


class Place:
    def __init__(self):
        c = lax.axis_index("exp")
        self.c = c
        self.r = lax.axis_index("req")
        self.z = c // 8
        self.x = lax.rem(c // 2, 4)
        self.k = lax.rem(c, 2)
        self.partner = c + 1 - 2 * self.k

    def at(self, dx, dz):
        return lax.rem(self.z + dz + 4, 4) * 8 + lax.rem(self.x + dx + 4, 4) * 2 + self.k

    def step(self, dim, s):
        return self.at(s, 0) if dim == "x" else self.at(0, s)

    def up(self, s):
        return lax.rem(self.r + s + 4, 4)

    def barrier(self, along_y):
        sem = pltpu.get_barrier_semaphore()
        peers = [self.at(1, 0), self.at(-1, 0), self.at(0, 1), self.at(0, -1), self.partner]
        for p in peers:
            pl.semaphore_signal(sem, inc=1, device_id={"exp": p}, device_id_type=MESH)
        for s in along_y:
            pl.semaphore_signal(sem, inc=1, device_id={"req": self.up(s)}, device_id_type=MESH)
        pl.semaphore_wait(sem, len(peers) + len(along_y))


def route(q):
    first, second = ("x", "z") if q < 2 else ("z", "x")
    return first, second, (1 if q % 2 == 0 else -1)


def shift(q, a, b):
    first, _, t = route(q)
    u, v = CODES[a] * t, CODES[b] * t
    return (u, v) if first == "x" else (v, u)


def hop(code, t):
    return -t if code == 2 else t


def depth(a, b):
    return abs(CODES[a]) + abs(CODES[b])


def children(q, a, b):
    first, second, t = route(q)
    out = []
    if b == 0:
        if a == 0:
            out += [(first, t, 1, 0), (first, -t, 2, 0)]
        elif a == 1:
            out += [(first, t, 3, 0)]
        out += [(second, t, a, 1), (second, -t, a, 2)]
    elif b == 1:
        out += [(second, t, a, 3)]
    return out


class Gather:
    def __init__(self, place, own, every, rows, pieces, send_sem, recv_sem, pair_sem):
        self.p, self.own, self.every, self.rows, self.pieces = place, own, every, rows, pieces
        self.rq = rows // pieces
        self.send_sem, self.recv_sem, self.pair_sem = send_sem, recv_sem, pair_sem

    def slot(self, src, q):
        return self.every.at[pl.ds(pl.multiple_of(src * self.rows + q * self.rq, self.rq), self.rq)]

    def block(self, src):
        return self.every.at[pl.ds(pl.multiple_of(src * self.rows, self.rows), self.rows)]

    def source(self, q, a, b):
        dx, dz = shift(q, a, b)
        return self.p.at(-dx, -dz)

    def recv_of(self, q, a, b):
        return self.recv_sem.at[q * 15 + a * 4 + b - 1]

    def pass_on(self, q, a, b):
        src = self.source(q, a, b)
        ref = self.own.at[pl.ds(q * self.rq, self.rq)] if a == 0 and b == 0 else self.slot(src, q)
        for dim, s, na, nb in children(q, a, b):
            pltpu.make_async_remote_copy(
                ref, self.slot(src, q), self.send_sem, self.recv_of(q, na, nb),
                device_id={"exp": self.p.step(dim, s)}, device_id_type=MESH,
            ).start()

    def to_pair(self, ref, dst):
        pltpu.make_async_remote_copy(
            ref, dst, self.send_sem, self.pair_sem,
            device_id={"exp": self.p.partner}, device_id_type=MESH,
        ).start()

    def start(self):
        for q in range(self.pieces):
            self.pass_on(q, 0, 0)
        self.to_pair(self.own, self.block(self.p.c))

    def events(self):
        out = []
        for q in range(self.pieces):
            for a in range(4):
                for b in range(4):
                    if a or b:
                        out.append((depth(a, b), b, a, q))
        return sorted(out)

    def take(self, ev):
        _, b, a, q = ev
        ref = self.slot(self.source(q, a, b), q)
        pltpu.make_async_remote_copy(
            ref, ref, self.send_sem, self.recv_of(q, a, b),
            device_id={"exp": self.p.partner}, device_id_type=MESH,
        ).wait_recv()
        self.pass_on(q, a, b)
        self.to_pair(ref, ref)

    def wait_pair(self):
        ref = self.every.at[pl.ds(0, 16 * self.rows)]
        pltpu.make_async_remote_copy(
            ref, ref, self.send_sem, self.pair_sem,
            device_id={"exp": self.p.partner}, device_id_type=MESH,
        ).wait_recv()

    def drain(self):
        ref = self.every.at[pl.ds(0, 31 * self.rows)]
        pltpu.make_async_copy(ref, ref, self.send_sem).wait()


class RingY:
    def __init__(self, place, own, every, rows, send_sem, recv_sem):
        self.p, self.own, self.every, self.rows = place, own, every, rows
        self.h = rows // 2
        self.send_sem, self.recv_sem = send_sem, recv_sem

    def slot(self, src, q):
        return self.every.at[pl.ds(pl.multiple_of(src * self.rows + q * self.h, self.h), self.h)]

    def send(self, ref, src, q, s, code):
        pltpu.make_async_remote_copy(
            ref, self.slot(src, q), self.send_sem, self.recv_sem.at[q * 3 + code - 1],
            device_id={"req": self.p.up(s)}, device_id_type=MESH,
        ).start()

    def start(self):
        for q, t in ((0, 1), (1, -1)):
            ref = self.own.at[pl.ds(q * self.h, self.h)]
            self.send(ref, self.p.r, q, t, 1)
            self.send(ref, self.p.r, q, -t, 2)

    def finish(self):
        for code in (1, 2, 3):
            for q, t in ((0, 1), (1, -1)):
                src = self.p.up(-CODES[code] * t)
                ref = self.slot(src, q)
                pltpu.make_async_remote_copy(
                    ref, ref, self.send_sem, self.recv_sem.at[q * 3 + code - 1],
                    device_id={"req": self.p.up(1)}, device_id_type=MESH,
                ).wait_recv()
                if code == 1:
                    self.send(ref, src, q, t, 3)

    def drain(self):
        ref = self.every.at[pl.ds(0, 3 * self.rows)]
        pltpu.make_async_copy(ref, ref, self.send_sem).wait()


def kernel_gather(kv_ref, w_ref, meta_ref, kv_all, w_all, meta_all, pg_all,
                  kv_r, w_r, meta_r, pg_r, send, pair, local):
    p = Place()
    p.barrier((1, -1))
    kv = Gather(p, kv_ref, kv_all, TOK, 4, send.at[0], kv_r, pair.at[0])
    w = Gather(p, w_ref, w_all, 64, 4, send.at[1], w_r, pair.at[1])
    meta = Gather(p, meta_ref, meta_all, 16, 1, send.at[2], meta_r, pair.at[2])
    pages = RingY(p, kv_ref, pg_all, TOK, send.at[3], pg_r)
    owns = [pltpu.make_async_copy(g.own, g.block(p.c), local.at[i]) for i, g in enumerate((kv, w, meta))]
    owns.append(pltpu.make_async_copy(kv_ref, pg_all.at[pl.ds(pl.multiple_of(p.r * TOK, TOK), TOK)], local.at[3]))
    meta.start()
    kv.start()
    pages.start()
    for c in owns:
        c.start()
    evs = kv.events()
    for ev in evs[:16]:
        kv.take(ev)
    w.start()
    for ev in evs[16:]:
        kv.take(ev)
    for ev in meta.events():
        meta.take(ev)
    pages.finish()
    for ev in w.events():
        w.take(ev)
    for g in (kv, w, meta):
        g.wait_pair()
        g.drain()
    pages.drain()
    for c in owns:
        c.wait()


def call_gather(kv, wcat, meta):
    return pl.pallas_call(
        kernel_gather,
        out_shape=(
            jax.ShapeDtypeStruct((32 * TOK, 1024), BF16),
            jax.ShapeDtypeStruct((D, 3 * SPAD), BF16),
            jax.ShapeDtypeStruct((512, 128), F32),
            jax.ShapeDtypeStruct((512, 1024), BF16),
        ),
        in_specs=[VM] * 3,
        out_specs=(ANY,) * 4,
        scratch_shapes=[
            pltpu.SemaphoreType.DMA((60,)),
            pltpu.SemaphoreType.DMA((60,)),
            pltpu.SemaphoreType.DMA((15,)),
            pltpu.SemaphoreType.DMA((6,)),
            pltpu.SemaphoreType.DMA((4,)),
            pltpu.SemaphoreType.DMA((3,)),
            pltpu.SemaphoreType.DMA((4,)),
        ],
        compiler_params=pltpu.CompilerParams(collective_id=0, has_side_effects=True, vmem_limit_bytes=VMEM_LIMIT),
        name="gather_start",
    )(kv, wcat, meta)


def kernel_rows(n_ref, n_all, y_all, n_r, y_r, send, pair, local):
    p = Place()
    p.barrier((1, -1))
    g = Gather(p, n_ref, n_all, TOK, 4, send.at[0], n_r, pair.at[0])
    y = RingY(p, n_ref, y_all, TOK, send.at[1], y_r)
    owns = [
        pltpu.make_async_copy(n_ref, g.block(p.c), local.at[0]),
        pltpu.make_async_copy(n_ref, y_all.at[pl.ds(pl.multiple_of(p.r * TOK, TOK), TOK)], local.at[1]),
    ]
    g.start()
    y.start()
    for c in owns:
        c.start()
    evs = g.events()
    for ev in evs[:32]:
        g.take(ev)
    y.finish()
    for ev in evs[32:]:
        g.take(ev)
    g.wait_pair()
    g.drain()
    y.drain()
    for c in owns:
        c.wait()


def call_rows(normed):
    return pl.pallas_call(
        kernel_rows,
        out_shape=(
            jax.ShapeDtypeStruct((32 * TOK, D), BF16),
            jax.ShapeDtypeStruct((512, D), BF16),
        ),
        in_specs=[VM],
        out_specs=(ANY, ANY),
        scratch_shapes=[
            pltpu.SemaphoreType.DMA((60,)),
            pltpu.SemaphoreType.DMA((6,)),
            pltpu.SemaphoreType.DMA((2,)),
            pltpu.SemaphoreType.DMA((1,)),
            pltpu.SemaphoreType.DMA((2,)),
        ],
        compiler_params=pltpu.CompilerParams(collective_id=1, has_side_effects=True, vmem_limit_bytes=VMEM_LIMIT),
        name="gather_rows",
    )(normed)


def attend(c, q_ref, kv_ref, ends_ref, res_ref, gain_ref, hid_ref, normed_ref, lt_ref,
           qs, m_s, l_s, acc_s, lt_s):
    rows = 4 * TOK
    for h in range(QUERY_HEADS):
        qs[pl.ds(h * TOK, TOK), :] = q_ref[:, h * HEAD_SIZE:(h + 1) * HEAD_SIZE]
    qpos = c * TOK + lax.broadcasted_iota(jnp.int32, (TOK, 128), 0)
    ends = jnp.broadcast_to(ends_ref[...], (TOK, 128))
    begin = jnp.max(jnp.where(ends <= qpos, ends, 0).astype(F32), axis=1, keepdims=True).astype(jnp.int32)
    m_s[...] = jnp.full_like(m_s, -5e29)
    l_s[...] = jnp.zeros_like(l_s)
    acc_s[...] = jnp.zeros_like(acc_s)
    lt_s[...] = jnp.zeros_like(lt_s)
    first = jnp.maximum(c * TOK - MAXLEN, 0) // 256
    last = c // 2

    def chunk(i, _):
        k0 = pl.multiple_of(i * 256, 256)
        kpos = k0 + lax.broadcasted_iota(jnp.int32, (TOK, 256), 1)
        qp = c * TOK + lax.broadcasted_iota(jnp.int32, (TOK, 256), 0)
        seen = (kpos >= begin) & (kpos <= qp)
        bias = jnp.where(seen, 0.0, -1e30).astype(F32)
        bias = jnp.concatenate([bias] * 4, axis=0)
        for g in range(KEY_VALUE_HEADS):
            at = pl.ds(g * rows, rows)
            keys = kv_ref[pl.ds(k0, 256), g * HEAD_SIZE:(g + 1) * HEAD_SIZE]
            values = kv_ref[pl.ds(k0, 256), 512 + g * HEAD_SIZE:512 + (g + 1) * HEAD_SIZE]
            s = lax.dot_general(qs[at, :], keys, (((1,), (1,)), ((), ())), preferred_element_type=F32)
            s = s * HEAD_SIZE ** (-0.5) + bias
            old = m_s[at, :]
            new = jnp.maximum(old, jnp.max(s, axis=1, keepdims=True))
            e = jnp.exp(s - new)
            alpha = jnp.exp(old - new)
            m_s[at, :] = new
            l_s[at, :] = l_s[at, :] * alpha + jnp.sum(e, axis=1, keepdims=True)
            acc_s[at, :] = acc_s[at, :] * alpha + jnp.dot(e.astype(BF16), values, preferred_element_type=F32)
        return 0

    lax.fori_loop(first, last + 1, chunk, 0)
    total = jnp.zeros((TOK, 1), F32)
    for h in range(QUERY_HEADS):
        at = pl.ds(h * TOK, TOK)
        cols = slice(h * HEAD_SIZE, (h + 1) * HEAD_SIZE)
        att = (acc_s[at, :] / l_s[at, :]).astype(BF16)
        lt_s[:, h:h + 1] = m_s[at, :] + jnp.log(l_s[at, :])
        hid = res_ref[:, cols].astype(F32) + att.astype(F32)
        hid_ref[:, cols] = hid
        total = total + jnp.sum(hid * hid, axis=1, keepdims=True)
    scale = lax.rsqrt(total * (1.0 / D) + eps_norm)
    for h in range(QUERY_HEADS):
        cols = slice(h * HEAD_SIZE, (h + 1) * HEAD_SIZE)
        normed_ref[:, cols] = (hid_ref[:, cols] * scale * gain_ref[:, cols].astype(F32)).astype(BF16)
    lt_ref[...] = jnp.transpose(lt_s[...])[:QUERY_HEADS, :]


def kernel_attend(inv_ref, q_ref, kv_ref, ends_ref, res_ref, gain_ref, pg_ref,
                  hid_ref, normed_ref, lt_ref, cache_ref, qs, m_s, l_s, acc_s, lt_s, sem):
    copies = []
    for i in range(8):
        copies.append(pltpu.make_async_copy(pg_ref.at[inv_ref[0, i]], cache_ref.at[i], sem.at[i]))
        copies[-1].start()
    attend(lax.axis_index("exp"), q_ref, kv_ref, ends_ref, res_ref, gain_ref, hid_ref, normed_ref, lt_ref,
           qs, m_s, l_s, acc_s, lt_s)
    for c in copies:
        c.wait()


def attend_scratch():
    n = QUERY_HEADS * TOK
    return [
        pltpu.VMEM((n, HEAD_SIZE), BF16),
        pltpu.VMEM((n, 1), F32),
        pltpu.VMEM((n, 1), F32),
        pltpu.VMEM((n, HEAD_SIZE), F32),
        pltpu.VMEM((TOK, 128), F32),
    ]


def call_attend(inv, q, kv_all, ends, res, gain, pg_all):
    return pl.pallas_call(
        kernel_attend,
        out_shape=(
            jax.ShapeDtypeStruct((TOK, D), F32),
            jax.ShapeDtypeStruct((TOK, D), BF16),
            jax.ShapeDtypeStruct((QUERY_HEADS, TOK), F32),
            jax.ShapeDtypeStruct((8, PAGE, 1024), BF16),
        ),
        in_specs=[SM, VM, VM, VM, VM, VM, ANY],
        out_specs=(VM, VM, VM, VM),
        scratch_shapes=attend_scratch() + [pltpu.SemaphoreType.DMA((8,))],
        compiler_params=pltpu.CompilerParams(vmem_limit_bytes=VMEM_LIMIT),
        name="attend",
    )(inv, q, kv_all, ends, res, gain, pg_all.reshape(32, PAGE, 1024))


def silu_mul(g, u):
    return (g / (1.0 + jnp.exp(-g)) * u).astype(BF16)


def shared_part(rows_ref, w_ref, act_s, out_ref):
    def up(j, _):
        col = pl.multiple_of(j * 256, 256)
        g = jnp.dot(rows_ref[...], w_ref[:, pl.ds(col, 256)], preferred_element_type=F32)
        u = jnp.dot(rows_ref[...], w_ref[:, pl.ds(SPAD + col, 256)], preferred_element_type=F32)
        act_s[:, pl.ds(col, 256)] = silu_mul(g, u)
        return 0

    lax.fori_loop(0, 3, up, 0)

    def down(j, _):
        col = pl.multiple_of(j * 256, 256)
        o = lax.dot_general(act_s[...], w_ref[pl.ds(col, 256), 2 * SPAD:], (((1,), (1,)), ((), ())),
                            preferred_element_type=F32)
        out_ref[:, pl.ds(col, 256)] = o.astype(BF16)
        return 0

    lax.fori_loop(0, 8, down, 0)


def kernel_shared(rows_ref, w_ref, out_ref, act_s):
    shared_part(rows_ref, w_ref, act_s, out_ref)


def call_shared(rows, w_all):
    return pl.pallas_call(
        kernel_shared,
        out_shape=jax.ShapeDtypeStruct((512, D), BF16),
        in_specs=[VM, VM],
        out_specs=VM,
        scratch_shapes=[pltpu.VMEM((512, SPAD), BF16)],
        compiler_params=pltpu.CompilerParams(vmem_limit_bytes=VMEM_LIMIT),
        name="shared",
    )(rows, w_all)


def plan_rows(e, meta_ref, tgt_s, wt_s):
    tgt_s[...] = jnp.zeros_like(tgt_s)
    for s in range(32):
        ids = meta_ref[pl.ds(s * 16, 8), :]
        wts = meta_ref[pl.ds(s * 16 + 8, 8), :]
        hit = jnp.where(ids == e, 1.0, 0.0).astype(F32)
        tgt_s[s:s + 1, :] = jnp.sum(hit, axis=0, keepdims=True)
        wt_s[s:s + 1, :] = jnp.sum(hit * wts, axis=0, keepdims=True)
    sel = tgt_s[...]
    i0 = lax.broadcasted_iota(jnp.int32, (128, 128), 0)
    i1 = lax.broadcasted_iota(jnp.int32, (128, 128), 1)
    tri = jnp.where(i0 <= i1, 1.0, 0.0).astype(BF16)
    rank = jnp.dot(sel.astype(BF16), tri, preferred_element_type=F32)
    src = lax.rem(lax.broadcasted_iota(jnp.int32, (32, 128), 0), 4).astype(F32)
    tgt_s[...] = jnp.where(sel > 0.5, src * CAP + rank - 1.0, -1.0)


def pick(tgt_s, wt_s, s0):
    t4 = tgt_s[s0:s0 + 4, :]
    w4 = wt_s[s0:s0 + 4, :]
    trow = jnp.concatenate([t4[i:i + 1, :] for i in range(4)], axis=1)
    wrow = jnp.concatenate([w4[i:i + 1, :] for i in range(4)], axis=1)
    lane = lax.broadcasted_iota(jnp.int32, (4 * CAP, 512), 0).astype(F32)
    hit = lane == trow
    return jnp.where(hit, 1.0, 0.0).astype(BF16), jnp.sum(jnp.where(hit, wrow, 0.0), axis=1, keepdims=True)


def expert_up(x_s, wg, wu, act_s):
    def tile(col, n):
        g = jnp.dot(x_s[...], wg[:, pl.ds(col, n)], preferred_element_type=F32)
        u = jnp.dot(x_s[...], wu[:, pl.ds(col, n)], preferred_element_type=F32)
        act_s[:, pl.ds(col, n)] = silu_mul(g, u)

    def body(j, _):
        tile(pl.multiple_of(j * 256, 256), 256)
        return 0

    lax.fori_loop(0, 5, body, 0)
    tile(1280, 128)


def expert_down(act_s, wd, wcol, y_s):
    def body(j, _):
        col = pl.multiple_of(j * 256, 256)
        o = jnp.dot(act_s[...], wd[:, pl.ds(col, 256)], preferred_element_type=F32)
        y_s[:, pl.ds(col, 256)] = (o * wcol).astype(BF16)
        return 0

    lax.fori_loop(0, 8, body, 0)


def kernel_expert(meta_ref, n_all, wg_h, wu_h, wd_h, out,
                  wg, wu, wd, rows_s, x_s, act_s, y_s, o_s, tgt_s, wt_s, w_sem, in_sem, out_sem):
    e = lax.axis_index("exp").astype(F32)
    loads = [pltpu.make_async_copy(n_all.at[pl.ds(i * 1024, 1024)], rows_s.at[i % 2], in_sem.at[i % 2]) for i in range(4)]
    stores = [pltpu.make_async_copy(o_s.at[i % 2], out.at[pl.ds(i * 1024, 1024)], out_sem.at[i % 2]) for i in range(4)]
    ws = [pltpu.make_async_copy(a.at[0], b, w_sem.at[i]) for i, (a, b) in enumerate(((wg_h, wg), (wu_h, wu), (wd_h, wd)))]
    loads[0].start()
    for w in ws:
        w.start()
    plan_rows(e, meta_ref, tgt_s, wt_s)
    for i in range(4):
        if i + 1 < 4:
            loads[i + 1].start()
        loads[i].wait()
        hits, wcols = [], []
        for j in range(2):
            hit, wcol = pick(tgt_s, wt_s, i * 8 + j * 4)
            hits.append(hit)
            wcols.append(wcol)

            def fetch(n, _, j=j, hit=hit, i=i):
                col = pl.multiple_of(n * 256, 256)
                x_s[pl.ds(j * 144, 144), pl.ds(col, 256)] = jnp.dot(
                    hit, rows_s[i % 2, pl.ds(j * 512, 512), pl.ds(col, 256)], preferred_element_type=F32).astype(BF16)
                return 0

            lax.fori_loop(0, 8, fetch, 0)
        if i == 0:
            ws[0].wait()
            ws[1].wait()
        expert_up(x_s, wg, wu, act_s)
        if i == 0:
            ws[2].wait()
        expert_down(act_s, wd, jnp.concatenate(wcols, axis=0), y_s)
        if i >= 2:
            stores[i - 2].wait()
        for j in range(2):
            def put(n, _, j=j, hit=hits[j], i=i):
                col = pl.multiple_of(n * 256, 256)
                o_s[i % 2, pl.ds(j * 512, 512), pl.ds(col, 256)] = lax.dot_general(
                    hit, y_s[pl.ds(j * 144, 144), pl.ds(col, 256)], (((0,), (0,)), ((), ())),
                    preferred_element_type=F32).astype(BF16)
                return 0

            lax.fori_loop(0, 8, put, 0)
        stores[i].start()
    stores[2].wait()
    stores[3].wait()


def call_expert(meta_all, n_all, wg, wu, wd):
    return pl.pallas_call(
        kernel_expert,
        out_shape=jax.ShapeDtypeStruct((32 * TOK, D), BF16),
        in_specs=[VM, ANY, ANY, ANY, ANY],
        out_specs=ANY,
        scratch_shapes=[
            pltpu.VMEM((D, FF), BF16),
            pltpu.VMEM((D, FF), BF16),
            pltpu.VMEM((FF, D), BF16),
            pltpu.VMEM((2, 1024, D), BF16),
            pltpu.VMEM((8 * CAP, D), BF16),
            pltpu.VMEM((8 * CAP, FF), BF16),
            pltpu.VMEM((8 * CAP, D), BF16),
            pltpu.VMEM((2, 1024, D), BF16),
            pltpu.VMEM((32, 128), F32),
            pltpu.VMEM((32, 128), F32),
            pltpu.SemaphoreType.DMA((3,)),
            pltpu.SemaphoreType.DMA((2,)),
            pltpu.SemaphoreType.DMA((2,)),
        ],
        compiler_params=pltpu.CompilerParams(vmem_limit_bytes=VMEM_LIMIT),
        name="expert",
    )(meta_all, n_all, wg, wu, wd)


def kernel_return(hid_ref, parts, sh, out_ref, mine, pair, rbuf, shbuf, load_sem, pair_sem, recv_sem,
                  sh_recv, send):
    p = Place()
    p.barrier((1, -1, 2))
    offs = sorted(((dx, dz) for dx in CODES for dz in CODES), key=lambda o: -abs(o[0]) - abs(o[1]))

    def blk(dev):
        return parts.at[pl.ds(pl.multiple_of(dev * TOK, TOK), TOK)]

    loads, pairs = {}, {}
    for j, (dx, dz) in enumerate(offs):
        dest = p.at(-dx, -dz)
        other = dest + 1 - 2 * p.k
        loads[dx, dz] = pltpu.make_async_copy(blk(dest), mine.at[j], load_sem.at[j])
        pairs[dx, dz] = pltpu.make_async_remote_copy(
            blk(other), pair.at[j], send.at[0], pair_sem.at[j],
            device_id={"exp": p.partner}, device_id_type=MESH)
        loads[dx, dz].start()
        pairs[dx, dz].start()
    shares = []
    for i, s in enumerate((1, -1, 2)):
        shares.append(pltpu.make_async_remote_copy(
            sh.at[pl.ds(pl.multiple_of(p.up(s) * TOK, TOK), TOK)], shbuf.at[i], send.at[1], sh_recv.at[i],
            device_id={"req": p.up(s)}, device_id_type=MESH))
        shares[-1].start()
    sh_own = pltpu.make_async_copy(sh.at[pl.ds(pl.multiple_of(p.r * TOK, TOK), TOK)], shbuf.at[3], sh_recv.at[3])
    sh_own.start()
    done = set()
    nodes = sorted(((-depth(a, b), b, a, q) for q in range(4) for a in range(4) for b in range(4)))
    for _, b, a, q in nodes:
        o = shift(q, a, b)
        o = tuple(2 if v == -2 else v for v in o)
        j = offs.index(o)
        if o not in done:
            done.add(o)
            loads[o].wait()
            pairs[o].wait_recv()
        kids = []
        for _, _, na, nb in children(q, a, b):
            i = q * 15 + na * 4 + nb - 1
            kids.append(i)
            pltpu.make_async_remote_copy(
                rbuf.at[i], rbuf.at[i], send.at[2], recv_sem.at[i],
                device_id={"exp": p.partner}, device_id_type=MESH).wait_recv()
        rows = pl.ds(q * 32, 32)
        root = a == 0 and b == 0
        if root and q == 0:
            for s in shares:
                s.wait_recv()
            sh_own.wait()

        def add(n, _, j=j, kids=kids, rows=rows, root=root):
            cols = pl.ds(pl.multiple_of(n * 256, 256), 256)
            v = mine[j, rows, cols].astype(F32) + pair[j, rows, cols].astype(F32)
            for i in kids:
                v = v + rbuf[i, :, cols].astype(F32)
            if root:
                t = shbuf[3, rows, cols].astype(F32)
                for i in range(3):
                    t = t + shbuf[i, rows, cols].astype(F32)
                out_ref[rows, cols] = (hid_ref[rows, cols] + v + t).astype(BF16)
            else:
                mine[j, rows, cols] = v.astype(BF16)
            return 0

        lax.fori_loop(0, 8, add, 0)
        if not root:
            first, second, t = route(q)
            dim, code = (second, b) if b else (first, a)
            i = q * 15 + a * 4 + b - 1
            pltpu.make_async_remote_copy(
                mine.at[j, rows], rbuf.at[i], send.at[2], recv_sem.at[i],
                device_id={"exp": p.step(dim, -hop(code, t))}, device_id_type=MESH).start()
    ref = mine
    pltpu.make_async_copy(ref, ref, send.at[0]).wait()
    ref = shbuf.at[pl.ds(0, 3)]
    pltpu.make_async_copy(ref, ref, send.at[1]).wait()
    pltpu.make_async_copy(rbuf, rbuf, send.at[2]).wait()


def call_return(hid, parts, sh):
    return pl.pallas_call(
        kernel_return,
        out_shape=jax.ShapeDtypeStruct((TOK, D), BF16),
        in_specs=[VM, ANY, ANY],
        out_specs=VM,
        scratch_shapes=[
            pltpu.VMEM((16, TOK, D), BF16),
            pltpu.VMEM((16, TOK, D), BF16),
            pltpu.VMEM((60, 32, D), BF16),
            pltpu.VMEM((4, TOK, D), BF16),
            pltpu.SemaphoreType.DMA((16,)),
            pltpu.SemaphoreType.DMA((16,)),
            pltpu.SemaphoreType.DMA((60,)),
            pltpu.SemaphoreType.DMA((4,)),
            pltpu.SemaphoreType.DMA((3,)),
        ],
        compiler_params=pltpu.CompilerParams(collective_id=2, has_side_effects=True, vmem_limit_bytes=VMEM_LIMIT),
        name="give_back",
    )(hid, parts, sh)


def on_device(queries, keys_then_values, residual, norm_gain, prompt_lengths, expert_ids, router_logits,
              w_gate, w_up, w_down, w_shared_gate, w_shared_up, w_shared_down, page_table):
    c = lax.axis_index("exp")
    r = lax.axis_index("req")
    pad = ((0, 0), (0, SPAD - 704))
    wcat = jnp.concatenate([jnp.pad(w, pad) for w in (w_shared_gate, w_shared_up, w_shared_down)], axis=1)
    weights = jax.nn.softmax(router_logits, axis=-1)
    two = ((0, 0), (0, 2))
    meta = jnp.concatenate([
        jnp.pad(expert_ids.astype(F32), two, constant_values=-1.0), jnp.pad(weights, two)], axis=1).T
    lengths = prompt_lengths[0]
    upto = jnp.arange(16)[:, None] >= jnp.arange(16)[None, :]
    ends = jnp.sum(jnp.where(upto, lengths[None, :], 0), axis=1)
    ends = jnp.pad(ends, (0, 112), constant_values=1 << 20).reshape(1, 128)
    cols = lax.dynamic_slice_in_dim(page_table, c * 8, 8, 1) - (r * 256 + c * 8)
    where_from = jnp.arange(32, dtype=jnp.int32).reshape(4, 8, 1)
    inv = jnp.sum(jnp.where(cols[:, :, None] == jnp.arange(8)[None, None, :], where_from, 0), axis=(0, 1))

    kv_all, w_all, meta_all, pg_all = call_gather(keys_then_values, wcat, meta)
    hid, normed, log_totals, cache = call_attend(
        inv.reshape(1, 8).astype(jnp.int32), queries, kv_all, ends, residual, norm_gain.reshape(1, D), pg_all)
    n_all, y_all = call_rows(normed)
    sh = call_shared(y_all, w_all)
    parts = call_expert(meta_all, n_all, w_gate, w_up, w_down)
    out = call_return(hid, parts, sh)
    return out, cache, log_totals


def solution(mesh):
    tok = P(("req", "exp"), None)
    ex = P("exp", None, None)
    sh = P("exp", "req")
    return jax.shard_map(
        on_device,
        mesh=mesh,
        in_specs=(tok, tok, tok, P(), P("req", None), tok, tok, ex, ex, ex, sh, sh, sh, P()),
        out_specs=(tok, P(("req", "exp"), None, None), P(None, ("req", "exp"))),
        check_vma=False,
    )
```

```python
import functools

import jax
import jax.numpy as jnp
from jax import lax
from jax.experimental import pallas as pl
from jax.experimental.pallas import tpu as pltpu
from jax.sharding import PartitionSpec as P

D = 2048
QUERY_HEADS = 16
KEY_VALUE_HEADS = 4
HEAD_SIZE = 128
FF = 1408
TOPK = 6
PAGE = 16
CAP = 36
TOK = 128
SPAD = 768
MAXLEN = 3072
eps_norm = 1e-06
MESH = pl.DeviceIdType.MESH
CODES = (0, 1, -1, 2)
ANY = pl.BlockSpec(memory_space=pl.ANY)
VM = pl.BlockSpec(memory_space=pltpu.VMEM)
SM = pl.BlockSpec(memory_space=pltpu.SMEM)
F32 = jnp.float32
BF16 = jnp.bfloat16
VMEM_LIMIT = 62 * 1024 * 1024


class Place:
    def __init__(self):
        c = lax.axis_index("exp")
        self.c = c
        self.r = lax.axis_index("req")
        self.z = c // 8
        self.x = lax.rem(c // 2, 4)
        self.k = lax.rem(c, 2)
        self.partner = c + 1 - 2 * self.k

    def at(self, dx, dz):
        return lax.rem(self.z + dz + 4, 4) * 8 + lax.rem(self.x + dx + 4, 4) * 2 + self.k

    def step(self, dim, s):
        return self.at(s, 0) if dim == "x" else self.at(0, s)

    def up(self, s):
        return lax.rem(self.r + s + 4, 4)

    def barrier(self, along_y):
        sem = pltpu.get_barrier_semaphore()
        peers = [self.at(1, 0), self.at(-1, 0), self.at(0, 1), self.at(0, -1), self.partner]
        for p in peers:
            pl.semaphore_signal(sem, inc=1, device_id={"exp": p}, device_id_type=MESH)
        for s in along_y:
            pl.semaphore_signal(sem, inc=1, device_id={"req": self.up(s)}, device_id_type=MESH)
        pl.semaphore_wait(sem, len(peers) + len(along_y))


def route(q):
    first, second = ("x", "z") if q < 2 else ("z", "x")
    return first, second, (1 if q % 2 == 0 else -1)


def shift(q, a, b):
    first, _, t = route(q)
    u, v = CODES[a] * t, CODES[b] * t
    return (u, v) if first == "x" else (v, u)


def hop(code, t):
    return -t if code == 2 else t


def depth(a, b):
    return abs(CODES[a]) + abs(CODES[b])


def children(q, a, b):
    first, second, t = route(q)
    out = []
    if b == 0:
        if a == 0:
            out += [(first, t, 1, 0), (first, -t, 2, 0)]
        elif a == 1:
            out += [(first, t, 3, 0)]
        out += [(second, t, a, 1), (second, -t, a, 2)]
    elif b == 1:
        out += [(second, t, a, 3)]
    return out


class Gather:
    def __init__(self, place, own, every, rows, pieces, send_sem, recv_sem, pair_sem, by_row=False):
        self.by_row = by_row
        self.p, self.own, self.every, self.rows, self.pieces = place, own, every, rows, pieces
        self.rq = rows // pieces
        self.send_sem, self.recv_sem, self.pair_sem = send_sem, recv_sem, pair_sem

    def slot(self, src, q):
        return self.every.at[pl.ds(pl.multiple_of(src * self.rows + q * self.rq, self.rq), self.rq)]

    def block(self, src):
        return self.every.at[pl.ds(pl.multiple_of(src * self.rows, self.rows), self.rows)]

    def source(self, q, a, b):
        dx, dz = shift(q, a, b)
        return self.p.at(-dx, -dz)

    def recv_of(self, q, a, b):
        return self.recv_sem.at[q * 15 + a * 4 + b - 1]

    def pass_on(self, q, a, b):
        src = self.source(q, a, b)
        ref = self.own.at[pl.ds(q * self.rq, self.rq)] if a == 0 and b == 0 else self.slot(src, q)
        for dim, s, na, nb in children(q, a, b):
            pltpu.make_async_remote_copy(
                ref, self.slot(src, q), self.send_sem, self.recv_of(q, na, nb),
                device_id={"exp": self.p.step(dim, s)}, device_id_type=MESH,
            ).start()

    def pair_of(self, row):
        return self.pair_sem.at[row % 4] if self.by_row else self.pair_sem

    def to_pair(self, ref, dst, row):
        pltpu.make_async_remote_copy(
            ref, dst, self.send_sem, self.pair_of(row),
            device_id={"exp": self.p.partner}, device_id_type=MESH,
        ).start()

    def start(self):
        for q in range(self.pieces):
            self.pass_on(q, 0, 0)
        self.to_pair(self.own, self.block(self.p.c), 0)

    def events(self):
        out = []
        for q in range(self.pieces):
            for a in range(4):
                for b in range(4):
                    if a or b:
                        out.append((depth(a, b), b, a, q))
        return sorted(out)

    def take(self, ev):
        _, b, a, q = ev
        ref = self.slot(self.source(q, a, b), q)
        pltpu.make_async_remote_copy(
            ref, ref, self.send_sem, self.recv_of(q, a, b),
            device_id={"exp": self.p.partner}, device_id_type=MESH,
        ).wait_recv()
        self.pass_on(q, a, b)
        self.to_pair(ref, ref, -shift(q, a, b)[1])

    def wait_pair(self, row=0):
        ref = self.every.at[pl.ds(0, (4 if self.by_row else 16) * self.rows)]
        pltpu.make_async_remote_copy(
            ref, ref, self.send_sem, self.pair_of(row),
            device_id={"exp": self.p.partner}, device_id_type=MESH,
        ).wait_recv()

    def drain(self):
        ref = self.every.at[pl.ds(0, 31 * self.rows)]
        pltpu.make_async_copy(ref, ref, self.send_sem).wait()


class RingY:
    def __init__(self, place, own, every, rows, send_sem, recv_sem):
        self.p, self.own, self.every, self.rows = place, own, every, rows
        self.h = rows // 2
        self.send_sem, self.recv_sem = send_sem, recv_sem

    def slot(self, src, q):
        return self.every.at[pl.ds(pl.multiple_of(src * self.rows + q * self.h, self.h), self.h)]

    def send(self, ref, src, q, s, code):
        pltpu.make_async_remote_copy(
            ref, self.slot(src, q), self.send_sem, self.recv_sem.at[q * 3 + code - 1],
            device_id={"req": self.p.up(s)}, device_id_type=MESH,
        ).start()

    def start(self):
        for q, t in ((0, 1), (1, -1)):
            ref = self.own.at[pl.ds(q * self.h, self.h)]
            self.send(ref, self.p.r, q, t, 1)
            self.send(ref, self.p.r, q, -t, 2)

    def finish(self, codes=(1, 2, 3)):
        for code in codes:
            for q, t in ((0, 1), (1, -1)):
                src = self.p.up(-CODES[code] * t)
                ref = self.slot(src, q)
                pltpu.make_async_remote_copy(
                    ref, ref, self.send_sem, self.recv_sem.at[q * 3 + code - 1],
                    device_id={"req": self.p.up(1)}, device_id_type=MESH,
                ).wait_recv()
                if code == 1:
                    self.send(ref, src, q, t, 3)

    def drain(self):
        ref = self.every.at[pl.ds(0, 3 * self.rows)]
        pltpu.make_async_copy(ref, ref, self.send_sem).wait()


def attend_start(c, q_ref, ends_ref, qs, m_s, l_s, acc_s, lt_s, beg_s):
    for h in range(QUERY_HEADS):
        qs[pl.ds(h * TOK, TOK), :] = q_ref[:, h * HEAD_SIZE:(h + 1) * HEAD_SIZE]
    qpos = c * TOK + lax.broadcasted_iota(jnp.int32, (TOK, 128), 0)
    ends = jnp.broadcast_to(ends_ref[...], (TOK, 128))
    beg_s[...] = jnp.max(jnp.where(ends <= qpos, ends, 0).astype(F32), axis=1, keepdims=True)
    m_s[...] = jnp.full_like(m_s, -5e29)
    l_s[...] = jnp.zeros_like(l_s)
    acc_s[...] = jnp.zeros_like(acc_s)
    lt_s[...] = jnp.zeros_like(lt_s)


def attend_chunks(c, lo, hi, kv_ref, qs, m_s, l_s, acc_s, beg_s):
    rows = 4 * TOK

    def chunk(i, _):
        k0 = pl.multiple_of(i * 256, 256)
        kpos = k0 + lax.broadcasted_iota(jnp.int32, (TOK, 256), 1)
        qp = c * TOK + lax.broadcasted_iota(jnp.int32, (TOK, 256), 0)
        seen = (kpos >= beg_s[...].astype(jnp.int32)) & (kpos <= qp)
        bias = jnp.where(seen, 0.0, -1e30).astype(F32)
        bias = jnp.concatenate([bias] * 4, axis=0)
        for g in range(KEY_VALUE_HEADS):
            at = pl.ds(g * rows, rows)
            keys = kv_ref[pl.ds(k0, 256), g * HEAD_SIZE:(g + 1) * HEAD_SIZE]
            values = kv_ref[pl.ds(k0, 256), 512 + g * HEAD_SIZE:512 + (g + 1) * HEAD_SIZE]
            s = lax.dot_general(qs[at, :], keys, (((1,), (1,)), ((), ())), preferred_element_type=F32)
            s = s * HEAD_SIZE ** (-0.5) + bias
            old = m_s[at, :]
            new = jnp.maximum(old, jnp.max(s, axis=1, keepdims=True))
            e = jnp.exp(s - new)
            alpha = jnp.exp(old - new)
            m_s[at, :] = new
            l_s[at, :] = l_s[at, :] * alpha + jnp.sum(e, axis=1, keepdims=True)
            acc_s[at, :] = acc_s[at, :] * alpha + jnp.dot(e.astype(BF16), values, preferred_element_type=F32)
        return 0

    lax.fori_loop(lo, hi, chunk, 0)


def attend_end(res_ref, gain_ref, hid_ref, normed_ref, lt_ref, m_s, l_s, acc_s, lt_s):
    total = jnp.zeros((TOK, 1), F32)
    for h in range(QUERY_HEADS):
        at = pl.ds(h * TOK, TOK)
        cols = slice(h * HEAD_SIZE, (h + 1) * HEAD_SIZE)
        att = (acc_s[at, :] / l_s[at, :]).astype(BF16)
        lt_s[:, h:h + 1] = m_s[at, :] + jnp.log(l_s[at, :])
        hid = res_ref[:, cols].astype(F32) + att.astype(F32)
        hid_ref[:, cols] = hid
        total = total + jnp.sum(hid * hid, axis=1, keepdims=True)
    scale = lax.rsqrt(total * (1.0 / D) + eps_norm)
    for h in range(QUERY_HEADS):
        cols = slice(h * HEAD_SIZE, (h + 1) * HEAD_SIZE)
        normed_ref[:, cols] = (hid_ref[:, cols] * scale * gain_ref[:, cols].astype(F32)).astype(BF16)
    lt_ref[...] = jnp.transpose(lt_s[...])[:QUERY_HEADS, :]


def kernel_attend(kv_ref, w_ref, meta_ref, srow_ref, q_ref, ends_ref, res_ref, gain_ref,
                  w_all, hid_ref, normed_ref, lt_ref, cache_ref, tgt_ref, wt_ref,
                  kv_all, meta_all, pg_all, qs, m_s, l_s, acc_s, lt_s, beg_s,
                  kv_r, w_r, meta_r, pg_r, send, pair, local):
    p = Place()
    c = p.c
    p.barrier((1, -1))
    kv = Gather(p, kv_ref, kv_all, TOK, 4, send.at[0], kv_r, pair.at[0])
    w = Gather(p, w_ref, w_all, 64, 4, send.at[1], w_r, pair.at[1])
    meta = Gather(p, meta_ref, meta_all, 16, 1, send.at[2], meta_r, pair.at[2])
    pages = RingY(p, kv_ref, pg_all, TOK, send.at[3], pg_r)
    meta.start()
    kv.start()
    pages.start()
    own_w = pltpu.make_async_copy(w_ref, w.block(c), local)
    own_w.start()
    kv_all[pl.ds(pl.multiple_of(c * TOK, TOK), TOK), :] = kv_ref[...]
    meta_all[pl.ds(pl.multiple_of(c * 16, 16), 16), :] = meta_ref[...]
    pg_all[pl.ds(pl.multiple_of(p.r * TOK, TOK), TOK), :] = kv_ref[...]
    evs = kv.events()
    for ev in evs[:16]:
        kv.take(ev)
    for ev in meta.events():
        meta.take(ev)
    pages.finish((1,))
    attend_start(c, q_ref, ends_ref, qs, m_s, l_s, acc_s, lt_s, beg_s)
    for ev in evs[16:40]:
        kv.take(ev)
    meta.wait_pair()
    plan_rows(c.astype(F32), meta_all, tgt_ref, wt_ref)
    for ev in evs[40:56]:
        kv.take(ev)
    w.start()
    pages.finish((2, 3))
    hit = lax.broadcasted_iota(jnp.int32, (TOK, 512), 1).astype(F32) == srow_ref[...]
    hit = jnp.where(hit, 1.0, 0.0).astype(BF16)
    cache_ref[...] = jnp.dot(hit, pg_all[...], preferred_element_type=F32).astype(BF16)
    for ev in evs[56:]:
        kv.take(ev)
    kv.wait_pair()
    first = jnp.maximum(c * TOK - MAXLEN, 0) // 256
    stop = c // 2 + 1
    w_evs = w.events()
    cut = (0, 16, 40, 56, 60)
    for i in range(5):
        attend_chunks(c, jnp.minimum(first + 3 * i, stop), jnp.minimum(first + 3 * i + 3, stop),
                      kv_all, qs, m_s, l_s, acc_s, beg_s)
        if i < 4:
            for ev in w_evs[cut[i]:cut[i + 1]]:
                w.take(ev)
    attend_end(res_ref, gain_ref, hid_ref, normed_ref, lt_ref, m_s, l_s, acc_s, lt_s)
    w.wait_pair()
    for g in (kv, w, meta):
        g.drain()
    pages.drain()
    own_w.wait()


def call_attend(kv, wcat, meta, srow, q, ends, res, gain):
    n = QUERY_HEADS * TOK
    return pl.pallas_call(
        kernel_attend,
        out_shape=(
            jax.ShapeDtypeStruct((D, 3 * SPAD), BF16),
            jax.ShapeDtypeStruct((TOK, D), F32),
            jax.ShapeDtypeStruct((TOK, D), BF16),
            jax.ShapeDtypeStruct((QUERY_HEADS, TOK), F32),
            jax.ShapeDtypeStruct((TOK, 1024), BF16),
            jax.ShapeDtypeStruct((32, 128), F32),
            jax.ShapeDtypeStruct((32, 128), F32),
        ),
        in_specs=[VM] * 8,
        out_specs=(ANY,) + (VM,) * 6,
        scratch_shapes=[
            pltpu.VMEM((32 * TOK, 1024), BF16),
            pltpu.VMEM((512, 128), F32),
            pltpu.VMEM((512, 1024), BF16),
            pltpu.VMEM((n, HEAD_SIZE), BF16),
            pltpu.VMEM((n, 1), F32),
            pltpu.VMEM((n, 1), F32),
            pltpu.VMEM((n, HEAD_SIZE), F32),
            pltpu.VMEM((TOK, 128), F32),
            pltpu.VMEM((TOK, 1), F32),
            pltpu.SemaphoreType.DMA((60,)),
            pltpu.SemaphoreType.DMA((60,)),
            pltpu.SemaphoreType.DMA((15,)),
            pltpu.SemaphoreType.DMA((6,)),
            pltpu.SemaphoreType.DMA((4,)),
            pltpu.SemaphoreType.DMA((3,)),
            pltpu.SemaphoreType.DMA,
        ],
        compiler_params=pltpu.CompilerParams(collective_id=0, has_side_effects=True, vmem_limit_bytes=VMEM_LIMIT),
        name="attend",
    )(kv, wcat, meta, srow, q, ends, res, gain)


def silu_mul(g, u):
    return (g / (1.0 + jnp.exp(-g)) * u).astype(BF16)


def shared_up(rows_ref, w_ref, act_s):
    def up(j, _):
        col = pl.multiple_of(j * 256, 256)
        g = jnp.dot(rows_ref[...], w_ref[:, pl.ds(col, 256)], preferred_element_type=F32)
        u = jnp.dot(rows_ref[...], w_ref[:, pl.ds(SPAD + col, 256)], preferred_element_type=F32)
        act_s[:, pl.ds(col, 256)] = silu_mul(g, u)
        return 0

    lax.fori_loop(0, 3, up, 0)


def shared_down(w_ref, act_s, out_ref):
    def down(j, _):
        col = pl.multiple_of(j * 256, 256)
        o = lax.dot_general(act_s[...], w_ref[pl.ds(col, 256), 2 * SPAD:], (((1,), (1,)), ((), ())),
                            preferred_element_type=F32)
        out_ref[:, pl.ds(col, 256)] = o.astype(BF16)
        return 0

    lax.fori_loop(0, 8, down, 0)


def plan_rows(e, meta_ref, tgt_s, wt_s):
    tgt_s[...] = jnp.zeros_like(tgt_s)
    for s in range(32):
        ids = meta_ref[pl.ds(s * 16, 8), :]
        wts = meta_ref[pl.ds(s * 16 + 8, 8), :]
        hit = jnp.where(ids == e, 1.0, 0.0).astype(F32)
        tgt_s[s:s + 1, :] = jnp.sum(hit, axis=0, keepdims=True)
        wt_s[s:s + 1, :] = jnp.sum(hit * wts, axis=0, keepdims=True)
    sel = tgt_s[...]
    i0 = lax.broadcasted_iota(jnp.int32, (128, 128), 0)
    i1 = lax.broadcasted_iota(jnp.int32, (128, 128), 1)
    tri = jnp.where(i0 <= i1, 1.0, 0.0).astype(BF16)
    rank = jnp.dot(sel.astype(BF16), tri, preferred_element_type=F32)
    src = lax.rem(lax.broadcasted_iota(jnp.int32, (32, 128), 0), 4).astype(F32)
    tgt_s[...] = jnp.where(sel > 0.5, src * CAP + rank - 1.0, -1.0)


def pick(tgt_ref, s0):
    t4 = tgt_ref[pl.ds(s0, 4), :]
    trow = jnp.concatenate([t4[i:i + 1, :] for i in range(4)], axis=1)
    return lax.broadcasted_iota(jnp.int32, (4 * CAP, 512), 0).astype(F32) == trow


ROWS = (0, 1, -1, 2)


def kernel_moe(n_ref, tgt_ref, wt_ref, w_hbm, wg_h, wu_h, wd_h, y_out, sh_out,
               n_all, y_all, w_s, wg, wu, wd, x_s, act_s, y_s, sact, sho,
               n_r, y_r, send, pair, w_sem, out_sem):
    p = Place()
    p.barrier((1, -1))
    g = Gather(p, n_ref, n_all, TOK, 4, send.at[0], n_r, pair, by_row=True)
    y = RingY(p, n_ref, y_all, TOK, send.at[1], y_r)
    g.start()
    y.start()
    ws = [pltpu.make_async_copy(a, b, w_sem.at[i]) for i, (a, b) in enumerate(
        ((wg_h.at[0], wg), (wu_h.at[0], wu), (wd_h.at[0], wd), (w_hbm, w_s)))]
    for w in ws:
        w.start()
    n_all[pl.ds(pl.multiple_of(p.c * TOK, TOK), TOK), :] = n_ref[...]
    y_all[pl.ds(pl.multiple_of(p.r * TOK, TOK), TOK), :] = n_ref[...]
    evs = g.events()
    evs.sort(key=lambda ev: (ev[0], abs(shift(ev[3], ev[2], ev[1])[1])))
    state = {"at": 0}
    last = {}
    for i, ev in enumerate(evs):
        last[-shift(ev[3], ev[2], ev[1])[1] % 4] = i

    def tick(n):
        for ev in evs[state["at"]:state["at"] + n]:
            g.take(ev)
        state["at"] = min(len(evs), state["at"] + n)

    def chunk(i):
        row = ROWS[i]
        tick(max(0, last[row % 4] + 1 - state["at"]))
        g.wait_pair(row)
        base = lax.rem(p.z + row + 4, 4) * 8
        wcols = []
        for j in range(2):
            s0 = pl.multiple_of(base + j * 4, 4)
            hit = pick(tgt_ref, s0)
            w4 = wt_ref[pl.ds(s0, 4), :]
            wrow = jnp.concatenate([w4[k:k + 1, :] for k in range(4)], axis=1)
            wcols.append(jnp.sum(jnp.where(hit, wrow, 0.0), axis=1, keepdims=True))
            one = jnp.where(hit, 1.0, 0.0).astype(BF16)
            r0 = pl.multiple_of(s0 * TOK, 512)

            def fetch(n, _, j=j, one=one, r0=r0):
                col = pl.multiple_of(n * 512, 512)
                x_s[pl.ds(j * 144, 144), pl.ds(col, 512)] = jnp.dot(
                    one, n_all[pl.ds(r0, 512), pl.ds(col, 512)], preferred_element_type=F32).astype(BF16)
                return 0

            lax.fori_loop(0, 4, fetch, 0)
            tick(2)
        wcol = jnp.concatenate(wcols, axis=0)
        if i == 0:
            ws[0].wait()
            ws[1].wait()

        def up(col, n):
            gv = jnp.dot(x_s[...], wg[:, pl.ds(col, n)], preferred_element_type=F32)
            uv = jnp.dot(x_s[...], wu[:, pl.ds(col, n)], preferred_element_type=F32)
            act_s[:, pl.ds(col, n)] = silu_mul(gv, uv)

        def up_body(j, _):
            up(pl.multiple_of(j * 512, 512), 512)
            return 0

        lax.fori_loop(0, 2, up_body, 0)
        tick(4)
        up(1024, 384)
        tick(2)
        if i == 0:
            ws[2].wait()

        def down(j, _, i=i):
            col = pl.multiple_of(j * 512, 512)
            o = jnp.dot(act_s[...], wd[:, pl.ds(col, 512)], preferred_element_type=F32)
            y_s[pl.ds(i * 288, 288), pl.ds(col, 512)] = (o * wcol).astype(BF16)
            return 0

        lax.fori_loop(0, 4, down, 0)
        tick(3)
        out = pltpu.make_async_copy(y_s.at[pl.ds(i * 288, 288)], y_out.at[pl.ds(i * 288, 288)], out_sem.at[i])
        out.start()
        return out

    tick(16)
    y.finish((1,))
    outs = [chunk(0)]
    y.finish((2, 3))
    ws[3].wait()
    shared_up(y_all, w_s, sact)
    tick(6)
    shared_down(w_s, sact, sho)
    tick(3)
    outs.append(pltpu.make_async_copy(sho, sh_out, out_sem.at[4]))
    outs[-1].start()
    for i in range(1, 4):
        outs.append(chunk(i))
    g.drain()
    y.drain()
    for o in outs:
        o.wait()


def call_moe(normed, tgt, wt, w_all, wg, wu, wd):
    return pl.pallas_call(
        kernel_moe,
        out_shape=(
            jax.ShapeDtypeStruct((32 * CAP, D), BF16),
            jax.ShapeDtypeStruct((512, D), BF16),
        ),
        in_specs=[VM, VM, VM, ANY, ANY, ANY, ANY],
        out_specs=(ANY, ANY),
        scratch_shapes=[
            pltpu.VMEM((32 * TOK, D), BF16),
            pltpu.VMEM((512, D), BF16),
            pltpu.VMEM((D, 3 * SPAD), BF16),
            pltpu.VMEM((D, FF), BF16),
            pltpu.VMEM((D, FF), BF16),
            pltpu.VMEM((FF, D), BF16),
            pltpu.VMEM((8 * CAP, D), BF16),
            pltpu.VMEM((8 * CAP, FF), BF16),
            pltpu.VMEM((32 * CAP, D), BF16),
            pltpu.VMEM((512, SPAD), BF16),
            pltpu.VMEM((512, D), BF16),
            pltpu.SemaphoreType.DMA((60,)),
            pltpu.SemaphoreType.DMA((6,)),
            pltpu.SemaphoreType.DMA((2,)),
            pltpu.SemaphoreType.DMA((4,)),
            pltpu.SemaphoreType.DMA((4,)),
            pltpu.SemaphoreType.DMA((5,)),
        ],
        compiler_params=pltpu.CompilerParams(collective_id=1, has_side_effects=True, vmem_limit_bytes=VMEM_LIMIT),
        name="moe",
    )(normed, tgt, wt, w_all, wg, wu, wd)


def kernel_return(hid_ref, tgt_ref, y_ref, sh, out_ref, mine, pair, rbuf, shbuf, pair_sem, recv_sem,
                  sh_recv, send):
    p = Place()
    p.barrier((1, -1, 2))
    shares = []
    for i, s in enumerate((1, -1, 2)):
        shares.append(pltpu.make_async_remote_copy(
            sh.at[pl.ds(pl.multiple_of(p.up(s) * TOK, TOK), TOK)], shbuf.at[i], send.at[1], sh_recv.at[i],
            device_id={"req": p.up(s)}, device_id_type=MESH))
        shares[-1].start()
    sh_own = pltpu.make_async_copy(sh.at[pl.ds(pl.multiple_of(p.r * TOK, TOK), TOK)], shbuf.at[3], sh_recv.at[3])
    sh_own.start()

    def blk(dev):
        return mine.at[pl.ds(pl.multiple_of(dev * TOK, TOK), TOK)]

    pairs = {}

    def put(row):
        i = ROWS.index(row)
        base = lax.rem(p.z + row + 4, 4) * 8
        for j in range(2):
            s0 = pl.multiple_of(base + j * 4, 4)
            one = jnp.where(pick(tgt_ref, s0), 1.0, 0.0).astype(BF16)
            r0 = pl.multiple_of(s0 * TOK, 512)

            def body(n, _, j=j, one=one, r0=r0):
                col = pl.multiple_of(n * 1024, 1024)
                mine[pl.ds(r0, 512), pl.ds(col, 1024)] = lax.dot_general(
                    one, y_ref[pl.ds(i * 288 + j * 144, 144), pl.ds(col, 1024)], (((0,), (0,)), ((), ())),
                    preferred_element_type=F32).astype(BF16)
                return 0

            lax.fori_loop(0, 2, body, 0)
        for dx in (2, 1, -1, 0):
            j = (dx % 4) * 4 + row % 4
            dest = p.at(dx, row)
            pairs[dx % 4, row % 4] = pltpu.make_async_remote_copy(
                blk(dest + 1 - 2 * p.k), pair.at[j], send.at[0], pair_sem.at[j],
                device_id={"exp": p.partner}, device_id_type=MESH)
            pairs[dx % 4, row % 4].start()

    done = set()

    def node(q, a, b):
        dx, dz = shift(q, a, b)
        o = (-dx % 4, -dz % 4)
        j = o[0] * 4 + o[1]
        if o not in done:
            done.add(o)
            pairs[o].wait_recv()
        kids = []
        for _, _, na, nb in children(q, a, b):
            i = q * 15 + na * 4 + nb - 1
            kids.append(i)
            pltpu.make_async_remote_copy(
                rbuf.at[i], rbuf.at[i], send.at[2], recv_sem.at[i],
                device_id={"exp": p.partner}, device_id_type=MESH).wait_recv()
        dest = p.at(-dx, -dz)
        rows = pl.ds(q * 32, 32)
        drows = pl.ds(pl.multiple_of(dest * TOK + q * 32, 32), 32)
        root = a == 0 and b == 0

        def add(n, _):
            cols = pl.ds(pl.multiple_of(n * 512, 512), 512)
            v = mine[drows, cols].astype(F32) + pair[j, rows, cols].astype(F32)
            for i in kids:
                v = v + rbuf[i, :, cols].astype(F32)
            if root:
                t = shbuf[3, rows, cols].astype(F32)
                for i in range(3):
                    t = t + shbuf[i, rows, cols].astype(F32)
                out_ref[rows, cols] = (hid_ref[rows, cols] + v + t).astype(BF16)
            else:
                mine[drows, cols] = v.astype(BF16)
            return 0

        lax.fori_loop(0, 4, add, 0)
        if not root:
            first, second, t = route(q)
            dim, code = (second, b) if b else (first, a)
            i = q * 15 + a * 4 + b - 1
            pltpu.make_async_remote_copy(
                mine.at[drows], rbuf.at[i], send.at[2], recv_sem.at[i],
                device_id={"exp": p.step(dim, -hop(code, t))}, device_id_type=MESH).start()

    todo = [(-depth(a, b), -abs(shift(q, a, b)[1]), b, a, q) for q in range(4) for a in range(4) for b in range(4)]
    todo.sort()

    def nodes(test):
        for item in list(todo):
            if test(-item[0], -item[1]):
                node(item[4], item[3], item[2])
                todo.remove(item)

    put(2)
    put(1)
    nodes(lambda d, dz: dz == 2 and d > 2)
    put(-1)
    nodes(lambda d, dz: d > 2)
    put(0)
    nodes(lambda d, dz: d > 0)
    for s in shares:
        s.wait_recv()
    sh_own.wait()
    nodes(lambda d, dz: True)
    ref = pair
    pltpu.make_async_copy(ref, ref, send.at[0]).wait()
    ref = shbuf.at[pl.ds(0, 3)]
    pltpu.make_async_copy(ref, ref, send.at[1]).wait()
    pltpu.make_async_copy(rbuf, rbuf, send.at[2]).wait()


def call_return(hid, tgt, y, sh):
    return pl.pallas_call(
        kernel_return,
        out_shape=jax.ShapeDtypeStruct((TOK, D), BF16),
        in_specs=[VM, VM, VM, ANY],
        out_specs=VM,
        scratch_shapes=[
            pltpu.VMEM((32 * TOK, D), BF16),
            pltpu.VMEM((16, TOK, D), BF16),
            pltpu.VMEM((60, 32, D), BF16),
            pltpu.VMEM((4, TOK, D), BF16),
            pltpu.SemaphoreType.DMA((16,)),
            pltpu.SemaphoreType.DMA((60,)),
            pltpu.SemaphoreType.DMA((4,)),
            pltpu.SemaphoreType.DMA((3,)),
        ],
        compiler_params=pltpu.CompilerParams(collective_id=2, has_side_effects=True, vmem_limit_bytes=VMEM_LIMIT),
        name="give_back",
    )(hid, tgt, y, sh)


def on_device(queries, keys_then_values, residual, norm_gain, prompt_lengths, expert_ids, router_logits,
              w_gate, w_up, w_down, w_shared_gate, w_shared_up, w_shared_down, page_table):
    c = lax.axis_index("exp")
    r = lax.axis_index("req")
    pad = ((0, 0), (0, SPAD - 704))
    wcat = jnp.concatenate([jnp.pad(w, pad) for w in (w_shared_gate, w_shared_up, w_shared_down)], axis=1)
    weights = jax.nn.softmax(router_logits, axis=-1)
    two = ((0, 0), (0, 2))
    meta = jnp.concatenate([
        jnp.pad(expert_ids.astype(F32), two, constant_values=-1.0), jnp.pad(weights, two)], axis=1).T
    lengths = prompt_lengths[0]
    upto = jnp.arange(16)[:, None] >= jnp.arange(16)[None, :]
    ends = jnp.sum(jnp.where(upto, lengths[None, :], 0), axis=1)
    ends = jnp.pad(ends, (0, 112), constant_values=1 << 20).reshape(1, 128)
    cols = lax.dynamic_slice_in_dim(page_table, c * 8, 8, 1) - (r * 256 + c * 8)
    where_from = jnp.arange(32, dtype=jnp.int32).reshape(4, 8, 1)
    inv = jnp.sum(jnp.where(cols[:, :, None] == jnp.arange(8)[None, None, :], where_from, 0), axis=(0, 1))

    srow = (inv[:, None] * PAGE + jnp.arange(PAGE)[None, :]).astype(F32).reshape(TOK, 1)
    w_all, hid, normed, log_totals, cache, tgt, wt = call_attend(
        keys_then_values, wcat, meta, srow, queries, ends, residual, norm_gain.reshape(1, D))
    y, sh = call_moe(normed, tgt, wt, w_all, w_gate, w_up, w_down)
    out = call_return(hid, tgt, y, sh)
    return out, cache.reshape(8, PAGE, 1024), log_totals


def solution(mesh):
    tok = P(("req", "exp"), None)
    ex = P("exp", None, None)
    sh = P("exp", "req")
    return jax.shard_map(
        on_device,
        mesh=mesh,
        in_specs=(tok, tok, tok, P(), P("req", None), tok, tok, ex, ex, ex, sh, sh, sh, P()),
        out_specs=(tok, P(("req", "exp"), None, None), P(None, ("req", "exp"))),
        check_vma=False,
    )
```

```python
import functools

import jax
import jax.numpy as jnp
from jax import lax
from jax.experimental import pallas as pl
from jax.experimental.pallas import tpu as pltpu
from jax.sharding import PartitionSpec as P

D = 2048
QUERY_HEADS = 16
KEY_VALUE_HEADS = 4
HEAD_SIZE = 128
FF = 1408
TOPK = 6
PAGE = 16
CAP = 36
TOK = 128
SPAD = 768
MAXLEN = 3072
eps_norm = 1e-06
MESH = pl.DeviceIdType.MESH
CODES = (0, 1, -1, 2)
ANY = pl.BlockSpec(memory_space=pl.ANY)
VM = pl.BlockSpec(memory_space=pltpu.VMEM)
SM = pl.BlockSpec(memory_space=pltpu.SMEM)
F32 = jnp.float32
BF16 = jnp.bfloat16
VMEM_LIMIT = 62 * 1024 * 1024


class Place:
    def __init__(self):
        c = lax.axis_index("exp")
        self.c = c
        self.r = lax.axis_index("req")
        self.z = c // 8
        self.x = lax.rem(c // 2, 4)
        self.k = lax.rem(c, 2)
        self.partner = c + 1 - 2 * self.k

    def at(self, dx, dz):
        return lax.rem(self.z + dz + 4, 4) * 8 + lax.rem(self.x + dx + 4, 4) * 2 + self.k

    def step(self, dim, s):
        return self.at(s, 0) if dim == "x" else self.at(0, s)

    def up(self, s):
        return lax.rem(self.r + s + 4, 4)

    def barrier(self, along_y):
        sem = pltpu.get_barrier_semaphore()
        peers = [self.at(1, 0), self.at(-1, 0), self.at(0, 1), self.at(0, -1), self.partner]
        for p in peers:
            pl.semaphore_signal(sem, inc=1, device_id={"exp": p}, device_id_type=MESH)
        for s in along_y:
            pl.semaphore_signal(sem, inc=1, device_id={"req": self.up(s)}, device_id_type=MESH)
        pl.semaphore_wait(sem, len(peers) + len(along_y))


def route(q):
    first, second = ("x", "z") if q < 2 else ("z", "x")
    return first, second, (1 if q % 2 == 0 else -1)


def shift(q, a, b):
    first, _, t = route(q)
    u, v = CODES[a] * t, CODES[b] * t
    return (u, v) if first == "x" else (v, u)


def hop(code, t):
    return -t if code == 2 else t


def depth(a, b):
    return abs(CODES[a]) + abs(CODES[b])


def children(q, a, b):
    first, second, t = route(q)
    out = []
    if b == 0:
        if a == 0:
            out += [(first, t, 1, 0), (first, -t, 2, 0)]
        elif a == 1:
            out += [(first, t, 3, 0)]
        out += [(second, t, a, 1), (second, -t, a, 2)]
    elif b == 1:
        out += [(second, t, a, 3)]
    return out


NEAR = (
    ((0, 0), (1, 0), (3, 0), (0, 1), (0, 3)),
    ((1, 1), (1, 3), (3, 1), (3, 3), (2, 0), (0, 2)),
    ((2, 1), (2, 3), (1, 2), (3, 2), (2, 2)),
)
CHUNKS = (
    ((0, 0), (1, 0), (3, 0), (0, 1)),
    ((0, 3), (1, 1), (1, 3), (3, 1)),
    ((3, 3), (2, 0), (0, 2), (2, 1)),
    ((2, 3), (1, 2), (3, 2), (2, 2)),
)


class Gather:
    def __init__(self, place, own, every, rows, pieces, send_sem, recv_sem, pair_sem, groups=None):
        self.groups = groups or (tuple((i, j) for i in range(4) for j in range(4)),)
        self.p, self.own, self.every, self.rows, self.pieces = place, own, every, rows, pieces
        self.rq = rows // pieces
        self.send_sem, self.recv_sem, self.pair_sem = send_sem, recv_sem, pair_sem

    def slot(self, src, q):
        return self.every.at[pl.ds(pl.multiple_of(src * self.rows + q * self.rq, self.rq), self.rq)]

    def block(self, src):
        return self.every.at[pl.ds(pl.multiple_of(src * self.rows, self.rows), self.rows)]

    def source(self, q, a, b):
        dx, dz = shift(q, a, b)
        return self.p.at(-dx, -dz)

    def recv_of(self, q, a, b):
        return self.recv_sem.at[q * 15 + a * 4 + b - 1]

    def pass_on(self, q, a, b):
        src = self.source(q, a, b)
        ref = self.own.at[pl.ds(q * self.rq, self.rq)] if a == 0 and b == 0 else self.slot(src, q)
        for dim, s, na, nb in children(q, a, b):
            pltpu.make_async_remote_copy(
                ref, self.slot(src, q), self.send_sem, self.recv_of(q, na, nb),
                device_id={"exp": self.p.step(dim, s)}, device_id_type=MESH,
            ).start()

    def group(self, q, a, b):
        dx, dz = shift(q, a, b)
        return [i for i, g in enumerate(self.groups) if (-dx % 4, -dz % 4) in g][0]

    def to_pair(self, ref, dst, group):
        pltpu.make_async_remote_copy(
            ref, dst, self.send_sem, self.pair_sem.at[group],
            device_id={"exp": self.p.partner}, device_id_type=MESH,
        ).start()

    def start(self):
        for q in range(self.pieces):
            self.pass_on(q, 0, 0)
        self.to_pair(self.own, self.block(self.p.c), 0)

    def events(self):
        out = []
        for q in range(self.pieces):
            for a in range(4):
                for b in range(4):
                    if a or b:
                        out.append((self.group(q, a, b), depth(a, b), b, a, q))
        return sorted(out)

    def take(self, ev):
        _, _, b, a, q = ev
        ref = self.slot(self.source(q, a, b), q)
        pltpu.make_async_remote_copy(
            ref, ref, self.send_sem, self.recv_of(q, a, b),
            device_id={"exp": self.p.partner}, device_id_type=MESH,
        ).wait_recv()
        self.pass_on(q, a, b)
        self.to_pair(ref, ref, self.group(q, a, b))

    def wait_pair(self, group=0):
        ref = self.every.at[pl.ds(0, len(self.groups[group]) * self.rows)]
        pltpu.make_async_remote_copy(
            ref, ref, self.send_sem, self.pair_sem.at[group],
            device_id={"exp": self.p.partner}, device_id_type=MESH,
        ).wait_recv()

    def drain(self):
        ref = self.every.at[pl.ds(0, 31 * self.rows)]
        pltpu.make_async_copy(ref, ref, self.send_sem).wait()


class RingY:
    def __init__(self, place, own, every, rows, send_sem, recv_sem):
        self.p, self.own, self.every, self.rows = place, own, every, rows
        self.h = rows // 2
        self.send_sem, self.recv_sem = send_sem, recv_sem

    def slot(self, src, q):
        return self.every.at[pl.ds(pl.multiple_of(src * self.rows + q * self.h, self.h), self.h)]

    def send(self, ref, src, q, s, code):
        pltpu.make_async_remote_copy(
            ref, self.slot(src, q), self.send_sem, self.recv_sem.at[q * 3 + code - 1],
            device_id={"req": self.p.up(s)}, device_id_type=MESH,
        ).start()

    def start(self):
        for q, t in ((0, 1), (1, -1)):
            ref = self.own.at[pl.ds(q * self.h, self.h)]
            self.send(ref, self.p.r, q, t, 1)
            self.send(ref, self.p.r, q, -t, 2)

    def finish(self, codes=(1, 2, 3)):
        for code in codes:
            for q, t in ((0, 1), (1, -1)):
                src = self.p.up(-CODES[code] * t)
                ref = self.slot(src, q)
                pltpu.make_async_remote_copy(
                    ref, ref, self.send_sem, self.recv_sem.at[q * 3 + code - 1],
                    device_id={"req": self.p.up(1)}, device_id_type=MESH,
                ).wait_recv()
                if code == 1:
                    self.send(ref, src, q, t, 3)

    def drain(self):
        ref = self.every.at[pl.ds(0, 3 * self.rows)]
        pltpu.make_async_copy(ref, ref, self.send_sem).wait()


def attend_start(c, q_ref, len_ref, qs, m_s, l_s, acc_s, lt_s, beg_s):
    for h in range(QUERY_HEADS):
        qs[pl.ds(h * TOK, TOK), :] = q_ref[:, h * HEAD_SIZE:(h + 1) * HEAD_SIZE]
    qpos = c * TOK + lax.broadcasted_iota(jnp.int32, (TOK, 1), 0)
    begin = jnp.zeros((TOK, 1), jnp.int32)
    end = len_ref[0, 0]
    for j in range(16):
        begin = jnp.where(qpos >= end, end, begin)
        if j < 15:
            end = end + len_ref[0, j + 1]
    beg_s[...] = begin
    m_s[...] = jnp.full_like(m_s, -5e29)
    l_s[...] = jnp.zeros_like(l_s)
    acc_s[...] = jnp.zeros_like(acc_s)
    lt_s[...] = jnp.zeros_like(lt_s)


def near_offset(group, i):
    odd = 1 + 2 * lax.rem(i, 2)
    if group == 1:
        h = i // 4
        v = 1 + 2 * lax.rem(i // 2, 2)
        return (1 - h) * v + h * 2 * (1 - lax.rem(i, 2)), (1 - h) * odd + h * 2 * lax.rem(i, 2)
    h, k = i // 4, lax.rem(i // 2, 2)
    if group == 0:
        return (1 - h) * (1 - k) * odd, (1 - h) * k * odd
    return (1 - h) * ((1 - k) * 2 + k * odd) + 2 * h, (1 - h) * ((1 - k) * odd + k * 2) + 2 * h


def attend_chunks(p, group, kv_ref, qs, m_s, l_s, acc_s, beg_s):
    rows = 4 * TOK
    c = p.c
    first = jnp.maximum(c * TOK - MAXLEN, 0) // 256
    last = c // 2

    def chunk(i, _):
        dx, dz = near_offset(group, i)
        chip = lax.rem(p.z + dz, 4) * 4 + lax.rem(p.x + dx, 4)

        @pl.when((chip >= first) & (chip <= last))
        def _():
            k0 = pl.multiple_of(chip * 256, 256)
            kpos = k0 + lax.broadcasted_iota(jnp.int32, (TOK, 256), 1)
            qp = c * TOK + lax.broadcasted_iota(jnp.int32, (TOK, 256), 0)
            seen = (kpos >= beg_s[...]) & (kpos <= qp)
            bias = jnp.where(seen, 0.0, -1e30).astype(F32)
            bias = jnp.concatenate([bias] * 4, axis=0)
            for g in range(KEY_VALUE_HEADS):
                at = pl.ds(g * rows, rows)
                keys = kv_ref[pl.ds(k0, 256), g * HEAD_SIZE:(g + 1) * HEAD_SIZE]
                values = kv_ref[pl.ds(k0, 256), 512 + g * HEAD_SIZE:512 + (g + 1) * HEAD_SIZE]
                s = lax.dot_general(qs[at, :], keys, (((1,), (1,)), ((), ())), preferred_element_type=F32)
                s = s * HEAD_SIZE ** (-0.5) + bias
                old = m_s[at, :]
                new = jnp.maximum(old, jnp.max(s, axis=1, keepdims=True))
                e = jnp.exp(s - new)
                alpha = jnp.exp(old - new)
                m_s[at, :] = new
                l_s[at, :] = l_s[at, :] * alpha + jnp.sum(e, axis=1, keepdims=True)
                acc_s[at, :] = acc_s[at, :] * alpha + jnp.dot(e.astype(BF16), values, preferred_element_type=F32)

        return 0

    lax.fori_loop(0, len(NEAR[group]), chunk, 0)


def place_pages(p, table_ref, pg_all, cache_ref):
    block = lax.broadcasted_iota(jnp.int32, (1, 512), 1) // PAGE
    slot = jnp.full((1, 512), -1, jnp.int32)
    for g in range(4):
        for j in range(8):
            slot = jnp.where(block == g * 8 + j, table_ref[g, p.c * 8 + j] - (p.r * 256 + p.c * 8), slot)
    i0 = lax.broadcasted_iota(jnp.int32, (TOK, 512), 0)
    i1 = lax.broadcasted_iota(jnp.int32, (TOK, 512), 1)
    hit = (slot == i0 // PAGE) & (lax.rem(i0, PAGE) == lax.rem(i1, PAGE))
    one = jnp.where(hit, 1.0, 0.0).astype(BF16)
    cache_ref[...] = jnp.dot(one, pg_all[...], preferred_element_type=F32).astype(BF16)


def attend_end(res_ref, gain_ref, hid_ref, normed_ref, lt_ref, m_s, l_s, acc_s, lt_s):
    total = jnp.zeros((TOK, 1), F32)
    for h in range(QUERY_HEADS):
        at = pl.ds(h * TOK, TOK)
        cols = slice(h * HEAD_SIZE, (h + 1) * HEAD_SIZE)
        att = (acc_s[at, :] / l_s[at, :]).astype(BF16)
        lt_s[:, h:h + 1] = m_s[at, :] + jnp.log(l_s[at, :])
        hid = res_ref[:, cols].astype(F32) + att.astype(F32)
        hid_ref[:, cols] = hid
        total = total + jnp.sum(hid * hid, axis=1, keepdims=True)
    scale = lax.rsqrt(total * (1.0 / D) + eps_norm)
    for h in range(QUERY_HEADS):
        cols = slice(h * HEAD_SIZE, (h + 1) * HEAD_SIZE)
        normed_ref[:, cols] = (hid_ref[:, cols] * scale * gain_ref[:, cols].astype(F32)).astype(BF16)
    lt_ref[...] = jnp.transpose(lt_s[...])[:QUERY_HEADS, :]


def kernel_attend(len_ref, table_ref, kv_ref, w_ref, meta_ref, q_ref, res_ref, gain_ref,
                  w_all, hid_ref, normed_ref, lt_ref, cache_ref, tgt_ref, wt_ref,
                  kv_all, meta_all, pg_all, qs, m_s, l_s, acc_s, lt_s, beg_s,
                  kv_r, w_r, meta_r, pg_r, send, kv_pair, pair, local):
    p = Place()
    c = p.c
    p.barrier((1, -1))
    kv = Gather(p, kv_ref, kv_all, TOK, 4, send.at[0], kv_r, kv_pair, NEAR)
    w = Gather(p, w_ref, w_all, 64, 4, send.at[1], w_r, pair.at[pl.ds(0, 1)], None)
    meta = Gather(p, meta_ref, meta_all, 16, 1, send.at[2], meta_r, pair.at[pl.ds(1, 1)], None)
    pages = RingY(p, kv_ref, pg_all, TOK, send.at[3], pg_r)
    meta.start()
    kv.start()
    pages.start()
    own_w = pltpu.make_async_copy(w_ref, w.block(c), local)
    own_w.start()
    kv_all[pl.ds(pl.multiple_of(c * TOK, TOK), TOK), :] = kv_ref[...]
    meta_all[pl.ds(pl.multiple_of(c * 16, 16), 16), :] = meta_ref[...]
    pg_all[pl.ds(pl.multiple_of(p.r * TOK, TOK), TOK), :] = kv_ref[...]
    def run(g, d):
        for ev in sorted(g.events(), key=lambda ev: ev[1:]):
            if ev[1] in d:
                g.take(ev)

    attention = (kv_all, qs, m_s, l_s, acc_s, beg_s)
    attend_start(c, q_ref, len_ref, qs, m_s, l_s, acc_s, lt_s, beg_s)
    run(kv, (1,))
    w.start()
    run(meta, (1, 2, 3, 4))
    pages.finish((1,))
    kv.wait_pair(0)
    attend_chunks(p, 0, *attention)
    run(kv, (2,))
    run(w, (1,))
    pages.finish((2, 3))
    kv.wait_pair(1)
    attend_chunks(p, 1, *attention)
    run(kv, (3, 4))
    run(w, (2,))
    kv.wait_pair(2)
    attend_chunks(p, 2, *attention)
    run(w, (3,))
    attend_end(res_ref, gain_ref, hid_ref, normed_ref, lt_ref, m_s, l_s, acc_s, lt_s)
    run(w, (4,))
    meta.wait_pair()
    plan_rows(c.astype(F32), meta_all, tgt_ref, wt_ref)
    place_pages(p, table_ref, pg_all, cache_ref)
    w.wait_pair()
    for g in (kv, w, meta):
        g.drain()
    pages.drain()
    own_w.wait()


def call_attend(lengths, table, kv, wcat, meta, q, res, gain):
    n = QUERY_HEADS * TOK
    return pl.pallas_call(
        kernel_attend,
        out_shape=(
            jax.ShapeDtypeStruct((D, 3 * SPAD), BF16),
            jax.ShapeDtypeStruct((TOK, D), F32),
            jax.ShapeDtypeStruct((TOK, D), BF16),
            jax.ShapeDtypeStruct((QUERY_HEADS, TOK), F32),
            jax.ShapeDtypeStruct((TOK, 1024), BF16),
            jax.ShapeDtypeStruct((32, 128), F32),
            jax.ShapeDtypeStruct((32, 128), F32),
        ),
        in_specs=[SM, SM] + [VM] * 6,
        out_specs=(ANY,) + (VM,) * 6,
        scratch_shapes=[
            pltpu.VMEM((32 * TOK, 1024), BF16),
            pltpu.VMEM((512, 128), F32),
            pltpu.VMEM((512, 1024), BF16),
            pltpu.VMEM((n, HEAD_SIZE), BF16),
            pltpu.VMEM((n, 1), F32),
            pltpu.VMEM((n, 1), F32),
            pltpu.VMEM((n, HEAD_SIZE), F32),
            pltpu.VMEM((TOK, 128), F32),
            pltpu.VMEM((TOK, 1), jnp.int32),
            pltpu.SemaphoreType.DMA((60,)),
            pltpu.SemaphoreType.DMA((60,)),
            pltpu.SemaphoreType.DMA((15,)),
            pltpu.SemaphoreType.DMA((6,)),
            pltpu.SemaphoreType.DMA((4,)),
            pltpu.SemaphoreType.DMA((3,)),
            pltpu.SemaphoreType.DMA((2,)),
            pltpu.SemaphoreType.DMA,
        ],
        compiler_params=pltpu.CompilerParams(collective_id=0, has_side_effects=True, vmem_limit_bytes=VMEM_LIMIT),
        name="attend",
    )(lengths, table, kv, wcat, meta, q, res, gain)


def silu_mul(g, u):
    return (g / (1.0 + jnp.exp(-g)) * u).astype(BF16)


def shared_up(rows_ref, w_ref, act_s):
    def up(j, _):
        col = pl.multiple_of(j * 256, 256)
        g = jnp.dot(rows_ref[...], w_ref[:, pl.ds(col, 256)], preferred_element_type=F32)
        u = jnp.dot(rows_ref[...], w_ref[:, pl.ds(SPAD + col, 256)], preferred_element_type=F32)
        act_s[:, pl.ds(col, 256)] = silu_mul(g, u)
        return 0

    lax.fori_loop(0, 3, up, 0)


def shared_down(w_ref, act_s, out_ref):
    def down(j, _):
        col = pl.multiple_of(j * 256, 256)
        o = lax.dot_general(act_s[...], w_ref[pl.ds(col, 256), 2 * SPAD:], (((1,), (1,)), ((), ())),
                            preferred_element_type=F32)
        out_ref[:, pl.ds(col, 256)] = o.astype(BF16)
        return 0

    lax.fori_loop(0, 8, down, 0)


def plan_rows(e, meta_ref, tgt_s, wt_s):
    tgt_s[...] = jnp.zeros_like(tgt_s)
    for s in range(32):
        ids = meta_ref[pl.ds(s * 16, 8), :]
        logits = meta_ref[pl.ds(s * 16 + 8, 8), :]
        wts = jnp.exp(logits - jnp.max(logits, axis=0, keepdims=True))
        wts = wts / jnp.sum(wts, axis=0, keepdims=True)
        hit = jnp.where(ids == e, 1.0, 0.0).astype(F32)
        tgt_s[s:s + 1, :] = jnp.sum(hit, axis=0, keepdims=True)
        wt_s[s:s + 1, :] = jnp.sum(hit * wts, axis=0, keepdims=True)
    sel = tgt_s[...]
    i0 = lax.broadcasted_iota(jnp.int32, (128, 128), 0)
    i1 = lax.broadcasted_iota(jnp.int32, (128, 128), 1)
    tri = jnp.where(i0 <= i1, 1.0, 0.0).astype(BF16)
    rank = jnp.dot(sel.astype(BF16), tri, preferred_element_type=F32)
    core = lax.rem(lax.broadcasted_iota(jnp.int32, (32, 128), 0), 2).astype(F32)
    tgt_s[...] = jnp.where(sel > 0.5, core * CAP + rank - 1.0, -1000.0)


def pick(tgt_ref, d0, d1):
    t0, t1 = tgt_ref[pl.ds(d0, 2), :], tgt_ref[pl.ds(d1, 2), :] + 2.0 * CAP
    trow = jnp.concatenate([t0[0:1, :], t0[1:2, :], t1[0:1, :], t1[1:2, :]], axis=1)
    return lax.broadcasted_iota(jnp.int32, (4 * CAP, 512), 0).astype(F32) == trow


def chip_of(p, o):
    return pl.multiple_of(p.at(o[0], o[1]) - p.k, 2)


def kernel_moe(n_ref, tgt_ref, wt_ref, w_hbm, wg_h, wu_h, wd_h, y_out, sh_out,
               n_all, y_all, w_s, wg, wu, wd, x_s, act_s, y_s, sact, sho,
               n_r, y_r, send, pair, w_sem, out_sem):
    p = Place()
    p.barrier((1, -1))
    g = Gather(p, n_ref, n_all, TOK, 4, send.at[0], n_r, pair, CHUNKS)
    y = RingY(p, n_ref, y_all, TOK, send.at[1], y_r)
    g.start()
    y.start()
    ws = [pltpu.make_async_copy(a, b, w_sem.at[i]) for i, (a, b) in enumerate(
        ((wg_h.at[0], wg), (wu_h.at[0], wu), (wd_h.at[0], wd), (w_hbm, w_s)))]
    for w in ws:
        w.start()
    n_all[pl.ds(pl.multiple_of(p.c * TOK, TOK), TOK), :] = n_ref[...]
    y_all[pl.ds(pl.multiple_of(p.r * TOK, TOK), TOK), :] = n_ref[...]
    evs = g.events()
    state = {"at": 0}
    last = {ev[0]: i for i, ev in enumerate(evs)}

    def tick(n):
        for ev in evs[state["at"]:state["at"] + n]:
            g.take(ev)
        state["at"] = min(len(evs), state["at"] + n)

    def chunk(i):
        tick(max(0, last[i] + 1 - state["at"]))
        g.wait_pair(i)
        wcols = []
        for j in range(2):
            d0, d1 = chip_of(p, CHUNKS[i][2 * j]), chip_of(p, CHUNKS[i][2 * j + 1])
            hit = pick(tgt_ref, d0, d1)
            w0, w1 = wt_ref[pl.ds(d0, 2), :], wt_ref[pl.ds(d1, 2), :]
            wrow = jnp.concatenate([w0[0:1, :], w0[1:2, :], w1[0:1, :], w1[1:2, :]], axis=1)
            wcols.append(jnp.sum(jnp.where(hit, wrow, 0.0), axis=1, keepdims=True))
            one = jnp.where(hit, 1.0, 0.0).astype(BF16)
            r0, r1 = pl.multiple_of(d0 * TOK, 256), pl.multiple_of(d1 * TOK, 256)

            def fetch(n, _, j=j, one=one, r0=r0, r1=r1):
                col = pl.multiple_of(n * 512, 512)
                v = jnp.dot(one[:, :256], n_all[pl.ds(r0, 256), pl.ds(col, 512)], preferred_element_type=F32)
                v = v + jnp.dot(one[:, 256:], n_all[pl.ds(r1, 256), pl.ds(col, 512)], preferred_element_type=F32)
                x_s[pl.ds(j * 144, 144), pl.ds(col, 512)] = v.astype(BF16)
                return 0

            lax.fori_loop(0, 4, fetch, 0)
            tick(2)
        wcol = jnp.concatenate(wcols, axis=0)
        if i == 0:
            ws[0].wait()
            ws[1].wait()

        def up(col, n):
            gv = jnp.dot(x_s[...], wg[:, pl.ds(col, n)], preferred_element_type=F32)
            uv = jnp.dot(x_s[...], wu[:, pl.ds(col, n)], preferred_element_type=F32)
            act_s[:, pl.ds(col, n)] = silu_mul(gv, uv)

        def up_body(j, _):
            up(pl.multiple_of(j * 512, 512), 512)
            return 0

        lax.fori_loop(0, 2, up_body, 0)
        tick(4)
        up(1024, 384)
        tick(2)
        if i == 0:
            ws[2].wait()

        def down(j, _, i=i):
            col = pl.multiple_of(j * 512, 512)
            o = jnp.dot(act_s[...], wd[:, pl.ds(col, 512)], preferred_element_type=F32)
            y_s[pl.ds(i * 288, 288), pl.ds(col, 512)] = (o * wcol).astype(BF16)
            return 0

        lax.fori_loop(0, 4, down, 0)
        tick(3)
        out = pltpu.make_async_copy(y_s.at[pl.ds(i * 288, 288)], y_out.at[pl.ds(i * 288, 288)], out_sem.at[i])
        out.start()
        return out

    tick(last[0] + 1)
    y.finish((1,))
    tick(4)
    outs = [chunk(0)]
    y.finish((2, 3))
    ws[3].wait()
    shared_up(y_all, w_s, sact)
    tick(6)
    shared_down(w_s, sact, sho)
    tick(3)
    outs.append(pltpu.make_async_copy(sho, sh_out, out_sem.at[4]))
    outs[-1].start()
    for i in range(1, 4):
        outs.append(chunk(i))
    g.drain()
    y.drain()
    for o in outs:
        o.wait()


def call_moe(normed, tgt, wt, w_all, wg, wu, wd):
    return pl.pallas_call(
        kernel_moe,
        out_shape=(
            jax.ShapeDtypeStruct((32 * CAP, D), BF16),
            jax.ShapeDtypeStruct((512, D), BF16),
        ),
        in_specs=[VM, VM, VM, ANY, ANY, ANY, ANY],
        out_specs=(ANY, ANY),
        scratch_shapes=[
            pltpu.VMEM((32 * TOK, D), BF16),
            pltpu.VMEM((512, D), BF16),
            pltpu.VMEM((D, 3 * SPAD), BF16),
            pltpu.VMEM((D, FF), BF16),
            pltpu.VMEM((D, FF), BF16),
            pltpu.VMEM((FF, D), BF16),
            pltpu.VMEM((8 * CAP, D), BF16),
            pltpu.VMEM((8 * CAP, FF), BF16),
            pltpu.VMEM((32 * CAP, D), BF16),
            pltpu.VMEM((512, SPAD), BF16),
            pltpu.VMEM((512, D), BF16),
            pltpu.SemaphoreType.DMA((60,)),
            pltpu.SemaphoreType.DMA((6,)),
            pltpu.SemaphoreType.DMA((2,)),
            pltpu.SemaphoreType.DMA((4,)),
            pltpu.SemaphoreType.DMA((4,)),
            pltpu.SemaphoreType.DMA((5,)),
        ],
        compiler_params=pltpu.CompilerParams(collective_id=1, has_side_effects=True, vmem_limit_bytes=VMEM_LIMIT),
        name="moe",
    )(normed, tgt, wt, w_all, wg, wu, wd)


def kernel_return(hid_ref, tgt_ref, y_hbm, sh, out_ref, y_ref, mine, pair, rbuf, shbuf, pair_sem, recv_sem,
                  sh_recv, send, y_sem):
    p = Place()
    loads = [pltpu.make_async_copy(y_hbm.at[pl.ds(i * 288, 288)], y_ref.at[pl.ds(i * 288, 288)], y_sem.at[i])
             for i in range(4)]
    for i in (3, 2, 1, 0):
        loads[i].start()
    p.barrier((1, -1, 2))
    shares = []
    for i, s in enumerate((1, -1, 2)):
        shares.append(pltpu.make_async_remote_copy(
            sh.at[pl.ds(pl.multiple_of(p.up(s) * TOK, TOK), TOK)], shbuf.at[i], send.at[1], sh_recv.at[i],
            device_id={"req": p.up(s)}, device_id_type=MESH))
        shares[-1].start()
    sh_own = pltpu.make_async_copy(sh.at[pl.ds(pl.multiple_of(p.r * TOK, TOK), TOK)], shbuf.at[3], sh_recv.at[3])
    sh_own.start()

    def blk(dev):
        return mine.at[pl.ds(pl.multiple_of(dev * TOK, TOK), TOK)]

    pairs = {}

    def put(i):
        loads[i].wait()
        for j in (1, 0):
            offs = CHUNKS[i][2 * j:2 * j + 2]
            d0, d1 = chip_of(p, offs[0]), chip_of(p, offs[1])
            one = jnp.where(pick(tgt_ref, d0, d1), 1.0, 0.0).astype(BF16)
            r0, r1 = pl.multiple_of(d0 * TOK, 256), pl.multiple_of(d1 * TOK, 256)

            def body(n, _, j=j, one=one, r0=r0, r1=r1):
                col = pl.multiple_of(n * 1024, 1024)
                v = lax.dot_general(
                    one, y_ref[pl.ds(i * 288 + j * 144, 144), pl.ds(col, 1024)], (((0,), (0,)), ((), ())),
                    preferred_element_type=F32).astype(BF16)
                mine[pl.ds(r0, 256), pl.ds(col, 1024)] = v[:256]
                mine[pl.ds(r1, 256), pl.ds(col, 1024)] = v[256:]
                return 0

            lax.fori_loop(0, 2, body, 0)
            for o in offs[::-1]:
                k = o[0] * 4 + o[1]
                pairs[o] = pltpu.make_async_remote_copy(
                    blk(p.at(o[0], o[1]) + 1 - 2 * p.k), pair.at[k], send.at[0], pair_sem.at[k],
                    device_id={"exp": p.partner}, device_id_type=MESH)
                pairs[o].start()

    done = set()

    def node(q, a, b):
        dx, dz = shift(q, a, b)
        o = (-dx % 4, -dz % 4)
        j = o[0] * 4 + o[1]
        if o not in done:
            done.add(o)
            pairs[o].wait_recv()
        kids = []
        for _, _, na, nb in children(q, a, b):
            i = q * 15 + na * 4 + nb - 1
            kids.append(i)
            pltpu.make_async_remote_copy(
                rbuf.at[i], rbuf.at[i], send.at[2], recv_sem.at[i],
                device_id={"exp": p.partner}, device_id_type=MESH).wait_recv()
        dest = p.at(-dx, -dz)
        rows = pl.ds(q * 32, 32)
        drows = pl.ds(pl.multiple_of(dest * TOK + q * 32, 32), 32)
        root = a == 0 and b == 0

        def add(n, _):
            cols = pl.ds(pl.multiple_of(n * 512, 512), 512)
            v = mine[drows, cols].astype(F32) + pair[j, rows, cols].astype(F32)
            for i in kids:
                v = v + rbuf[i, :, cols].astype(F32)
            if root:
                t = shbuf[3, rows, cols].astype(F32)
                for i in range(3):
                    t = t + shbuf[i, rows, cols].astype(F32)
                out_ref[rows, cols] = (hid_ref[rows, cols] + v + t).astype(BF16)
            else:
                mine[drows, cols] = v.astype(BF16)
            return 0

        lax.fori_loop(0, 4, add, 0)
        if not root:
            first, second, t = route(q)
            dim, code = (second, b) if b else (first, a)
            i = q * 15 + a * 4 + b - 1
            pltpu.make_async_remote_copy(
                mine.at[drows], rbuf.at[i], send.at[2], recv_sem.at[i],
                device_id={"exp": p.step(dim, -hop(code, t))}, device_id_type=MESH).start()

    todo = sorted((-depth(a, b), b, a, q) for q in range(4) for a in range(4) for b in range(4))

    def nodes(i):
        for _, b, a, q in todo:
            dx, dz = shift(q, a, b)
            if (-dx % 4, -dz % 4) in CHUNKS[i] and (a or b):
                node(q, a, b)

    put(3)
    nodes(3)
    put(2)
    nodes(2)
    put(1)
    nodes(1)
    put(0)
    nodes(0)
    for s in shares:
        s.wait_recv()
    sh_own.wait()
    for q in range(4):
        node(q, 0, 0)
    ref = pair
    pltpu.make_async_copy(ref, ref, send.at[0]).wait()
    ref = shbuf.at[pl.ds(0, 3)]
    pltpu.make_async_copy(ref, ref, send.at[1]).wait()
    pltpu.make_async_copy(rbuf, rbuf, send.at[2]).wait()


def call_return(hid, tgt, y, sh):
    return pl.pallas_call(
        kernel_return,
        out_shape=jax.ShapeDtypeStruct((TOK, D), BF16),
        in_specs=[VM, VM, ANY, ANY],
        out_specs=VM,
        scratch_shapes=[
            pltpu.VMEM((32 * CAP, D), BF16),
            pltpu.VMEM((32 * TOK, D), BF16),
            pltpu.VMEM((16, TOK, D), BF16),
            pltpu.VMEM((60, 32, D), BF16),
            pltpu.VMEM((4, TOK, D), BF16),
            pltpu.SemaphoreType.DMA((16,)),
            pltpu.SemaphoreType.DMA((60,)),
            pltpu.SemaphoreType.DMA((4,)),
            pltpu.SemaphoreType.DMA((3,)),
            pltpu.SemaphoreType.DMA((4,)),
        ],
        compiler_params=pltpu.CompilerParams(collective_id=2, has_side_effects=True, vmem_limit_bytes=VMEM_LIMIT),
        name="give_back",
    )(hid, tgt, y, sh)


def on_device(queries, keys_then_values, residual, norm_gain, prompt_lengths, expert_ids, router_logits,
              w_gate, w_up, w_down, w_shared_gate, w_shared_up, w_shared_down, page_table):
    pad = ((0, 0), (0, SPAD - 704))
    wcat = jnp.concatenate([jnp.pad(w, pad) for w in (w_shared_gate, w_shared_up, w_shared_down)], axis=1)
    two = ((0, 0), (0, 2))
    meta = jnp.concatenate([
        jnp.pad(expert_ids.astype(F32), two, constant_values=-1.0),
        jnp.pad(router_logits, two, constant_values=-1e30)], axis=1).T
    w_all, hid, normed, log_totals, cache, tgt, wt = call_attend(
        prompt_lengths, page_table, keys_then_values, wcat, meta, queries, residual, norm_gain.reshape(1, D))
    y, sh = call_moe(normed, tgt, wt, w_all, w_gate, w_up, w_down)
    out = call_return(hid, tgt, y, sh)
    return out, cache.reshape(8, PAGE, 1024), log_totals


def solution(mesh):
    tok = P(("req", "exp"), None)
    ex = P("exp", None, None)
    sh = P("exp", "req")
    return jax.shard_map(
        on_device,
        mesh=mesh,
        in_specs=(tok, tok, tok, P(), P("req", None), tok, tok, ex, ex, ex, sh, sh, sh, P()),
        out_specs=(tok, P(("req", "exp"), None, None), P(None, ("req", "exp"))),
        check_vma=False,
    )
```

```python
import functools

import jax
import jax.numpy as jnp
from jax import lax
from jax.experimental import pallas as pl
from jax.experimental.pallas import tpu as pltpu
from jax.sharding import PartitionSpec as P

D = 2048
QUERY_HEADS = 16
KEY_VALUE_HEADS = 4
HEAD_SIZE = 128
FF = 1408
TOPK = 6
PAGE = 16
CAP = 36
TOK = 128
SPAD = 768
MAXLEN = 3072
eps_norm = 1e-06
MESH = pl.DeviceIdType.MESH
CODES = (0, 1, -1, 2)
ANY = pl.BlockSpec(memory_space=pl.ANY)
VM = pl.BlockSpec(memory_space=pltpu.VMEM)
SM = pl.BlockSpec(memory_space=pltpu.SMEM)
F32 = jnp.float32
BF16 = jnp.bfloat16
VMEM_LIMIT = 62 * 1024 * 1024


class Place:
    def __init__(self):
        c = lax.axis_index("exp")
        self.c = c
        self.r = lax.axis_index("req")
        self.z = c // 8
        self.x = lax.rem(c // 2, 4)
        self.k = lax.rem(c, 2)
        self.partner = c + 1 - 2 * self.k

    def at(self, dx, dz):
        return lax.rem(self.z + dz + 4, 4) * 8 + lax.rem(self.x + dx + 4, 4) * 2 + self.k

    def step(self, dim, s):
        return self.at(s, 0) if dim == "x" else self.at(0, s)

    def up(self, s):
        return lax.rem(self.r + s + 4, 4)

    def barrier(self, along_y):
        sem = pltpu.get_barrier_semaphore()
        peers = [self.at(1, 0), self.at(-1, 0), self.at(0, 1), self.at(0, -1), self.partner]
        for p in peers:
            pl.semaphore_signal(sem, inc=1, device_id={"exp": p}, device_id_type=MESH)
        for s in along_y:
            pl.semaphore_signal(sem, inc=1, device_id={"req": self.up(s)}, device_id_type=MESH)
        pl.semaphore_wait(sem, len(peers) + len(along_y))


def route(q):
    first, second = ("x", "z") if q < 2 else ("z", "x")
    return first, second, (1 if q % 2 == 0 else -1)


def shift(q, a, b):
    first, _, t = route(q)
    u, v = CODES[a] * t, CODES[b] * t
    return (u, v) if first == "x" else (v, u)


def hop(code, t):
    return -t if code == 2 else t


def depth(a, b):
    return abs(CODES[a]) + abs(CODES[b])


def children(q, a, b):
    first, second, t = route(q)
    out = []
    if b == 0:
        if a == 0:
            out += [(first, t, 1, 0), (first, -t, 2, 0)]
        elif a == 1:
            out += [(first, t, 3, 0)]
        out += [(second, t, a, 1), (second, -t, a, 2)]
    elif b == 1:
        out += [(second, t, a, 3)]
    return out


NEAR = (
    ((0, 0), (1, 0), (3, 0), (0, 1), (0, 3)),
    ((1, 1), (1, 3), (3, 1), (3, 3), (2, 0), (0, 2)),
    ((2, 1), (2, 3), (1, 2), (3, 2), (2, 2)),
)
CHUNKS = (
    ((0, 0), (1, 0), (3, 0), (0, 1)),
    ((0, 3), (1, 1), (1, 3), (3, 1)),
    ((3, 3), (2, 0), (0, 2), (2, 1)),
    ((2, 3), (1, 2), (3, 2), (2, 2)),
)


class Gather:
    def __init__(self, place, own, every, rows, pieces, send_sem, recv_sem, pair_sem, groups=None):
        self.groups = groups or (tuple((i, j) for i in range(4) for j in range(4)),)
        self.p, self.own, self.every, self.rows, self.pieces = place, own, every, rows, pieces
        self.rq = rows // pieces
        self.send_sem, self.recv_sem, self.pair_sem = send_sem, recv_sem, pair_sem

    def slot(self, src, q):
        return self.every.at[pl.ds(pl.multiple_of(src * self.rows + q * self.rq, self.rq), self.rq)]

    def block(self, src):
        return self.every.at[pl.ds(pl.multiple_of(src * self.rows, self.rows), self.rows)]

    def source(self, q, a, b):
        dx, dz = shift(q, a, b)
        return self.p.at(-dx, -dz)

    def recv_of(self, q, a, b):
        return self.recv_sem.at[q * 15 + a * 4 + b - 1]

    def pass_on(self, q, a, b):
        src = self.source(q, a, b)
        ref = self.own.at[pl.ds(q * self.rq, self.rq)] if a == 0 and b == 0 else self.slot(src, q)
        for dim, s, na, nb in children(q, a, b):
            pltpu.make_async_remote_copy(
                ref, self.slot(src, q), self.send_sem, self.recv_of(q, na, nb),
                device_id={"exp": self.p.step(dim, s)}, device_id_type=MESH,
            ).start()

    def group(self, q, a, b):
        dx, dz = shift(q, a, b)
        return [i for i, g in enumerate(self.groups) if (-dx % 4, -dz % 4) in g][0]

    def to_pair(self, ref, dst, group):
        pltpu.make_async_remote_copy(
            ref, dst, self.send_sem, self.pair_sem.at[group],
            device_id={"exp": self.p.partner}, device_id_type=MESH,
        ).start()

    def start(self):
        for q in range(self.pieces):
            self.pass_on(q, 0, 0)
        self.to_pair(self.own, self.block(self.p.c), 0)

    def events(self):
        out = []
        for q in range(self.pieces):
            for a in range(4):
                for b in range(4):
                    if a or b:
                        out.append((self.group(q, a, b), depth(a, b), b, a, q))
        return sorted(out)

    def take(self, ev):
        _, _, b, a, q = ev
        ref = self.slot(self.source(q, a, b), q)
        pltpu.make_async_remote_copy(
            ref, ref, self.send_sem, self.recv_of(q, a, b),
            device_id={"exp": self.p.partner}, device_id_type=MESH,
        ).wait_recv()
        self.pass_on(q, a, b)
        self.to_pair(ref, ref, self.group(q, a, b))

    def wait_pair(self, group=0):
        ref = self.every.at[pl.ds(0, len(self.groups[group]) * self.rows)]
        pltpu.make_async_remote_copy(
            ref, ref, self.send_sem, self.pair_sem.at[group],
            device_id={"exp": self.p.partner}, device_id_type=MESH,
        ).wait_recv()

    def drain(self):
        ref = self.every.at[pl.ds(0, 31 * self.rows)]
        pltpu.make_async_copy(ref, ref, self.send_sem).wait()


class RingY:
    def __init__(self, place, own, every, rows, send_sem, recv_sem):
        self.p, self.own, self.every, self.rows = place, own, every, rows
        self.h = rows // 2
        self.send_sem, self.recv_sem = send_sem, recv_sem

    def slot(self, src, q):
        return self.every.at[pl.ds(pl.multiple_of(src * self.rows + q * self.h, self.h), self.h)]

    def send(self, ref, src, q, s, code):
        pltpu.make_async_remote_copy(
            ref, self.slot(src, q), self.send_sem, self.recv_sem.at[q * 3 + code - 1],
            device_id={"req": self.p.up(s)}, device_id_type=MESH,
        ).start()

    def start(self):
        for q, t in ((0, 1), (1, -1)):
            ref = self.own.at[pl.ds(q * self.h, self.h)]
            self.send(ref, self.p.r, q, t, 1)
            self.send(ref, self.p.r, q, -t, 2)

    def finish(self, codes=(1, 2, 3)):
        for code in codes:
            for q, t in ((0, 1), (1, -1)):
                src = self.p.up(-CODES[code] * t)
                ref = self.slot(src, q)
                pltpu.make_async_remote_copy(
                    ref, ref, self.send_sem, self.recv_sem.at[q * 3 + code - 1],
                    device_id={"req": self.p.up(1)}, device_id_type=MESH,
                ).wait_recv()
                if code == 1:
                    self.send(ref, src, q, t, 3)

    def drain(self):
        ref = self.every.at[pl.ds(0, 3 * self.rows)]
        pltpu.make_async_copy(ref, ref, self.send_sem).wait()


def attend_start(c, q_ref, len_ref, qs, m_s, l_s, acc_s, lt_s, beg_s):
    for h in range(QUERY_HEADS):
        qs[pl.ds(h * TOK, TOK), :] = q_ref[:, h * HEAD_SIZE:(h + 1) * HEAD_SIZE]
    qpos = c * TOK + lax.broadcasted_iota(jnp.int32, (TOK, 1), 0)
    begin = jnp.zeros((TOK, 1), jnp.int32)
    end = len_ref[0, 0]
    for j in range(16):
        begin = jnp.where(qpos >= end, end, begin)
        if j < 15:
            end = end + len_ref[0, j + 1]
    beg_s[...] = begin
    m_s[...] = jnp.full_like(m_s, -5e29)
    l_s[...] = jnp.zeros_like(l_s)
    acc_s[...] = jnp.zeros_like(acc_s)
    lt_s[...] = jnp.zeros_like(lt_s)


def near_offset(group, i):
    odd = 1 + 2 * lax.rem(i, 2)
    if group == 1:
        h = i // 4
        v = 1 + 2 * lax.rem(i // 2, 2)
        return (1 - h) * v + h * 2 * (1 - lax.rem(i, 2)), (1 - h) * odd + h * 2 * lax.rem(i, 2)
    h, k = i // 4, lax.rem(i // 2, 2)
    if group == 0:
        return (1 - h) * (1 - k) * odd, (1 - h) * k * odd
    return (1 - h) * ((1 - k) * 2 + k * odd) + 2 * h, (1 - h) * ((1 - k) * odd + k * 2) + 2 * h


def attend_chunks(p, group, kv_ref, qs, m_s, l_s, acc_s, beg_s):
    rows = 4 * TOK
    c = p.c
    first = jnp.maximum(c * TOK - MAXLEN, 0) // 256
    last = c // 2

    def chunk(i, _):
        dx, dz = near_offset(group, i)
        chip = lax.rem(p.z + dz, 4) * 4 + lax.rem(p.x + dx, 4)

        @pl.when((chip >= first) & (chip <= last))
        def _():
            k0 = pl.multiple_of(chip * 256, 256)
            kpos = k0 + lax.broadcasted_iota(jnp.int32, (TOK, 256), 1)
            qp = c * TOK + lax.broadcasted_iota(jnp.int32, (TOK, 256), 0)
            seen = (kpos >= beg_s[...]) & (kpos <= qp)
            bias = jnp.where(seen, 0.0, -1e30).astype(F32)
            bias = jnp.concatenate([bias] * 4, axis=0)
            for g in range(KEY_VALUE_HEADS):
                at = pl.ds(g * rows, rows)
                keys = kv_ref[pl.ds(k0, 256), g * HEAD_SIZE:(g + 1) * HEAD_SIZE]
                values = kv_ref[pl.ds(k0, 256), 512 + g * HEAD_SIZE:512 + (g + 1) * HEAD_SIZE]
                s = lax.dot_general(qs[at, :], keys, (((1,), (1,)), ((), ())), preferred_element_type=F32)
                s = s * HEAD_SIZE ** (-0.5) + bias
                old = m_s[at, :]
                new = jnp.maximum(old, jnp.max(s, axis=1, keepdims=True))
                e = jnp.exp(s - jnp.concatenate([new, new], axis=1))
                alpha = jnp.exp(old - new)
                m_s[at, :] = new
                l_s[at, :] = l_s[at, :] * alpha + jnp.sum(e, axis=1, keepdims=True)
                acc_s[at, :] = acc_s[at, :] * alpha + jnp.dot(e.astype(BF16), values, preferred_element_type=F32)

        return 0

    lax.fori_loop(0, len(NEAR[group]), chunk, 0)


def place_pages(p, table_ref, pg_all, cache_ref):
    block = lax.broadcasted_iota(jnp.int32, (1, 512), 1) // PAGE
    slot = jnp.full((1, 512), -1, jnp.int32)
    for g in range(4):
        for j in range(8):
            slot = jnp.where(block == g * 8 + j, table_ref[g, p.c * 8 + j] - (p.r * 256 + p.c * 8), slot)
    i0 = lax.broadcasted_iota(jnp.int32, (TOK, 512), 0)
    i1 = lax.broadcasted_iota(jnp.int32, (TOK, 512), 1)
    hit = (slot == i0 // PAGE) & (lax.rem(i0, PAGE) == lax.rem(i1, PAGE))
    one = jnp.where(hit, 1.0, 0.0).astype(BF16)
    cache_ref[...] = jnp.dot(one, pg_all[...], preferred_element_type=F32).astype(BF16)


def attend_end(res_ref, gain_ref, hid_ref, normed_ref, lt_ref, m_s, l_s, acc_s, lt_s):
    total = jnp.zeros((TOK, 1), F32)
    for h in range(QUERY_HEADS):
        at = pl.ds(h * TOK, TOK)
        cols = slice(h * HEAD_SIZE, (h + 1) * HEAD_SIZE)
        att = (acc_s[at, :] / l_s[at, :]).astype(BF16)
        lane = lax.broadcasted_iota(jnp.int32, (TOK, 128), 1)
        lt_s[...] = jnp.where(lane == h, m_s[at, :] + jnp.log(l_s[at, :]), lt_s[...])
        hid = res_ref[:, cols].astype(F32) + att.astype(F32)
        hid_ref[:, cols] = hid
        total = total + jnp.sum(hid * hid, axis=1, keepdims=True)
    scale = lax.rsqrt(total * (1.0 / D) + eps_norm)
    for h in range(QUERY_HEADS):
        cols = slice(h * HEAD_SIZE, (h + 1) * HEAD_SIZE)
        normed_ref[:, cols] = (hid_ref[:, cols] * scale * gain_ref[:, cols].astype(F32)).astype(BF16)
    lt_ref[...] = jnp.transpose(lt_s[...])[:QUERY_HEADS, :]


def kernel_attend(len_ref, table_ref, kv_ref, w_ref, meta_ref, q_ref, res_ref, gain_ref,
                  w_all, hid_ref, normed_ref, lt_ref, cache_ref, tgt_ref, wt_ref,
                  kv_all, w_s, meta_all, pg_all, qs, m_s, l_s, acc_s, lt_s, beg_s,
                  kv_r, w_r, meta_r, pg_r, send, kv_pair, pair, local):
    p = Place()
    c = p.c
    p.barrier((1, -1))
    kv = Gather(p, kv_ref, kv_all, TOK, 4, send.at[0], kv_r, kv_pair, NEAR)
    w = Gather(p, w_ref, w_s, 64, 4, send.at[1], w_r, pair.at[pl.ds(0, 1)], None)
    meta = Gather(p, meta_ref, meta_all, 16, 1, send.at[2], meta_r, pair.at[pl.ds(1, 1)], None)
    pages = RingY(p, kv_ref, pg_all, TOK, send.at[3], pg_r)
    meta.start()
    kv.start()
    pages.start()
    w_s[pl.ds(pl.multiple_of(c * 64, 64), 64), :] = w_ref[...]
    kv_all[pl.ds(pl.multiple_of(c * TOK, TOK), TOK), :] = kv_ref[...]
    meta_all[pl.ds(pl.multiple_of(c * 16, 16), 16), :] = meta_ref[...]
    pg_all[pl.ds(pl.multiple_of(p.r * TOK, TOK), TOK), :] = kv_ref[...]
    def run(g, d):
        for ev in sorted(g.events(), key=lambda ev: ev[1:]):
            if ev[1] in d:
                g.take(ev)

    attention = (kv_all, qs, m_s, l_s, acc_s, beg_s)
    attend_start(c, q_ref, len_ref, qs, m_s, l_s, acc_s, lt_s, beg_s)
    run(kv, (1,))
    run(meta, (1,))
    pages.finish((1,))
    run(meta, (2,))
    run(kv, (2,))
    w.start()
    kv.wait_pair(0)
    attend_chunks(p, 0, *attention)
    run(kv, (3, 4))
    run(w, (1,))
    run(meta, (3, 4))
    pages.finish((2, 3))
    kv.wait_pair(1)
    attend_chunks(p, 1, *attention)
    run(w, (2,))
    kv.wait_pair(2)
    attend_chunks(p, 2, *attention)
    run(w, (3,))
    attend_end(res_ref, gain_ref, hid_ref, normed_ref, lt_ref, m_s, l_s, acc_s, lt_s)
    run(w, (4,))
    w.wait_pair()
    w_out = pltpu.make_async_copy(w_s, w_all, local)
    w_out.start()
    meta.wait_pair()
    plan_rows(c.astype(F32), meta_all, tgt_ref, wt_ref)
    place_pages(p, table_ref, pg_all, cache_ref)
    for g in (kv, w, meta):
        g.drain()
    pages.drain()
    w_out.wait()


def call_attend(lengths, table, kv, wcat, meta, q, res, gain):
    n = QUERY_HEADS * TOK
    return pl.pallas_call(
        kernel_attend,
        out_shape=(
            jax.ShapeDtypeStruct((D, 3 * SPAD), BF16),
            jax.ShapeDtypeStruct((TOK, D), F32),
            jax.ShapeDtypeStruct((TOK, D), BF16),
            jax.ShapeDtypeStruct((QUERY_HEADS, TOK), F32),
            jax.ShapeDtypeStruct((TOK, 1024), BF16),
            jax.ShapeDtypeStruct((32, 128), F32),
            jax.ShapeDtypeStruct((32, 128), F32),
        ),
        in_specs=[SM, SM] + [VM] * 6,
        out_specs=(ANY,) + (VM,) * 6,
        scratch_shapes=[
            pltpu.VMEM((32 * TOK, 1024), BF16),
            pltpu.VMEM((D, 3 * SPAD), BF16),
            pltpu.VMEM((512, 128), F32),
            pltpu.VMEM((512, 1024), BF16),
            pltpu.VMEM((n, HEAD_SIZE), BF16),
            pltpu.VMEM((n, HEAD_SIZE), F32),
            pltpu.VMEM((n, HEAD_SIZE), F32),
            pltpu.VMEM((n, HEAD_SIZE), F32),
            pltpu.VMEM((TOK, 128), F32),
            pltpu.VMEM((TOK, 1), jnp.int32),
            pltpu.SemaphoreType.DMA((60,)),
            pltpu.SemaphoreType.DMA((60,)),
            pltpu.SemaphoreType.DMA((15,)),
            pltpu.SemaphoreType.DMA((6,)),
            pltpu.SemaphoreType.DMA((4,)),
            pltpu.SemaphoreType.DMA((3,)),
            pltpu.SemaphoreType.DMA((2,)),
            pltpu.SemaphoreType.DMA,
        ],
        compiler_params=pltpu.CompilerParams(collective_id=0, has_side_effects=True, vmem_limit_bytes=VMEM_LIMIT),
        name="attend",
    )(lengths, table, kv, wcat, meta, q, res, gain)


def silu_mul(g, u):
    return (g / (1.0 + jnp.exp(-g)) * u).astype(BF16)


def shared_up(rows_ref, w_ref, act_s):
    def up(j, _):
        col = pl.multiple_of(j * 256, 256)
        g = jnp.dot(rows_ref[...], w_ref[:, pl.ds(col, 256)], preferred_element_type=F32)
        u = jnp.dot(rows_ref[...], w_ref[:, pl.ds(SPAD + col, 256)], preferred_element_type=F32)
        act_s[:, pl.ds(col, 256)] = silu_mul(g, u)
        return 0

    lax.fori_loop(0, 3, up, 0)


def shared_down(w_ref, act_s, out_ref):
    def down(j, _):
        col = pl.multiple_of(j * 256, 256)
        o = lax.dot_general(act_s[...], w_ref[pl.ds(col, 256), 2 * SPAD:], (((1,), (1,)), ((), ())),
                            preferred_element_type=F32)
        out_ref[:, pl.ds(col, 256)] = o.astype(BF16)
        return 0

    lax.fori_loop(0, 8, down, 0)


def plan_rows(e, meta_ref, tgt_s, wt_s):
    tgt_s[...] = jnp.zeros_like(tgt_s)
    for s in range(32):
        ids = meta_ref[pl.ds(s * 16, 8), :]
        logits = meta_ref[pl.ds(s * 16 + 8, 8), :]
        wts = jnp.exp(logits - jnp.max(logits, axis=0, keepdims=True))
        wts = wts / jnp.sum(wts, axis=0, keepdims=True)
        hit = jnp.where(ids == e, 1.0, 0.0).astype(F32)
        tgt_s[s:s + 1, :] = jnp.sum(hit, axis=0, keepdims=True)
        wt_s[s:s + 1, :] = jnp.sum(hit * wts, axis=0, keepdims=True)
    sel = tgt_s[...]
    i0 = lax.broadcasted_iota(jnp.int32, (128, 128), 0)
    i1 = lax.broadcasted_iota(jnp.int32, (128, 128), 1)
    tri = jnp.where(i0 <= i1, 1.0, 0.0).astype(BF16)
    rank = jnp.dot(sel.astype(BF16), tri, preferred_element_type=F32)
    core = lax.rem(lax.broadcasted_iota(jnp.int32, (32, 128), 0), 2).astype(F32)
    tgt_s[...] = jnp.where(sel > 0.5, core * CAP + rank - 1.0, -1000.0)


def pick(tgt_ref, d0, d1):
    t0, t1 = tgt_ref[pl.ds(d0, 2), :], tgt_ref[pl.ds(d1, 2), :] + 2.0 * CAP
    trow = jnp.concatenate([t0[0:1, :], t0[1:2, :], t1[0:1, :], t1[1:2, :]], axis=1)
    return lax.broadcasted_iota(jnp.int32, (4 * CAP, 512), 0).astype(F32) == trow


def chip_of(p, o):
    return pl.multiple_of(p.at(o[0], o[1]) - p.k, 2)


def kernel_moe(n_ref, tgt_ref, wt_ref, w_hbm, wg_h, wu_h, wd_h, y_out, sh_out,
               n_all, y_all, w_s, wg, wu, wd, x_s, act_s, y_s, sact, sho,
               n_r, y_r, send, pair, w_sem, out_sem):
    p = Place()
    p.barrier((1, -1))
    g = Gather(p, n_ref, n_all, TOK, 4, send.at[0], n_r, pair, CHUNKS)
    y = RingY(p, n_ref, y_all, TOK, send.at[1], y_r)
    g.start()
    y.start()
    ws = [pltpu.make_async_copy(a, b, w_sem.at[i]) for i, (a, b) in enumerate(
        ((wg_h.at[0], wg), (wu_h.at[0], wu), (wd_h.at[0], wd), (w_hbm, w_s)))]
    for w in ws:
        w.start()
    n_all[pl.ds(pl.multiple_of(p.c * TOK, TOK), TOK), :] = n_ref[...]
    y_all[pl.ds(pl.multiple_of(p.r * TOK, TOK), TOK), :] = n_ref[...]
    evs = g.events()
    state = {"at": 0}
    last = {ev[0]: i for i, ev in enumerate(evs)}

    def tick(n):
        for ev in evs[state["at"]:state["at"] + n]:
            g.take(ev)
        state["at"] = min(len(evs), state["at"] + n)

    def chunk(i):
        tick(max(0, last[i] + 1 - state["at"]))
        g.wait_pair(i)
        wcols = []
        for j in range(2):
            d0, d1 = chip_of(p, CHUNKS[i][2 * j]), chip_of(p, CHUNKS[i][2 * j + 1])
            hit = pick(tgt_ref, d0, d1)
            w0, w1 = wt_ref[pl.ds(d0, 2), :], wt_ref[pl.ds(d1, 2), :]
            wrow = jnp.concatenate([w0[0:1, :], w0[1:2, :], w1[0:1, :], w1[1:2, :]], axis=1)
            wcols.append(jnp.sum(jnp.where(hit, wrow, 0.0), axis=1, keepdims=True))
            one = jnp.where(hit, 1.0, 0.0).astype(BF16)
            r0, r1 = pl.multiple_of(d0 * TOK, 256), pl.multiple_of(d1 * TOK, 256)

            def fetch(n, _, j=j, one=one, r0=r0, r1=r1):
                col = pl.multiple_of(n * 512, 512)
                v = jnp.dot(one[:, :256], n_all[pl.ds(r0, 256), pl.ds(col, 512)], preferred_element_type=F32)
                v = v + jnp.dot(one[:, 256:], n_all[pl.ds(r1, 256), pl.ds(col, 512)], preferred_element_type=F32)
                x_s[pl.ds(j * 144, 144), pl.ds(col, 512)] = v.astype(BF16)
                return 0

            lax.fori_loop(0, 4, fetch, 0)
            tick(2)
        wcol = jnp.concatenate(wcols, axis=0)
        if i == 0:
            ws[0].wait()
            ws[1].wait()

        def up(col, n):
            gv = jnp.dot(x_s[...], wg[:, pl.ds(col, n)], preferred_element_type=F32)
            uv = jnp.dot(x_s[...], wu[:, pl.ds(col, n)], preferred_element_type=F32)
            act_s[:, pl.ds(col, n)] = silu_mul(gv, uv)

        def up_body(j, _):
            up(pl.multiple_of(j * 512, 512), 512)
            return 0

        lax.fori_loop(0, 2, up_body, 0)
        tick(4)
        up(1024, 384)
        tick(2)
        if i == 0:
            ws[2].wait()

        def down(j, _, i=i):
            col = pl.multiple_of(j * 512, 512)
            o = jnp.dot(act_s[...], wd[:, pl.ds(col, 512)], preferred_element_type=F32)
            y_s[pl.ds(i * 288, 288), pl.ds(col, 512)] = (o * wcol).astype(BF16)
            return 0

        lax.fori_loop(0, 4, down, 0)
        tick(3)
        out = pltpu.make_async_copy(y_s.at[pl.ds(i * 288, 288)], y_out.at[pl.ds(i * 288, 288)], out_sem.at[i])
        out.start()
        return out

    tick(last[0] + 1)
    y.finish((1,))
    tick(4)
    outs = [chunk(0)]
    y.finish((2, 3))
    ws[3].wait()
    shared_up(y_all, w_s, sact)
    tick(6)
    shared_down(w_s, sact, sho)
    tick(3)
    outs.append(pltpu.make_async_copy(sho, sh_out, out_sem.at[4]))
    outs[-1].start()
    for i in range(1, 4):
        outs.append(chunk(i))
    g.drain()
    y.drain()
    for o in outs:
        o.wait()


def call_moe(normed, tgt, wt, w_all, wg, wu, wd):
    return pl.pallas_call(
        kernel_moe,
        out_shape=(
            jax.ShapeDtypeStruct((32 * CAP, D), BF16),
            jax.ShapeDtypeStruct((512, D), BF16),
        ),
        in_specs=[VM, VM, VM, ANY, ANY, ANY, ANY],
        out_specs=(ANY, ANY),
        scratch_shapes=[
            pltpu.VMEM((32 * TOK, D), BF16),
            pltpu.VMEM((512, D), BF16),
            pltpu.VMEM((D, 3 * SPAD), BF16),
            pltpu.VMEM((D, FF), BF16),
            pltpu.VMEM((D, FF), BF16),
            pltpu.VMEM((FF, D), BF16),
            pltpu.VMEM((8 * CAP, D), BF16),
            pltpu.VMEM((8 * CAP, FF), BF16),
            pltpu.VMEM((32 * CAP, D), BF16),
            pltpu.VMEM((512, SPAD), BF16),
            pltpu.VMEM((512, D), BF16),
            pltpu.SemaphoreType.DMA((60,)),
            pltpu.SemaphoreType.DMA((6,)),
            pltpu.SemaphoreType.DMA((2,)),
            pltpu.SemaphoreType.DMA((4,)),
            pltpu.SemaphoreType.DMA((4,)),
            pltpu.SemaphoreType.DMA((5,)),
        ],
        compiler_params=pltpu.CompilerParams(collective_id=1, has_side_effects=True, vmem_limit_bytes=VMEM_LIMIT),
        name="moe",
    )(normed, tgt, wt, w_all, wg, wu, wd)


def kernel_return(hid_ref, tgt_ref, y_hbm, sh, out_ref, y_ref, mine, pair, rbuf, shbuf, pair_sem, recv_sem,
                  sh_recv, send, y_sem):
    p = Place()
    loads = [pltpu.make_async_copy(y_hbm.at[pl.ds(i * 288, 288)], y_ref.at[pl.ds(i * 288, 288)], y_sem.at[i])
             for i in range(4)]
    for i in (3, 2, 1, 0):
        loads[i].start()
    p.barrier((1, -1, 2))
    shares = []
    for i, s in enumerate((1, -1, 2)):
        shares.append(pltpu.make_async_remote_copy(
            sh.at[pl.ds(pl.multiple_of(p.up(s) * TOK, TOK), TOK)], shbuf.at[i], send.at[1], sh_recv.at[i],
            device_id={"req": p.up(s)}, device_id_type=MESH))
        shares[-1].start()
    sh_own = pltpu.make_async_copy(sh.at[pl.ds(pl.multiple_of(p.r * TOK, TOK), TOK)], shbuf.at[3], sh_recv.at[3])
    sh_own.start()

    def blk(dev):
        return mine.at[pl.ds(pl.multiple_of(dev * TOK, TOK), TOK)]

    pairs = {}

    def put(i):
        loads[i].wait()
        for j in (1, 0):
            offs = CHUNKS[i][2 * j:2 * j + 2]
            d0, d1 = chip_of(p, offs[0]), chip_of(p, offs[1])
            one = jnp.where(pick(tgt_ref, d0, d1), 1.0, 0.0).astype(BF16)
            r0, r1 = pl.multiple_of(d0 * TOK, 256), pl.multiple_of(d1 * TOK, 256)

            def body(n, _, j=j, one=one, r0=r0, r1=r1):
                col = pl.multiple_of(n * 1024, 1024)
                v = lax.dot_general(
                    one, y_ref[pl.ds(i * 288 + j * 144, 144), pl.ds(col, 1024)], (((0,), (0,)), ((), ())),
                    preferred_element_type=F32).astype(BF16)
                mine[pl.ds(r0, 256), pl.ds(col, 1024)] = v[:256]
                mine[pl.ds(r1, 256), pl.ds(col, 1024)] = v[256:]
                return 0

            lax.fori_loop(0, 2, body, 0)
            for o in offs[::-1]:
                k = o[0] * 4 + o[1]
                pairs[o] = pltpu.make_async_remote_copy(
                    blk(p.at(o[0], o[1]) + 1 - 2 * p.k), pair.at[k], send.at[0], pair_sem.at[k],
                    device_id={"exp": p.partner}, device_id_type=MESH)
                pairs[o].start()

    done = set()

    def node(q, a, b):
        dx, dz = shift(q, a, b)
        o = (-dx % 4, -dz % 4)
        j = o[0] * 4 + o[1]
        if o not in done:
            done.add(o)
            pairs[o].wait_recv()
        kids = []
        for _, _, na, nb in children(q, a, b):
            i = q * 15 + na * 4 + nb - 1
            kids.append(i)
            pltpu.make_async_remote_copy(
                rbuf.at[i], rbuf.at[i], send.at[2], recv_sem.at[i],
                device_id={"exp": p.partner}, device_id_type=MESH).wait_recv()
        dest = p.at(-dx, -dz)
        rows = pl.ds(q * 32, 32)
        drows = pl.ds(pl.multiple_of(dest * TOK + q * 32, 32), 32)
        root = a == 0 and b == 0

        def add(n, _):
            cols = pl.ds(pl.multiple_of(n * 512, 512), 512)
            v = mine[drows, cols].astype(F32) + pair[j, rows, cols].astype(F32)
            for i in kids:
                v = v + rbuf[i, :, cols].astype(F32)
            if root:
                t = shbuf[3, rows, cols].astype(F32)
                for i in range(3):
                    t = t + shbuf[i, rows, cols].astype(F32)
                out_ref[rows, cols] = (hid_ref[rows, cols] + v + t).astype(BF16)
            else:
                mine[drows, cols] = v.astype(BF16)
            return 0

        lax.fori_loop(0, 4, add, 0)
        if not root:
            first, second, t = route(q)
            dim, code = (second, b) if b else (first, a)
            i = q * 15 + a * 4 + b - 1
            pltpu.make_async_remote_copy(
                mine.at[drows], rbuf.at[i], send.at[2], recv_sem.at[i],
                device_id={"exp": p.step(dim, -hop(code, t))}, device_id_type=MESH).start()

    todo = sorted((-depth(a, b), b, a, q) for q in range(4) for a in range(4) for b in range(4))

    def nodes(i):
        for _, b, a, q in todo:
            dx, dz = shift(q, a, b)
            if (-dx % 4, -dz % 4) in CHUNKS[i] and (a or b):
                node(q, a, b)

    put(3)
    put(2)
    nodes(3)
    put(1)
    nodes(2)
    put(0)
    nodes(1)
    nodes(0)
    for s in shares:
        s.wait_recv()
    sh_own.wait()
    for q in range(4):
        node(q, 0, 0)
    ref = pair
    pltpu.make_async_copy(ref, ref, send.at[0]).wait()
    ref = shbuf.at[pl.ds(0, 3)]
    pltpu.make_async_copy(ref, ref, send.at[1]).wait()
    pltpu.make_async_copy(rbuf, rbuf, send.at[2]).wait()


def call_return(hid, tgt, y, sh):
    return pl.pallas_call(
        kernel_return,
        out_shape=jax.ShapeDtypeStruct((TOK, D), BF16),
        in_specs=[VM, VM, ANY, ANY],
        out_specs=VM,
        scratch_shapes=[
            pltpu.VMEM((32 * CAP, D), BF16),
            pltpu.VMEM((32 * TOK, D), BF16),
            pltpu.VMEM((16, TOK, D), BF16),
            pltpu.VMEM((60, 32, D), BF16),
            pltpu.VMEM((4, TOK, D), BF16),
            pltpu.SemaphoreType.DMA((16,)),
            pltpu.SemaphoreType.DMA((60,)),
            pltpu.SemaphoreType.DMA((4,)),
            pltpu.SemaphoreType.DMA((3,)),
            pltpu.SemaphoreType.DMA((4,)),
        ],
        compiler_params=pltpu.CompilerParams(collective_id=2, has_side_effects=True, vmem_limit_bytes=VMEM_LIMIT),
        name="give_back",
    )(hid, tgt, y, sh)


def on_device(queries, keys_then_values, residual, norm_gain, prompt_lengths, expert_ids, router_logits,
              w_gate, w_up, w_down, w_shared_gate, w_shared_up, w_shared_down, page_table):
    pad = ((0, 0), (0, SPAD - 704))
    wcat = jnp.concatenate([jnp.pad(w, pad) for w in (w_shared_gate, w_shared_up, w_shared_down)], axis=1)
    two = ((0, 0), (0, 2))
    meta = jnp.concatenate([
        jnp.pad(expert_ids.astype(F32), two, constant_values=-1.0),
        jnp.pad(router_logits, two, constant_values=-1e30)], axis=1).T
    w_all, hid, normed, log_totals, cache, tgt, wt = call_attend(
        prompt_lengths, page_table, keys_then_values, wcat, meta, queries, residual, norm_gain.reshape(1, D))
    y, sh = call_moe(normed, tgt, wt, w_all, w_gate, w_up, w_down)
    out = call_return(hid, tgt, y, sh)
    return out, cache.reshape(8, PAGE, 1024), log_totals


def solution(mesh):
    tok = P(("req", "exp"), None)
    ex = P("exp", None, None)
    sh = P("exp", "req")
    return jax.shard_map(
        on_device,
        mesh=mesh,
        in_specs=(tok, tok, tok, P(), P("req", None), tok, tok, ex, ex, ex, sh, sh, sh, P()),
        out_specs=(tok, P(("req", "exp"), None, None), P(None, ("req", "exp"))),
        check_vma=False,
    )
```

```python
import functools

import jax
import jax.numpy as jnp
from jax import lax
from jax.experimental import pallas as pl
from jax.experimental.pallas import tpu as pltpu
from jax.sharding import PartitionSpec as P

D = 2048
QUERY_HEADS = 16
KEY_VALUE_HEADS = 4
HEAD_SIZE = 128
FF = 1408
TOPK = 6
PAGE = 16
CAP = 36
TOK = 128
SPAD = 768
MAXLEN = 3072
eps_norm = 1e-06
MESH = pl.DeviceIdType.MESH
CODES = (0, 1, -1, 2)
ANY = pl.BlockSpec(memory_space=pl.ANY)
VM = pl.BlockSpec(memory_space=pltpu.VMEM)
SM = pl.BlockSpec(memory_space=pltpu.SMEM)
F32 = jnp.float32
BF16 = jnp.bfloat16
VMEM_LIMIT = 62 * 1024 * 1024


class Place:
    def __init__(self):
        c = lax.axis_index("exp")
        self.c = c
        self.r = lax.axis_index("req")
        self.z = c // 8
        self.x = lax.rem(c // 2, 4)
        self.k = lax.rem(c, 2)
        self.partner = c + 1 - 2 * self.k

    def at(self, dx, dz):
        return lax.rem(self.z + dz + 4, 4) * 8 + lax.rem(self.x + dx + 4, 4) * 2 + self.k

    def step(self, dim, s):
        return self.at(s, 0) if dim == "x" else self.at(0, s)

    def up(self, s):
        return lax.rem(self.r + s + 4, 4)

    def barrier(self, along_y):
        sem = pltpu.get_barrier_semaphore()
        peers = [self.at(1, 0), self.at(-1, 0), self.at(0, 1), self.at(0, -1), self.partner]
        for p in peers:
            pl.semaphore_signal(sem, inc=1, device_id={"exp": p}, device_id_type=MESH)
        for s in along_y:
            pl.semaphore_signal(sem, inc=1, device_id={"req": self.up(s)}, device_id_type=MESH)
        pl.semaphore_wait(sem, len(peers) + len(along_y))


def route(q):
    first, second = ("x", "z") if q < 2 else ("z", "x")
    return first, second, (1 if q % 2 == 0 else -1)


def shift(q, a, b):
    first, _, t = route(q)
    u, v = CODES[a] * t, CODES[b] * t
    return (u, v) if first == "x" else (v, u)


def hop(code, t):
    return -t if code == 2 else t


def depth(a, b):
    return abs(CODES[a]) + abs(CODES[b])


def children(q, a, b):
    first, second, t = route(q)
    out = []
    if b == 0:
        if a == 0:
            out += [(first, t, 1, 0), (first, -t, 2, 0)]
        elif a == 1:
            out += [(first, t, 3, 0)]
        out += [(second, t, a, 1), (second, -t, a, 2)]
    elif b == 1:
        out += [(second, t, a, 3)]
    return out


NEAR = (
    ((0, 0), (1, 0), (3, 0), (0, 1), (0, 3)),
    ((1, 1), (1, 3), (3, 1), (3, 3), (2, 0), (0, 2)),
    ((2, 1), (2, 3), (1, 2), (3, 2), (2, 2)),
)
CHUNKS = (
    ((0, 0), (1, 0), (3, 0), (0, 1)),
    ((0, 3), (1, 1), (1, 3), (3, 1)),
    ((3, 3), (2, 0), (0, 2), (2, 1)),
    ((2, 3), (1, 2), (3, 2), (2, 2)),
)


class Gather:
    def __init__(self, place, own, every, rows, pieces, send_sem, recv_sem, pair_sem, groups=None):
        self.groups = groups or (tuple((i, j) for i in range(4) for j in range(4)),)
        self.p, self.own, self.every, self.rows, self.pieces = place, own, every, rows, pieces
        self.rq = rows // pieces
        self.send_sem, self.recv_sem, self.pair_sem = send_sem, recv_sem, pair_sem

    def slot(self, src, q):
        return self.every.at[pl.ds(pl.multiple_of(src * self.rows + q * self.rq, self.rq), self.rq)]

    def block(self, src):
        return self.every.at[pl.ds(pl.multiple_of(src * self.rows, self.rows), self.rows)]

    def source(self, q, a, b):
        dx, dz = shift(q, a, b)
        return self.p.at(-dx, -dz)

    def recv_of(self, q, a, b):
        return self.recv_sem.at[q * 15 + a * 4 + b - 1]

    def pass_on(self, q, a, b):
        src = self.source(q, a, b)
        ref = self.own.at[pl.ds(q * self.rq, self.rq)] if a == 0 and b == 0 else self.slot(src, q)
        for dim, s, na, nb in children(q, a, b):
            pltpu.make_async_remote_copy(
                ref, self.slot(src, q), self.send_sem, self.recv_of(q, na, nb),
                device_id={"exp": self.p.step(dim, s)}, device_id_type=MESH,
            ).start()

    def group(self, q, a, b):
        dx, dz = shift(q, a, b)
        return [i for i, g in enumerate(self.groups) if (-dx % 4, -dz % 4) in g][0]

    def to_pair(self, ref, dst, group):
        pltpu.make_async_remote_copy(
            ref, dst, self.send_sem, self.pair_sem.at[group],
            device_id={"exp": self.p.partner}, device_id_type=MESH,
        ).start()

    def start(self):
        for q in range(self.pieces):
            self.pass_on(q, 0, 0)
        self.to_pair(self.own, self.block(self.p.c), 0)

    def events(self):
        out = []
        for q in range(self.pieces):
            for a in range(4):
                for b in range(4):
                    if a or b:
                        out.append((self.group(q, a, b), depth(a, b), b, a, q))
        return sorted(out)

    def take(self, ev):
        _, _, b, a, q = ev
        ref = self.slot(self.source(q, a, b), q)
        pltpu.make_async_remote_copy(
            ref, ref, self.send_sem, self.recv_of(q, a, b),
            device_id={"exp": self.p.partner}, device_id_type=MESH,
        ).wait_recv()
        self.pass_on(q, a, b)
        self.to_pair(ref, ref, self.group(q, a, b))

    def wait_pair(self, group=0):
        ref = self.every.at[pl.ds(0, len(self.groups[group]) * self.rows)]
        pltpu.make_async_remote_copy(
            ref, ref, self.send_sem, self.pair_sem.at[group],
            device_id={"exp": self.p.partner}, device_id_type=MESH,
        ).wait_recv()

    def drain(self):
        ref = self.every.at[pl.ds(0, 31 * self.rows)]
        pltpu.make_async_copy(ref, ref, self.send_sem).wait()


class RingY:
    def __init__(self, place, own, every, rows, send_sem, recv_sem):
        self.p, self.own, self.every, self.rows = place, own, every, rows
        self.h = rows // 2
        self.send_sem, self.recv_sem = send_sem, recv_sem

    def slot(self, src, q):
        return self.every.at[pl.ds(pl.multiple_of(src * self.rows + q * self.h, self.h), self.h)]

    def send(self, ref, src, q, s, code):
        pltpu.make_async_remote_copy(
            ref, self.slot(src, q), self.send_sem, self.recv_sem.at[q * 3 + code - 1],
            device_id={"req": self.p.up(s)}, device_id_type=MESH,
        ).start()

    def start(self):
        for q, t in ((0, 1), (1, -1)):
            ref = self.own.at[pl.ds(q * self.h, self.h)]
            self.send(ref, self.p.r, q, t, 1)
            self.send(ref, self.p.r, q, -t, 2)

    def finish(self, codes=(1, 2, 3)):
        for code in codes:
            for q, t in ((0, 1), (1, -1)):
                src = self.p.up(-CODES[code] * t)
                ref = self.slot(src, q)
                pltpu.make_async_remote_copy(
                    ref, ref, self.send_sem, self.recv_sem.at[q * 3 + code - 1],
                    device_id={"req": self.p.up(1)}, device_id_type=MESH,
                ).wait_recv()
                if code == 1:
                    self.send(ref, src, q, t, 3)

    def drain(self):
        ref = self.every.at[pl.ds(0, 3 * self.rows)]
        pltpu.make_async_copy(ref, ref, self.send_sem).wait()


def attend_start(c, q_ref, len_ref, qs, m_s, l_s, acc_s, lt_s, beg_s):
    for h in range(QUERY_HEADS):
        qs[pl.ds(h * TOK, TOK), :] = q_ref[:, h * HEAD_SIZE:(h + 1) * HEAD_SIZE]
    qpos = c * TOK + lax.broadcasted_iota(jnp.int32, (TOK, 1), 0)
    begin = jnp.zeros((TOK, 1), jnp.int32)
    end = len_ref[0, 0]
    for j in range(16):
        begin = jnp.where(qpos >= end, end, begin)
        if j < 15:
            end = end + len_ref[0, j + 1]
    beg_s[...] = begin
    m_s[...] = jnp.full_like(m_s, -5e29)
    l_s[...] = jnp.zeros_like(l_s)
    acc_s[...] = jnp.zeros_like(acc_s)
    lt_s[...] = jnp.zeros_like(lt_s)


def near_offset(group, i):
    odd = 1 + 2 * lax.rem(i, 2)
    if group == 1:
        h = i // 4
        v = 1 + 2 * lax.rem(i // 2, 2)
        return (1 - h) * v + h * 2 * (1 - lax.rem(i, 2)), (1 - h) * odd + h * 2 * lax.rem(i, 2)
    h, k = i // 4, lax.rem(i // 2, 2)
    if group == 0:
        return (1 - h) * (1 - k) * odd, (1 - h) * k * odd
    return (1 - h) * ((1 - k) * 2 + k * odd) + 2 * h, (1 - h) * ((1 - k) * odd + k * 2) + 2 * h


def attend_chunks(p, group, kv_ref, qs, m_s, l_s, acc_s, beg_s):
    rows = 4 * TOK
    c = p.c
    first = jnp.maximum(c * TOK - MAXLEN, 0) // 256
    last = c // 2

    def chunk(i, _):
        dx, dz = near_offset(group, i)
        chip = lax.rem(p.z + dz, 4) * 4 + lax.rem(p.x + dx, 4)

        @pl.when((chip >= first) & (chip <= last))
        def _():
            k0 = pl.multiple_of(chip * 256, 256)
            kpos = k0 + lax.broadcasted_iota(jnp.int32, (TOK, 256), 1)
            qp = c * TOK + lax.broadcasted_iota(jnp.int32, (TOK, 256), 0)
            seen = (kpos >= beg_s[...]) & (kpos <= qp)
            bias = jnp.where(seen, 0.0, -1e30).astype(F32)
            bias = jnp.concatenate([bias] * 4, axis=0)
            for g in range(KEY_VALUE_HEADS):
                at = pl.ds(g * rows, rows)
                keys = kv_ref[pl.ds(k0, 256), g * HEAD_SIZE:(g + 1) * HEAD_SIZE]
                values = kv_ref[pl.ds(k0, 256), 512 + g * HEAD_SIZE:512 + (g + 1) * HEAD_SIZE]
                s = lax.dot_general(qs[at, :], keys, (((1,), (1,)), ((), ())), preferred_element_type=F32)
                s = s * HEAD_SIZE ** (-0.5) + bias
                old = m_s[at, :]
                new = jnp.maximum(old, jnp.max(s, axis=1, keepdims=True))
                e = jnp.exp(s - jnp.concatenate([new, new], axis=1))
                alpha = jnp.exp(old - new)
                m_s[at, :] = new
                l_s[at, :] = l_s[at, :] * alpha + jnp.sum(e, axis=1, keepdims=True)
                acc_s[at, :] = acc_s[at, :] * alpha + jnp.dot(e.astype(BF16), values, preferred_element_type=F32)

        return 0

    lax.fori_loop(0, len(NEAR[group]), chunk, 0)


def place_pages(p, table_ref, pg_all, cache_ref):
    block = lax.broadcasted_iota(jnp.int32, (1, 512), 1) // PAGE
    slot = jnp.full((1, 512), -1, jnp.int32)
    for g in range(4):
        for j in range(8):
            slot = jnp.where(block == g * 8 + j, table_ref[g, p.c * 8 + j] - (p.r * 256 + p.c * 8), slot)
    i0 = lax.broadcasted_iota(jnp.int32, (TOK, 512), 0)
    i1 = lax.broadcasted_iota(jnp.int32, (TOK, 512), 1)
    hit = (slot == i0 // PAGE) & (lax.rem(i0, PAGE) == lax.rem(i1, PAGE))
    one = jnp.where(hit, 1.0, 0.0).astype(BF16)
    cache_ref[...] = jnp.dot(one, pg_all[...], preferred_element_type=F32).astype(BF16)


def attend_end(res_ref, gain_ref, hid_ref, normed_ref, lt_ref, m_s, l_s, acc_s, lt_s):
    total = jnp.zeros((TOK, 1), F32)
    for h in range(QUERY_HEADS):
        at = pl.ds(h * TOK, TOK)
        cols = slice(h * HEAD_SIZE, (h + 1) * HEAD_SIZE)
        att = (acc_s[at, :] / l_s[at, :]).astype(BF16)
        lane = lax.broadcasted_iota(jnp.int32, (TOK, 128), 1)
        lt_s[...] = jnp.where(lane == h, m_s[at, :] + jnp.log(l_s[at, :]), lt_s[...])
        hid = res_ref[:, cols].astype(F32) + att.astype(F32)
        hid_ref[:, cols] = hid
        total = total + jnp.sum(hid * hid, axis=1, keepdims=True)
    scale = lax.rsqrt(total * (1.0 / D) + eps_norm)
    for h in range(QUERY_HEADS):
        cols = slice(h * HEAD_SIZE, (h + 1) * HEAD_SIZE)
        normed_ref[:, cols] = (hid_ref[:, cols] * scale * gain_ref[:, cols].astype(F32)).astype(BF16)
    lt_ref[...] = jnp.transpose(lt_s[...])[:QUERY_HEADS, :]


def kernel_attend(len_ref, table_ref, kv_ref, meta_ref, q_ref, res_ref, gain_ref,
                  hid_ref, normed_ref, lt_ref, cache_ref, tgt_ref, wt_ref,
                  kv_all, meta_all, pg_all, qs, m_s, l_s, acc_s, lt_s, beg_s,
                  kv_r, meta_r, pg_r, send, kv_pair, pair):
    p = Place()
    c = p.c
    p.barrier((1, -1))
    kv = Gather(p, kv_ref, kv_all, TOK, 4, send.at[0], kv_r, kv_pair, NEAR)
    meta = Gather(p, meta_ref, meta_all, 16, 1, send.at[2], meta_r, pair.at[pl.ds(1, 1)], None)
    pages = RingY(p, kv_ref, pg_all, TOK, send.at[3], pg_r)
    meta.start()
    kv.start()
    pages.start()
    kv_all[pl.ds(pl.multiple_of(c * TOK, TOK), TOK), :] = kv_ref[...]
    meta_all[pl.ds(pl.multiple_of(c * 16, 16), 16), :] = meta_ref[...]
    pg_all[pl.ds(pl.multiple_of(p.r * TOK, TOK), TOK), :] = kv_ref[...]
    def run(g, d):
        for ev in sorted(g.events(), key=lambda ev: ev[1:]):
            if ev[1] in d:
                g.take(ev)

    attention = (kv_all, qs, m_s, l_s, acc_s, beg_s)
    attend_start(c, q_ref, len_ref, qs, m_s, l_s, acc_s, lt_s, beg_s)
    run(kv, (1,))
    run(meta, (1,))
    pages.finish((1,))
    run(meta, (2,))
    run(kv, (2,))
    kv.wait_pair(0)
    attend_chunks(p, 0, *attention)
    run(kv, (3, 4))
    run(meta, (3, 4))
    pages.finish((2, 3))
    kv.wait_pair(1)
    attend_chunks(p, 1, *attention)
    kv.wait_pair(2)
    attend_chunks(p, 2, *attention)
    attend_end(res_ref, gain_ref, hid_ref, normed_ref, lt_ref, m_s, l_s, acc_s, lt_s)
    meta.wait_pair()
    plan_rows(c.astype(F32), meta_all, tgt_ref, wt_ref)
    place_pages(p, table_ref, pg_all, cache_ref)
    for g in (kv, meta):
        g.drain()
    pages.drain()


def call_attend(lengths, table, kv, meta, q, res, gain):
    n = QUERY_HEADS * TOK
    return pl.pallas_call(
        kernel_attend,
        out_shape=(
            jax.ShapeDtypeStruct((TOK, D), F32),
            jax.ShapeDtypeStruct((TOK, D), BF16),
            jax.ShapeDtypeStruct((QUERY_HEADS, TOK), F32),
            jax.ShapeDtypeStruct((TOK, 1024), BF16),
            jax.ShapeDtypeStruct((32, 128), F32),
            jax.ShapeDtypeStruct((32, 128), F32),
        ),
        in_specs=[SM, SM] + [VM] * 5,
        out_specs=(VM,) * 6,
        scratch_shapes=[
            pltpu.VMEM((32 * TOK, 1024), BF16),
            pltpu.VMEM((512, 128), F32),
            pltpu.VMEM((512, 1024), BF16),
            pltpu.VMEM((n, HEAD_SIZE), BF16),
            pltpu.VMEM((n, HEAD_SIZE), F32),
            pltpu.VMEM((n, HEAD_SIZE), F32),
            pltpu.VMEM((n, HEAD_SIZE), F32),
            pltpu.VMEM((TOK, 128), F32),
            pltpu.VMEM((TOK, 1), jnp.int32),
            pltpu.SemaphoreType.DMA((60,)),
            pltpu.SemaphoreType.DMA((15,)),
            pltpu.SemaphoreType.DMA((6,)),
            pltpu.SemaphoreType.DMA((4,)),
            pltpu.SemaphoreType.DMA((3,)),
            pltpu.SemaphoreType.DMA((2,)),
        ],
        compiler_params=pltpu.CompilerParams(collective_id=0, has_side_effects=True, vmem_limit_bytes=VMEM_LIMIT),
        name="attend",
    )(lengths, table, kv, meta, q, res, gain)


def silu_mul(g, u):
    return (g / (1.0 + jnp.exp(-g)) * u).astype(BF16)


def shared_up(rows_ref, w_ref, act_s, j):
    cols = slice(j * 256, (j + 1) * 256)
    g = jnp.dot(rows_ref[...], w_ref[:, cols], preferred_element_type=F32)
    u = jnp.dot(rows_ref[...], w_ref[:, SPAD + j * 256:SPAD + (j + 1) * 256], preferred_element_type=F32)
    act_s[:, cols] = silu_mul(g, u)


def shared_down(w_ref, act_s, out_ref):
    def down(j, _):
        col = pl.multiple_of(j * 256, 256)
        o = lax.dot_general(act_s[...], w_ref[pl.ds(col, 256), :], (((1,), (1,)), ((), ())),
                            preferred_element_type=F32)
        out_ref[:, pl.ds(col, 256)] = o.astype(BF16)
        return 0

    lax.fori_loop(0, 8, down, 0)


def plan_rows(e, meta_ref, tgt_s, wt_s):
    tgt_s[...] = jnp.zeros_like(tgt_s)
    for s in range(32):
        ids = meta_ref[pl.ds(s * 16, 8), :]
        logits = meta_ref[pl.ds(s * 16 + 8, 8), :]
        wts = jnp.exp(logits - jnp.max(logits, axis=0, keepdims=True))
        wts = wts / jnp.sum(wts, axis=0, keepdims=True)
        hit = jnp.where(ids == e, 1.0, 0.0).astype(F32)
        tgt_s[s:s + 1, :] = jnp.sum(hit, axis=0, keepdims=True)
        wt_s[s:s + 1, :] = jnp.sum(hit * wts, axis=0, keepdims=True)
    sel = tgt_s[...]
    i0 = lax.broadcasted_iota(jnp.int32, (128, 128), 0)
    i1 = lax.broadcasted_iota(jnp.int32, (128, 128), 1)
    tri = jnp.where(i0 <= i1, 1.0, 0.0).astype(BF16)
    rank = jnp.dot(sel.astype(BF16), tri, preferred_element_type=F32)
    core = lax.rem(lax.broadcasted_iota(jnp.int32, (32, 128), 0), 2).astype(F32)
    tgt_s[...] = jnp.where(sel > 0.5, core * CAP + rank - 1.0, -1000.0)


def pick(tgt_ref, d0, d1):
    t0, t1 = tgt_ref[pl.ds(d0, 2), :], tgt_ref[pl.ds(d1, 2), :] + 2.0 * CAP
    trow = jnp.concatenate([t0[0:1, :], t0[1:2, :], t1[0:1, :], t1[1:2, :]], axis=1)
    return lax.broadcasted_iota(jnp.int32, (4 * CAP, 512), 0).astype(F32) == trow


def chip_of(p, o):
    return pl.multiple_of(p.at(o[0], o[1]) - p.k, 2)


def kernel_moe(n_ref, tgt_ref, wt_ref, w1_ref, w2_ref, wg_h, wu_h, wd_h, y_out, sh_out,
               n_all, y_all, w1_s, w2_s, wg, wu, wd, x_s, act_s, y_s, sact, sho,
               n_r, y_r, w1_r, w2_r, send, pair, w_pair, w_sem, out_sem):
    p = Place()
    p.barrier((1, -1))
    g = Gather(p, n_ref, n_all, TOK, 4, send.at[0], n_r, pair, CHUNKS)
    y = RingY(p, n_ref, y_all, TOK, send.at[1], y_r)
    g.start()
    y.start()
    ws = [pltpu.make_async_copy(a, b, w_sem.at[i]) for i, (a, b) in enumerate(
        ((wg_h.at[0], wg), (wu_h.at[0], wu), (wd_h.at[0], wd)))]
    for w in ws:
        w.start()
    n_all[pl.ds(pl.multiple_of(p.c * TOK, TOK), TOK), :] = n_ref[...]
    y_all[pl.ds(pl.multiple_of(p.r * TOK, TOK), TOK), :] = n_ref[...]
    w1 = Gather(p, w1_ref, w1_s, 64, 4, send.at[2], w1_r, w_pair.at[pl.ds(0, 1)])
    w2 = Gather(p, w2_ref, w2_s, 64, 4, send.at[3], w2_r, w_pair.at[pl.ds(1, 1)])
    for w in (w1, w2):
        w.every[pl.ds(pl.multiple_of(p.c * 64, 64), 64), :] = w.own[...]
    queue = []
    last = {}
    for ev in g.events():
        if ev[0] == 3 and 3 not in last:
            queue.append(w1.start)
        queue.append(functools.partial(g.take, ev))
        last[ev[0]] = len(queue) - 1

    def level(w, d):
        return [functools.partial(w.take, ev) for ev in w.events() if ev[1] == d]

    queue += level(w1, 1) + level(w1, 2) + [w2.start] + level(w1, 3) + level(w2, 1) + level(w1, 4)
    first_part = len(queue)
    queue += level(w2, 2) + level(w2, 3) + level(w2, 4)
    state = {"at": 0}

    def tick(n):
        for do in queue[state["at"]:state["at"] + n]:
            do()
        state["at"] = min(len(queue), state["at"] + n)

    def chunk(i):
        tick(max(0, last[i] + 1 - state["at"]))
        g.wait_pair(i)
        wcols = []
        for j in range(2):
            d0, d1 = chip_of(p, CHUNKS[i][2 * j]), chip_of(p, CHUNKS[i][2 * j + 1])
            hit = pick(tgt_ref, d0, d1)
            w0, w1 = wt_ref[pl.ds(d0, 2), :], wt_ref[pl.ds(d1, 2), :]
            wrow = jnp.concatenate([w0[0:1, :], w0[1:2, :], w1[0:1, :], w1[1:2, :]], axis=1)
            wcols.append(jnp.sum(jnp.where(hit, wrow, 0.0), axis=1, keepdims=True))
            one = jnp.where(hit, 1.0, 0.0).astype(BF16)
            r0, r1 = pl.multiple_of(d0 * TOK, 256), pl.multiple_of(d1 * TOK, 256)

            def fetch(n, _, j=j, one=one, r0=r0, r1=r1):
                col = pl.multiple_of(n * 512, 512)
                v = jnp.dot(one[:, :256], n_all[pl.ds(r0, 256), pl.ds(col, 512)], preferred_element_type=F32)
                v = v + jnp.dot(one[:, 256:], n_all[pl.ds(r1, 256), pl.ds(col, 512)], preferred_element_type=F32)
                x_s[pl.ds(j * 144, 144), pl.ds(col, 512)] = v.astype(BF16)
                return 0

            lax.fori_loop(0, 4, fetch, 0)
            tick(2)
        wcol = jnp.concatenate(wcols, axis=0)
        if i == 0:
            ws[0].wait()
            ws[1].wait()

        def up(col, n):
            gv = jnp.dot(x_s[...], wg[:, pl.ds(col, n)], preferred_element_type=F32)
            uv = jnp.dot(x_s[...], wu[:, pl.ds(col, n)], preferred_element_type=F32)
            act_s[:, pl.ds(col, n)] = silu_mul(gv, uv)

        def up_body(j, _):
            up(pl.multiple_of(j * 512, 512), 512)
            return 0

        lax.fori_loop(0, 2, up_body, 0)
        tick(4)
        up(1024, 384)
        tick(2)
        if i == 0:
            ws[2].wait()

        def down(j, _, i=i):
            col = pl.multiple_of(j * 512, 512)
            o = jnp.dot(act_s[...], wd[:, pl.ds(col, 512)], preferred_element_type=F32)
            y_s[pl.ds(i * 288, 288), pl.ds(col, 512)] = (o * wcol).astype(BF16)
            return 0

        lax.fori_loop(0, 4, down, 0)
        tick(3)
        out = pltpu.make_async_copy(y_s.at[pl.ds(i * 288, 288)], y_out.at[pl.ds(i * 288, 288)], out_sem.at[i])
        out.start()
        return out

    tick(last[0] + 1)
    y.finish((1,))
    tick(4)
    outs = [chunk(0), chunk(1)]
    y.finish((2, 3))
    outs += [chunk(2), chunk(3)]
    tick(max(0, first_part - state["at"]))
    w1.wait_pair()
    for j in range(3):
        shared_up(y_all, w1_s, sact, j)
        tick((24, 16, 4)[j])
    tick(len(queue))
    w2.wait_pair()
    shared_down(w2_s, sact, sho)
    outs.append(pltpu.make_async_copy(sho, sh_out, out_sem.at[4]))
    outs[-1].start()
    for w in (g, w1, w2):
        w.drain()
    y.drain()
    for o in outs:
        o.wait()


def call_moe(normed, tgt, wt, w1, w2, wg, wu, wd):
    return pl.pallas_call(
        kernel_moe,
        out_shape=(
            jax.ShapeDtypeStruct((32 * CAP, D), BF16),
            jax.ShapeDtypeStruct((512, D), BF16),
        ),
        in_specs=[VM, VM, VM, VM, VM, ANY, ANY, ANY],
        out_specs=(ANY, ANY),
        scratch_shapes=[
            pltpu.VMEM((32 * TOK, D), BF16),
            pltpu.VMEM((512, D), BF16),
            pltpu.VMEM((D, 2 * SPAD), BF16),
            pltpu.VMEM((D, SPAD), BF16),
            pltpu.VMEM((D, FF), BF16),
            pltpu.VMEM((D, FF), BF16),
            pltpu.VMEM((FF, D), BF16),
            pltpu.VMEM((8 * CAP, D), BF16),
            pltpu.VMEM((8 * CAP, FF), BF16),
            pltpu.VMEM((32 * CAP, D), BF16),
            pltpu.VMEM((512, SPAD), BF16),
            pltpu.VMEM((512, D), BF16),
            pltpu.SemaphoreType.DMA((60,)),
            pltpu.SemaphoreType.DMA((6,)),
            pltpu.SemaphoreType.DMA((60,)),
            pltpu.SemaphoreType.DMA((60,)),
            pltpu.SemaphoreType.DMA((4,)),
            pltpu.SemaphoreType.DMA((4,)),
            pltpu.SemaphoreType.DMA((2,)),
            pltpu.SemaphoreType.DMA((3,)),
            pltpu.SemaphoreType.DMA((5,)),
        ],
        compiler_params=pltpu.CompilerParams(collective_id=1, has_side_effects=True, vmem_limit_bytes=VMEM_LIMIT),
        name="moe",
    )(normed, tgt, wt, w1, w2, wg, wu, wd)


def kernel_return(hid_ref, tgt_ref, y_hbm, sh, out_ref, y_ref, mine, pair, rbuf, shbuf, pair_sem, recv_sem,
                  sh_recv, send, y_sem):
    p = Place()
    loads = [pltpu.make_async_copy(y_hbm.at[pl.ds(i * 288, 288)], y_ref.at[pl.ds(i * 288, 288)], y_sem.at[i])
             for i in range(4)]
    for i in (3, 2, 1, 0):
        loads[i].start()
    p.barrier((1, -1, 2))
    shares = []
    for i, s in enumerate((1, -1, 2)):
        shares.append(pltpu.make_async_remote_copy(
            sh.at[pl.ds(pl.multiple_of(p.up(s) * TOK, TOK), TOK)], shbuf.at[i], send.at[1], sh_recv.at[i],
            device_id={"req": p.up(s)}, device_id_type=MESH))
        shares[-1].start()
    sh_own = pltpu.make_async_copy(sh.at[pl.ds(pl.multiple_of(p.r * TOK, TOK), TOK)], shbuf.at[3], sh_recv.at[3])
    sh_own.start()

    def blk(dev):
        return mine.at[pl.ds(pl.multiple_of(dev * TOK, TOK), TOK)]

    pairs = {}

    def put(i):
        loads[i].wait()
        for j in (1, 0):
            offs = CHUNKS[i][2 * j:2 * j + 2]
            d0, d1 = chip_of(p, offs[0]), chip_of(p, offs[1])
            one = jnp.where(pick(tgt_ref, d0, d1), 1.0, 0.0).astype(BF16)
            r0, r1 = pl.multiple_of(d0 * TOK, 256), pl.multiple_of(d1 * TOK, 256)

            def body(n, _, j=j, one=one, r0=r0, r1=r1):
                col = pl.multiple_of(n * 1024, 1024)
                v = lax.dot_general(
                    one, y_ref[pl.ds(i * 288 + j * 144, 144), pl.ds(col, 1024)], (((0,), (0,)), ((), ())),
                    preferred_element_type=F32).astype(BF16)
                mine[pl.ds(r0, 256), pl.ds(col, 1024)] = v[:256]
                mine[pl.ds(r1, 256), pl.ds(col, 1024)] = v[256:]
                return 0

            lax.fori_loop(0, 2, body, 0)
            for o in offs[::-1]:
                k = o[0] * 4 + o[1]
                pairs[o] = pltpu.make_async_remote_copy(
                    blk(p.at(o[0], o[1]) + 1 - 2 * p.k), pair.at[k], send.at[0], pair_sem.at[k],
                    device_id={"exp": p.partner}, device_id_type=MESH)
                pairs[o].start()

    done = set()

    def node(q, a, b):
        dx, dz = shift(q, a, b)
        o = (-dx % 4, -dz % 4)
        j = o[0] * 4 + o[1]
        if o not in done:
            done.add(o)
            pairs[o].wait_recv()
        kids = []
        for _, _, na, nb in children(q, a, b):
            i = q * 15 + na * 4 + nb - 1
            kids.append(i)
            pltpu.make_async_remote_copy(
                rbuf.at[i], rbuf.at[i], send.at[2], recv_sem.at[i],
                device_id={"exp": p.partner}, device_id_type=MESH).wait_recv()
        dest = p.at(-dx, -dz)
        rows = pl.ds(q * 32, 32)
        drows = pl.ds(pl.multiple_of(dest * TOK + q * 32, 32), 32)
        root = a == 0 and b == 0

        def add(n, _):
            cols = pl.ds(pl.multiple_of(n * 512, 512), 512)
            v = mine[drows, cols].astype(F32) + pair[j, rows, cols].astype(F32)
            for i in kids:
                v = v + rbuf[i, :, cols].astype(F32)
            if root:
                t = shbuf[3, rows, cols].astype(F32)
                for i in range(3):
                    t = t + shbuf[i, rows, cols].astype(F32)
                out_ref[rows, cols] = (hid_ref[rows, cols] + v + t).astype(BF16)
            else:
                mine[drows, cols] = v.astype(BF16)
            return 0

        lax.fori_loop(0, 4, add, 0)
        if not root:
            first, second, t = route(q)
            dim, code = (second, b) if b else (first, a)
            i = q * 15 + a * 4 + b - 1
            pltpu.make_async_remote_copy(
                mine.at[drows], rbuf.at[i], send.at[2], recv_sem.at[i],
                device_id={"exp": p.step(dim, -hop(code, t))}, device_id_type=MESH).start()

    todo = sorted((-depth(a, b), b, a, q) for q in range(4) for a in range(4) for b in range(4))

    def nodes(i):
        for _, b, a, q in todo:
            dx, dz = shift(q, a, b)
            if (-dx % 4, -dz % 4) in CHUNKS[i] and (a or b):
                node(q, a, b)

    put(3)
    put(2)
    nodes(3)
    put(1)
    nodes(2)
    put(0)
    nodes(1)
    nodes(0)
    for s in shares:
        s.wait_recv()
    sh_own.wait()
    for q in range(4):
        node(q, 0, 0)
    ref = pair
    pltpu.make_async_copy(ref, ref, send.at[0]).wait()
    ref = shbuf.at[pl.ds(0, 3)]
    pltpu.make_async_copy(ref, ref, send.at[1]).wait()
    pltpu.make_async_copy(rbuf, rbuf, send.at[2]).wait()


def call_return(hid, tgt, y, sh):
    return pl.pallas_call(
        kernel_return,
        out_shape=jax.ShapeDtypeStruct((TOK, D), BF16),
        in_specs=[VM, VM, ANY, ANY],
        out_specs=VM,
        scratch_shapes=[
            pltpu.VMEM((32 * CAP, D), BF16),
            pltpu.VMEM((32 * TOK, D), BF16),
            pltpu.VMEM((16, TOK, D), BF16),
            pltpu.VMEM((60, 32, D), BF16),
            pltpu.VMEM((4, TOK, D), BF16),
            pltpu.SemaphoreType.DMA((16,)),
            pltpu.SemaphoreType.DMA((60,)),
            pltpu.SemaphoreType.DMA((4,)),
            pltpu.SemaphoreType.DMA((3,)),
            pltpu.SemaphoreType.DMA((4,)),
        ],
        compiler_params=pltpu.CompilerParams(collective_id=2, has_side_effects=True, vmem_limit_bytes=VMEM_LIMIT),
        name="give_back",
    )(hid, tgt, y, sh)


def on_device(queries, keys_then_values, residual, norm_gain, prompt_lengths, expert_ids, router_logits,
              w_gate, w_up, w_down, w_shared_gate, w_shared_up, w_shared_down, page_table):
    pad = ((0, 0), (0, SPAD - 704))
    w1 = jnp.concatenate([jnp.pad(w, pad) for w in (w_shared_gate, w_shared_up)], axis=1)
    w2 = jnp.pad(w_shared_down, pad)
    two = ((0, 0), (0, 2))
    meta = jnp.concatenate([
        jnp.pad(expert_ids.astype(F32), two, constant_values=-1.0),
        jnp.pad(router_logits, two, constant_values=-1e30)], axis=1).T
    hid, normed, log_totals, cache, tgt, wt = call_attend(
        prompt_lengths, page_table, keys_then_values, meta, queries, residual, norm_gain.reshape(1, D))
    y, sh = call_moe(normed, tgt, wt, w1, w2, w_gate, w_up, w_down)
    out = call_return(hid, tgt, y, sh)
    return out, cache.reshape(8, PAGE, 1024), log_totals


def solution(mesh):
    tok = P(("req", "exp"), None)
    ex = P("exp", None, None)
    sh = P("exp", "req")
    return jax.shard_map(
        on_device,
        mesh=mesh,
        in_specs=(tok, tok, tok, P(), P("req", None), tok, tok, ex, ex, ex, sh, sh, sh, P()),
        out_specs=(tok, P(("req", "exp"), None, None), P(None, ("req", "exp"))),
        check_vma=False,
    )
```

```python
import functools

import jax
import jax.numpy as jnp
from jax import lax
from jax.experimental import pallas as pl
from jax.experimental.pallas import tpu as pltpu
from jax.sharding import PartitionSpec as P

D = 2048
QUERY_HEADS = 16
KEY_VALUE_HEADS = 4
HEAD_SIZE = 128
FF = 1408
TOPK = 6
PAGE = 16
CAP = 36
TOK = 128
SPAD = 768
MAXLEN = 3072
eps_norm = 1e-06
MESH = pl.DeviceIdType.MESH
CODES = (0, 1, -1, 2)
ANY = pl.BlockSpec(memory_space=pl.ANY)
VM = pl.BlockSpec(memory_space=pltpu.VMEM)
SM = pl.BlockSpec(memory_space=pltpu.SMEM)
F32 = jnp.float32
BF16 = jnp.bfloat16
VMEM_LIMIT = 62 * 1024 * 1024


class Place:
    def __init__(self):
        c = lax.axis_index("exp")
        self.c = c
        self.r = lax.axis_index("req")
        self.z = c // 8
        self.x = lax.rem(c // 2, 4)
        self.k = lax.rem(c, 2)
        self.partner = c + 1 - 2 * self.k

    def at(self, dx, dz):
        return lax.rem(self.z + dz + 4, 4) * 8 + lax.rem(self.x + dx + 4, 4) * 2 + self.k

    def step(self, dim, s):
        return self.at(s, 0) if dim == "x" else self.at(0, s)

    def up(self, s):
        return lax.rem(self.r + s + 4, 4)

    def barrier(self, along_y):
        sem = pltpu.get_barrier_semaphore()
        peers = [self.at(1, 0), self.at(-1, 0), self.at(0, 1), self.at(0, -1), self.partner]
        for p in peers:
            pl.semaphore_signal(sem, inc=1, device_id={"exp": p}, device_id_type=MESH)
        for s in along_y:
            pl.semaphore_signal(sem, inc=1, device_id={"req": self.up(s)}, device_id_type=MESH)
        pl.semaphore_wait(sem, len(peers) + len(along_y))


def route(q):
    first, second = ("x", "z") if q < 2 else ("z", "x")
    return first, second, (1 if q % 2 == 0 else -1)


def shift(q, a, b):
    first, _, t = route(q)
    u, v = CODES[a] * t, CODES[b] * t
    return (u, v) if first == "x" else (v, u)


def hop(code, t):
    return -t if code == 2 else t


def depth(a, b):
    return abs(CODES[a]) + abs(CODES[b])


def children(q, a, b):
    first, second, t = route(q)
    out = []
    if b == 0:
        if a == 0:
            out += [(first, t, 1, 0), (first, -t, 2, 0)]
        elif a == 1:
            out += [(first, t, 3, 0)]
        out += [(second, t, a, 1), (second, -t, a, 2)]
    elif b == 1:
        out += [(second, t, a, 3)]
    return out


NEAR = (
    ((0, 0), (1, 0), (3, 0), (0, 1), (0, 3)),
    ((1, 1), (1, 3), (3, 1), (3, 3), (2, 0), (0, 2)),
    ((2, 1), (2, 3), (1, 2), (3, 2), (2, 2)),
)
CHUNKS = (NEAR[0][:1], NEAR[0][1:], NEAR[1], NEAR[2])
BASE = (0, 80, 368, 800)
SPAN = (80, 288, 432, 368)
Y_ROWS = 1168


def parts_of(i):
    return [CHUNKS[i][k:k + 2] for k in range(0, len(CHUNKS[i]), 2)]


class Gather:
    def __init__(self, place, own, every, rows, pieces, send_sem, recv_sem, pair_sem, groups=None):
        self.groups = groups or (tuple((i, j) for i in range(4) for j in range(4)),)
        self.p, self.own, self.every, self.rows, self.pieces = place, own, every, rows, pieces
        self.rq = rows // pieces
        self.send_sem, self.recv_sem, self.pair_sem = send_sem, recv_sem, pair_sem

    def slot(self, src, q):
        return self.every.at[pl.ds(pl.multiple_of(src * self.rows + q * self.rq, self.rq), self.rq)]

    def block(self, src):
        return self.every.at[pl.ds(pl.multiple_of(src * self.rows, self.rows), self.rows)]

    def source(self, q, a, b):
        dx, dz = shift(q, a, b)
        return self.p.at(-dx, -dz)

    def recv_of(self, q, a, b):
        return self.recv_sem.at[q * 15 + a * 4 + b - 1]

    def pass_on(self, q, a, b):
        src = self.source(q, a, b)
        ref = self.own.at[pl.ds(q * self.rq, self.rq)] if a == 0 and b == 0 else self.slot(src, q)
        for dim, s, na, nb in children(q, a, b):
            pltpu.make_async_remote_copy(
                ref, self.slot(src, q), self.send_sem, self.recv_of(q, na, nb),
                device_id={"exp": self.p.step(dim, s)}, device_id_type=MESH,
            ).start()

    def group(self, q, a, b):
        dx, dz = shift(q, a, b)
        return [i for i, g in enumerate(self.groups) if (-dx % 4, -dz % 4) in g][0]

    def to_pair(self, ref, dst, group):
        pltpu.make_async_remote_copy(
            ref, dst, self.send_sem, self.pair_sem.at[group],
            device_id={"exp": self.p.partner}, device_id_type=MESH,
        ).start()

    def start(self):
        for q in range(self.pieces):
            self.pass_on(q, 0, 0)
        self.to_pair(self.own, self.block(self.p.c), 0)

    def events(self):
        out = []
        for q in range(self.pieces):
            for a in range(4):
                for b in range(4):
                    if a or b:
                        out.append((self.group(q, a, b), depth(a, b), b, a, q))
        return sorted(out)

    def take(self, ev):
        _, _, b, a, q = ev
        ref = self.slot(self.source(q, a, b), q)
        pltpu.make_async_remote_copy(
            ref, ref, self.send_sem, self.recv_of(q, a, b),
            device_id={"exp": self.p.partner}, device_id_type=MESH,
        ).wait_recv()
        self.pass_on(q, a, b)
        self.to_pair(ref, ref, self.group(q, a, b))

    def wait_pair(self, group=0):
        ref = self.every.at[pl.ds(0, len(self.groups[group]) * self.rows)]
        pltpu.make_async_remote_copy(
            ref, ref, self.send_sem, self.pair_sem.at[group],
            device_id={"exp": self.p.partner}, device_id_type=MESH,
        ).wait_recv()

    def drain(self):
        ref = self.every.at[pl.ds(0, 31 * self.rows)]
        pltpu.make_async_copy(ref, ref, self.send_sem).wait()


class RingY:
    def __init__(self, place, own, every, rows, send_sem, recv_sem):
        self.p, self.own, self.every, self.rows = place, own, every, rows
        self.h = rows // 2
        self.send_sem, self.recv_sem = send_sem, recv_sem

    def slot(self, src, q):
        return self.every.at[pl.ds(pl.multiple_of(src * self.rows + q * self.h, self.h), self.h)]

    def send(self, ref, src, q, s, code):
        pltpu.make_async_remote_copy(
            ref, self.slot(src, q), self.send_sem, self.recv_sem.at[q * 3 + code - 1],
            device_id={"req": self.p.up(s)}, device_id_type=MESH,
        ).start()

    def start(self):
        for q, t in ((0, 1), (1, -1)):
            ref = self.own.at[pl.ds(q * self.h, self.h)]
            self.send(ref, self.p.r, q, t, 1)
            self.send(ref, self.p.r, q, -t, 2)

    def finish(self, codes=(1, 2, 3)):
        for code in codes:
            for q, t in ((0, 1), (1, -1)):
                src = self.p.up(-CODES[code] * t)
                ref = self.slot(src, q)
                pltpu.make_async_remote_copy(
                    ref, ref, self.send_sem, self.recv_sem.at[q * 3 + code - 1],
                    device_id={"req": self.p.up(1)}, device_id_type=MESH,
                ).wait_recv()
                if code == 1:
                    self.send(ref, src, q, t, 3)

    def drain(self):
        ref = self.every.at[pl.ds(0, 3 * self.rows)]
        pltpu.make_async_copy(ref, ref, self.send_sem).wait()


def attend_start(c, q_ref, len_ref, qs, m_s, l_s, acc_s, lt_s, beg_s):
    for h in range(QUERY_HEADS):
        qs[pl.ds(h * TOK, TOK), :] = q_ref[:, h * HEAD_SIZE:(h + 1) * HEAD_SIZE]
    qpos = c * TOK + lax.broadcasted_iota(jnp.int32, (TOK, 1), 0)
    begin = jnp.zeros((TOK, 1), jnp.int32)
    end = len_ref[0, 0]
    for j in range(16):
        begin = jnp.where(qpos >= end, end, begin)
        if j < 15:
            end = end + len_ref[0, j + 1]
    beg_s[...] = begin
    m_s[...] = jnp.full_like(m_s, -5e29)
    l_s[...] = jnp.zeros_like(l_s)
    acc_s[...] = jnp.zeros_like(acc_s)
    lt_s[...] = jnp.zeros_like(lt_s)


def near_offset(group, i):
    odd = 1 + 2 * lax.rem(i, 2)
    if group == 1:
        h = i // 4
        v = 1 + 2 * lax.rem(i // 2, 2)
        return (1 - h) * v + h * 2 * (1 - lax.rem(i, 2)), (1 - h) * odd + h * 2 * lax.rem(i, 2)
    h, k = i // 4, lax.rem(i // 2, 2)
    if group == 0:
        return (1 - h) * (1 - k) * odd, (1 - h) * k * odd
    return (1 - h) * ((1 - k) * 2 + k * odd) + 2 * h, (1 - h) * ((1 - k) * odd + k * 2) + 2 * h


def attend_chunks(p, group, kv_ref, qs, m_s, l_s, acc_s, beg_s):
    rows = 4 * TOK
    c = p.c
    first = jnp.maximum(c * TOK - MAXLEN, 0) // 256
    last = c // 2

    def chunk(i, _):
        dx, dz = near_offset(group, i)
        chip = lax.rem(p.z + dz, 4) * 4 + lax.rem(p.x + dx, 4)

        @pl.when((chip >= first) & (chip <= last))
        def _():
            k0 = pl.multiple_of(chip * 256, 256)
            kpos = k0 + lax.broadcasted_iota(jnp.int32, (TOK, 256), 1)
            qp = c * TOK + lax.broadcasted_iota(jnp.int32, (TOK, 256), 0)
            seen = (kpos >= beg_s[...]) & (kpos <= qp)
            bias = jnp.where(seen, 0.0, -1e30).astype(F32)
            bias = jnp.concatenate([bias] * 4, axis=0)
            for g in range(KEY_VALUE_HEADS):
                at = pl.ds(g * rows, rows)
                keys = kv_ref[pl.ds(k0, 256), g * HEAD_SIZE:(g + 1) * HEAD_SIZE]
                values = kv_ref[pl.ds(k0, 256), 512 + g * HEAD_SIZE:512 + (g + 1) * HEAD_SIZE]
                s = lax.dot_general(qs[at, :], keys, (((1,), (1,)), ((), ())), preferred_element_type=F32)
                s = s * HEAD_SIZE ** (-0.5) + bias
                old = m_s[at, :]
                new = jnp.maximum(old, jnp.max(s, axis=1, keepdims=True))
                e = jnp.exp(s - jnp.concatenate([new, new], axis=1))
                alpha = jnp.exp(old - new)
                m_s[at, :] = new
                l_s[at, :] = l_s[at, :] * alpha + jnp.sum(e, axis=1, keepdims=True)
                acc_s[at, :] = acc_s[at, :] * alpha + jnp.dot(e.astype(BF16), values, preferred_element_type=F32)

        return 0

    lax.fori_loop(0, len(NEAR[group]), chunk, 0)


def place_pages(p, table_ref, pg_all, cache_ref):
    block = lax.broadcasted_iota(jnp.int32, (1, 512), 1) // PAGE
    slot = jnp.full((1, 512), -1, jnp.int32)
    for g in range(4):
        for j in range(8):
            slot = jnp.where(block == g * 8 + j, table_ref[g, p.c * 8 + j] - (p.r * 256 + p.c * 8), slot)
    i0 = lax.broadcasted_iota(jnp.int32, (TOK, 512), 0)
    i1 = lax.broadcasted_iota(jnp.int32, (TOK, 512), 1)
    hit = (slot == i0 // PAGE) & (lax.rem(i0, PAGE) == lax.rem(i1, PAGE))
    one = jnp.where(hit, 1.0, 0.0).astype(BF16)
    cache_ref[...] = jnp.dot(one, pg_all[...], preferred_element_type=F32).astype(BF16)


def attend_end(res_ref, gain_ref, hid_ref, normed_ref, lt_ref, m_s, l_s, acc_s, lt_s):
    total = jnp.zeros((TOK, 1), F32)
    for h in range(QUERY_HEADS):
        at = pl.ds(h * TOK, TOK)
        cols = slice(h * HEAD_SIZE, (h + 1) * HEAD_SIZE)
        att = (acc_s[at, :] / l_s[at, :]).astype(BF16)
        lane = lax.broadcasted_iota(jnp.int32, (TOK, 128), 1)
        lt_s[...] = jnp.where(lane == h, m_s[at, :] + jnp.log(l_s[at, :]), lt_s[...])
        hid = res_ref[:, cols].astype(F32) + att.astype(F32)
        hid_ref[:, cols] = hid
        total = total + jnp.sum(hid * hid, axis=1, keepdims=True)
    scale = lax.rsqrt(total * (1.0 / D) + eps_norm)
    for h in range(QUERY_HEADS):
        cols = slice(h * HEAD_SIZE, (h + 1) * HEAD_SIZE)
        normed_ref[:, cols] = (hid_ref[:, cols] * scale * gain_ref[:, cols].astype(F32)).astype(BF16)
    lt_ref[...] = jnp.transpose(lt_s[...])[:QUERY_HEADS, :]


def kernel_attend(len_ref, table_ref, kv_ref, w_ref, meta_ref, q_ref, res_ref, gain_ref,
                  w_all, hid_ref, normed_ref, lt_ref, cache_ref, tgt_ref, wt_ref,
                  kv_all, w_s, meta_all, pg_all, qs, m_s, l_s, acc_s, lt_s, beg_s,
                  kv_r, w_r, meta_r, pg_r, send, kv_pair, pair, local):
    p = Place()
    c = p.c
    p.barrier((1, -1))
    kv = Gather(p, kv_ref, kv_all, TOK, 4, send.at[0], kv_r, kv_pair, NEAR)
    w = Gather(p, w_ref, w_s, 64, 4, send.at[1], w_r, pair.at[pl.ds(0, 1)], None)
    meta = Gather(p, meta_ref, meta_all, 16, 1, send.at[2], meta_r, pair.at[pl.ds(1, 1)], None)
    pages = RingY(p, kv_ref, pg_all, TOK, send.at[3], pg_r)
    meta.start()
    kv.start()
    pages.start()
    w_s[pl.ds(pl.multiple_of(c * 64, 64), 64), :] = w_ref[...]
    kv_all[pl.ds(pl.multiple_of(c * TOK, TOK), TOK), :] = kv_ref[...]
    meta_all[pl.ds(pl.multiple_of(c * 16, 16), 16), :] = meta_ref[...]
    pg_all[pl.ds(pl.multiple_of(p.r * TOK, TOK), TOK), :] = kv_ref[...]
    def run(g, d):
        for ev in sorted(g.events(), key=lambda ev: ev[1:]):
            if ev[1] in d:
                g.take(ev)

    attention = (kv_all, qs, m_s, l_s, acc_s, beg_s)
    attend_start(c, q_ref, len_ref, qs, m_s, l_s, acc_s, lt_s, beg_s)
    run(kv, (1,))
    run(meta, (1,))
    pages.finish((1,))
    run(meta, (2,))
    run(kv, (2,))
    w.start()
    kv.wait_pair(0)
    attend_chunks(p, 0, *attention)
    run(kv, (3, 4))
    run(w, (1,))
    run(meta, (3, 4))
    pages.finish((2, 3))
    kv.wait_pair(1)
    attend_chunks(p, 1, *attention)
    run(w, (2,))
    kv.wait_pair(2)
    attend_chunks(p, 2, *attention)
    run(w, (3,))
    meta.wait_pair()
    plan_rows(c.astype(F32), meta_all, tgt_ref, wt_ref)
    run(w, (4,))
    w.wait_pair()
    w_out = pltpu.make_async_copy(w_s, w_all, local)
    w_out.start()
    attend_end(res_ref, gain_ref, hid_ref, normed_ref, lt_ref, m_s, l_s, acc_s, lt_s)
    place_pages(p, table_ref, pg_all, cache_ref)
    for g in (kv, w, meta):
        g.drain()
    pages.drain()
    w_out.wait()


def call_attend(lengths, table, kv, wcat, meta, q, res, gain):
    n = QUERY_HEADS * TOK
    return pl.pallas_call(
        kernel_attend,
        out_shape=(
            jax.ShapeDtypeStruct((D, 3 * SPAD), BF16),
            jax.ShapeDtypeStruct((TOK, D), F32),
            jax.ShapeDtypeStruct((TOK, D), BF16),
            jax.ShapeDtypeStruct((QUERY_HEADS, TOK), F32),
            jax.ShapeDtypeStruct((TOK, 1024), BF16),
            jax.ShapeDtypeStruct((32, 128), F32),
            jax.ShapeDtypeStruct((32, 128), F32),
        ),
        in_specs=[SM, SM] + [VM] * 6,
        out_specs=(ANY,) + (VM,) * 6,
        scratch_shapes=[
            pltpu.VMEM((32 * TOK, 1024), BF16),
            pltpu.VMEM((D, 3 * SPAD), BF16),
            pltpu.VMEM((512, 128), F32),
            pltpu.VMEM((512, 1024), BF16),
            pltpu.VMEM((n, HEAD_SIZE), BF16),
            pltpu.VMEM((n, HEAD_SIZE), F32),
            pltpu.VMEM((n, HEAD_SIZE), F32),
            pltpu.VMEM((n, HEAD_SIZE), F32),
            pltpu.VMEM((TOK, 128), F32),
            pltpu.VMEM((TOK, 1), jnp.int32),
            pltpu.SemaphoreType.DMA((60,)),
            pltpu.SemaphoreType.DMA((60,)),
            pltpu.SemaphoreType.DMA((15,)),
            pltpu.SemaphoreType.DMA((6,)),
            pltpu.SemaphoreType.DMA((4,)),
            pltpu.SemaphoreType.DMA((3,)),
            pltpu.SemaphoreType.DMA((2,)),
            pltpu.SemaphoreType.DMA,
        ],
        compiler_params=pltpu.CompilerParams(collective_id=0, has_side_effects=True, vmem_limit_bytes=VMEM_LIMIT),
        name="attend",
    )(lengths, table, kv, wcat, meta, q, res, gain)


def silu_mul(g, u):
    return (g / (1.0 + jnp.exp(-g)) * u).astype(BF16)


def shared_up(rows_ref, w_ref, act_s):
    def up(j, _):
        col = pl.multiple_of(j * 256, 256)
        g = jnp.dot(rows_ref[...], w_ref[:, pl.ds(col, 256)], preferred_element_type=F32)
        u = jnp.dot(rows_ref[...], w_ref[:, pl.ds(SPAD + col, 256)], preferred_element_type=F32)
        act_s[:, pl.ds(col, 256)] = silu_mul(g, u)
        return 0

    lax.fori_loop(0, 3, up, 0)


def shared_down(w_ref, act_s, out_ref):
    def down(j, _):
        col = pl.multiple_of(j * 256, 256)
        o = lax.dot_general(act_s[...], w_ref[pl.ds(col, 256), 2 * SPAD:], (((1,), (1,)), ((), ())),
                            preferred_element_type=F32)
        out_ref[:, pl.ds(col, 256)] = o.astype(BF16)
        return 0

    lax.fori_loop(0, 8, down, 0)


def plan_rows(e, meta_ref, tgt_s, wt_s):
    tgt_s[...] = jnp.zeros_like(tgt_s)
    for s in range(32):
        ids = meta_ref[pl.ds(s * 16, 8), :]
        logits = meta_ref[pl.ds(s * 16 + 8, 8), :]
        wts = jnp.exp(logits - jnp.max(logits, axis=0, keepdims=True))
        wts = wts / jnp.sum(wts, axis=0, keepdims=True)
        hit = jnp.where(ids == e, 1.0, 0.0).astype(F32)
        tgt_s[s:s + 1, :] = jnp.sum(hit, axis=0, keepdims=True)
        wt_s[s:s + 1, :] = jnp.sum(hit * wts, axis=0, keepdims=True)
    sel = tgt_s[...]
    i0 = lax.broadcasted_iota(jnp.int32, (128, 128), 0)
    i1 = lax.broadcasted_iota(jnp.int32, (128, 128), 1)
    tri = jnp.where(i0 <= i1, 1.0, 0.0).astype(BF16)
    rank = jnp.dot(sel.astype(BF16), tri, preferred_element_type=F32)
    core = lax.rem(lax.broadcasted_iota(jnp.int32, (32, 128), 0), 2).astype(F32)
    tgt_s[...] = jnp.where(sel > 0.5, core * CAP + rank - 1.0, -1000.0)


def join_rows(ref, devs, step):
    rows = []
    for k, d in enumerate(devs):
        t = ref[pl.ds(d, 2), :] + k * step
        rows += [t[0:1, :], t[1:2, :]]
    return jnp.concatenate(rows, axis=1)


def pick(tgt_ref, devs):
    n = len(devs)
    trow = join_rows(tgt_ref, devs, 2.0 * CAP)
    return lax.broadcasted_iota(jnp.int32, (2 * CAP * n, 256 * n), 0).astype(F32) == trow


def chip_of(p, o):
    return pl.multiple_of(p.at(o[0], o[1]) - p.k, 2)


def kernel_moe(n_ref, tgt_ref, wt_ref, w_hbm, wg_h, wu_h, wd_h, y_out, sh_out,
               n_all, y_all, w_s, wg, wu, wd, x_s, act_s, y_s, sact, sho,
               n_r, y_r, send, pair, w_sem, out_sem):
    p = Place()
    p.barrier((1, -1))
    g = Gather(p, n_ref, n_all, TOK, 4, send.at[0], n_r, pair, CHUNKS)
    y = RingY(p, n_ref, y_all, TOK, send.at[1], y_r)
    g.start()
    y.start()
    ws = [pltpu.make_async_copy(a, b, w_sem.at[i]) for i, (a, b) in enumerate(
        ((wg_h.at[0], wg), (wu_h.at[0], wu), (wd_h.at[0], wd), (w_hbm, w_s)))]
    for w in ws:
        w.start()
    n_all[pl.ds(pl.multiple_of(p.c * TOK, TOK), TOK), :] = n_ref[...]
    y_all[pl.ds(pl.multiple_of(p.r * TOK, TOK), TOK), :] = n_ref[...]
    evs = g.events()
    state = {"at": 0}
    last = {ev[0]: i for i, ev in enumerate(evs)}

    def tick(n):
        for ev in evs[state["at"]:state["at"] + n]:
            g.take(ev)
        state["at"] = min(len(evs), state["at"] + n)

    def chunk(i, ticks):
        tick(max(0, last.get(i, -1) + 1 - state["at"]))
        g.wait_pair(i)
        m = 2 * CAP * len(CHUNKS[i])
        wcols = []
        for j, part in enumerate(parts_of(i)):
            devs = [chip_of(p, o) for o in part]
            hit = pick(tgt_ref, devs)
            wcols.append(jnp.sum(jnp.where(hit, join_rows(wt_ref, devs, 0.0), 0.0), axis=1, keepdims=True))
            one = jnp.where(hit, 1.0, 0.0).astype(BF16)
            starts = [pl.multiple_of(d * TOK, 256) for d in devs]

            def fetch(n, _, j=j, one=one, starts=starts):
                col = pl.multiple_of(n * 512, 512)
                v = 0.0
                for k, r in enumerate(starts):
                    v = v + jnp.dot(one[:, k * 256:(k + 1) * 256], n_all[pl.ds(r, 256), pl.ds(col, 512)],
                                    preferred_element_type=F32)
                x_s[pl.ds(j * 144, 72 * len(starts)), pl.ds(col, 512)] = v.astype(BF16)
                return 0

            lax.fori_loop(0, 4, fetch, 0)
            tick(ticks[0])
        wcol = jnp.concatenate(wcols, axis=0) if len(wcols) > 1 else wcols[0]
        if i == 0:
            ws[0].wait()
            ws[1].wait()

        def up(col, n):
            gv = jnp.dot(x_s[:m, :], wg[:, pl.ds(col, n)], preferred_element_type=F32)
            uv = jnp.dot(x_s[:m, :], wu[:, pl.ds(col, n)], preferred_element_type=F32)
            act_s[:m, pl.ds(col, n)] = silu_mul(gv, uv)

        def up_body(j, _):
            up(pl.multiple_of(j * 512, 512), 512)
            return 0

        lax.fori_loop(0, 2, up_body, 0)
        tick(ticks[1])
        up(1024, 384)
        tick(ticks[2])
        if i == 0:
            ws[2].wait()

        def down(j, _):
            col = pl.multiple_of(j * 512, 512)
            o = jnp.dot(act_s[:m, :], wd[:, pl.ds(col, 512)], preferred_element_type=F32)
            y_s[pl.ds(BASE[i], m), pl.ds(col, 512)] = (o * wcol).astype(BF16)
            return 0

        lax.fori_loop(0, 4, down, 0)
        tick(ticks[3])
        rows = pl.ds(BASE[i], SPAN[i])
        out = pltpu.make_async_copy(y_s.at[rows], y_out.at[rows], out_sem.at[i])
        out.start()
        return out

    outs = [chunk(0, (0, 0, 0, 4))]
    y.finish((1,))
    outs.append(chunk(1, (2, 4, 2, 3)))
    y.finish((2, 3))
    ws[3].wait()
    shared_up(y_all, w_s, sact)
    tick(6)
    shared_down(w_s, sact, sho)
    tick(3)
    outs.append(pltpu.make_async_copy(sho, sh_out, out_sem.at[4]))
    outs[-1].start()
    outs.append(chunk(2, (2, 5, 3, 4)))
    outs.append(chunk(3, (0, 0, 0, 0)))
    g.drain()
    y.drain()
    for o in outs:
        o.wait()


def call_moe(normed, tgt, wt, w_all, wg, wu, wd):
    return pl.pallas_call(
        kernel_moe,
        out_shape=(
            jax.ShapeDtypeStruct((Y_ROWS, D), BF16),
            jax.ShapeDtypeStruct((512, D), BF16),
        ),
        in_specs=[VM, VM, VM, ANY, ANY, ANY, ANY],
        out_specs=(ANY, ANY),
        scratch_shapes=[
            pltpu.VMEM((32 * TOK, D), BF16),
            pltpu.VMEM((512, D), BF16),
            pltpu.VMEM((D, 3 * SPAD), BF16),
            pltpu.VMEM((D, FF), BF16),
            pltpu.VMEM((D, FF), BF16),
            pltpu.VMEM((FF, D), BF16),
            pltpu.VMEM((12 * CAP, D), BF16),
            pltpu.VMEM((12 * CAP, FF), BF16),
            pltpu.VMEM((Y_ROWS, D), BF16),
            pltpu.VMEM((512, SPAD), BF16),
            pltpu.VMEM((512, D), BF16),
            pltpu.SemaphoreType.DMA((60,)),
            pltpu.SemaphoreType.DMA((6,)),
            pltpu.SemaphoreType.DMA((2,)),
            pltpu.SemaphoreType.DMA((4,)),
            pltpu.SemaphoreType.DMA((4,)),
            pltpu.SemaphoreType.DMA((5,)),
        ],
        compiler_params=pltpu.CompilerParams(collective_id=1, has_side_effects=True, vmem_limit_bytes=VMEM_LIMIT),
        name="moe",
    )(normed, tgt, wt, w_all, wg, wu, wd)


def kernel_return(hid_ref, tgt_ref, y_hbm, sh, out_ref, y_ref, mine, pair, rbuf, shbuf, pair_sem, recv_sem,
                  sh_recv, send, y_sem):
    p = Place()
    loads = [pltpu.make_async_copy(y_hbm.at[pl.ds(b, n)], y_ref.at[pl.ds(b, n)], y_sem.at[i])
             for i, (b, n) in enumerate(zip(BASE, SPAN))]
    for i in (3, 2, 1, 0):
        loads[i].start()
    p.barrier((1, -1, 2))
    shares = []
    for i, s in enumerate((1, -1, 2)):
        shares.append(pltpu.make_async_remote_copy(
            sh.at[pl.ds(pl.multiple_of(p.up(s) * TOK, TOK), TOK)], shbuf.at[i], send.at[1], sh_recv.at[i],
            device_id={"req": p.up(s)}, device_id_type=MESH))
        shares[-1].start()
    sh_own = pltpu.make_async_copy(sh.at[pl.ds(pl.multiple_of(p.r * TOK, TOK), TOK)], shbuf.at[3], sh_recv.at[3])
    sh_own.start()

    def blk(dev):
        return mine.at[pl.ds(pl.multiple_of(dev * TOK, TOK), TOK)]

    pairs = {}

    def put(i, which):
        for j in which:
            part = parts_of(i)[j]
            devs = [chip_of(p, o) for o in part]
            one = jnp.where(pick(tgt_ref, devs), 1.0, 0.0).astype(BF16)
            starts = [pl.multiple_of(d * TOK, 256) for d in devs]

            def body(n, _, j=j, one=one, starts=starts):
                col = pl.multiple_of(n * 1024, 1024)
                v = lax.dot_general(
                    one, y_ref[pl.ds(BASE[i] + j * 144, 72 * len(starts)), pl.ds(col, 1024)],
                    (((0,), (0,)), ((), ())), preferred_element_type=F32).astype(BF16)
                for k, r in enumerate(starts):
                    mine[pl.ds(r, 256), pl.ds(col, 1024)] = v[k * 256:(k + 1) * 256]
                return 0

            lax.fori_loop(0, 2, body, 0)
            for o in part:
                k = o[0] * 4 + o[1]
                pairs[o] = pltpu.make_async_remote_copy(
                    blk(p.at(o[0], o[1]) + 1 - 2 * p.k), pair.at[k], send.at[0], pair_sem.at[k],
                    device_id={"exp": p.partner}, device_id_type=MESH)
                pairs[o].start()

    done = set()

    def node(q, a, b):
        dx, dz = shift(q, a, b)
        o = (-dx % 4, -dz % 4)
        j = o[0] * 4 + o[1]
        if o not in done:
            done.add(o)
            pairs[o].wait_recv()
        kids = []
        for _, _, na, nb in children(q, a, b):
            i = q * 15 + na * 4 + nb - 1
            kids.append(i)
            pltpu.make_async_remote_copy(
                rbuf.at[i], rbuf.at[i], send.at[2], recv_sem.at[i],
                device_id={"exp": p.partner}, device_id_type=MESH).wait_recv()
        dest = p.at(-dx, -dz)
        rows = pl.ds(q * 32, 32)
        drows = pl.ds(pl.multiple_of(dest * TOK + q * 32, 32), 32)
        root = a == 0 and b == 0

        def add(n, _):
            cols = pl.ds(pl.multiple_of(n * 512, 512), 512)
            v = mine[drows, cols].astype(F32) + pair[j, rows, cols].astype(F32)
            for i in kids:
                v = v + rbuf[i, :, cols].astype(F32)
            if root:
                t = shbuf[3, rows, cols].astype(F32)
                for i in range(3):
                    t = t + shbuf[i, rows, cols].astype(F32)
                out_ref[rows, cols] = (hid_ref[rows, cols] + v + t).astype(BF16)
            else:
                mine[drows, cols] = v.astype(BF16)
            return 0

        lax.fori_loop(0, 4, add, 0)
        if not root:
            first, second, t = route(q)
            dim, code = (second, b) if b else (first, a)
            i = q * 15 + a * 4 + b - 1
            pltpu.make_async_remote_copy(
                mine.at[drows], rbuf.at[i], send.at[2], recv_sem.at[i],
                device_id={"exp": p.step(dim, -hop(code, t))}, device_id_type=MESH).start()

    todo = sorted((-depth(a, b), b, a, q) for q in range(4) for a in range(4) for b in range(4))

    def nodes(d):
        for dist, b, a, q in todo:
            if -dist == d:
                node(q, a, b)

    loads[3].wait()
    put(3, (2, 1, 0))
    nodes(4)
    loads[2].wait()
    put(2, (0,))
    nodes(3)
    put(2, (1, 2))
    loads[1].wait()
    put(1, (0, 1))
    nodes(2)
    loads[0].wait()
    put(0, (0,))
    nodes(1)
    for s in shares:
        s.wait_recv()
    sh_own.wait()
    for q in range(4):
        node(q, 0, 0)
    ref = pair
    pltpu.make_async_copy(ref, ref, send.at[0]).wait()
    ref = shbuf.at[pl.ds(0, 3)]
    pltpu.make_async_copy(ref, ref, send.at[1]).wait()
    pltpu.make_async_copy(rbuf, rbuf, send.at[2]).wait()


def call_return(hid, tgt, y, sh):
    return pl.pallas_call(
        kernel_return,
        out_shape=jax.ShapeDtypeStruct((TOK, D), BF16),
        in_specs=[VM, VM, ANY, ANY],
        out_specs=VM,
        scratch_shapes=[
            pltpu.VMEM((Y_ROWS, D), BF16),
            pltpu.VMEM((32 * TOK, D), BF16),
            pltpu.VMEM((16, TOK, D), BF16),
            pltpu.VMEM((60, 32, D), BF16),
            pltpu.VMEM((4, TOK, D), BF16),
            pltpu.SemaphoreType.DMA((16,)),
            pltpu.SemaphoreType.DMA((60,)),
            pltpu.SemaphoreType.DMA((4,)),
            pltpu.SemaphoreType.DMA((3,)),
            pltpu.SemaphoreType.DMA((4,)),
        ],
        compiler_params=pltpu.CompilerParams(collective_id=2, has_side_effects=True, vmem_limit_bytes=VMEM_LIMIT),
        name="give_back",
    )(hid, tgt, y, sh)


def on_device(queries, keys_then_values, residual, norm_gain, prompt_lengths, expert_ids, router_logits,
              w_gate, w_up, w_down, w_shared_gate, w_shared_up, w_shared_down, page_table):
    pad = ((0, 0), (0, SPAD - 704))
    wcat = jnp.concatenate([jnp.pad(w, pad) for w in (w_shared_gate, w_shared_up, w_shared_down)], axis=1)
    two = ((0, 0), (0, 2))
    meta = jnp.concatenate([
        jnp.pad(expert_ids.astype(F32), two, constant_values=-1.0),
        jnp.pad(router_logits, two, constant_values=-1e30)], axis=1).T
    w_all, hid, normed, log_totals, cache, tgt, wt = call_attend(
        prompt_lengths, page_table, keys_then_values, wcat, meta, queries, residual, norm_gain.reshape(1, D))
    y, sh = call_moe(normed, tgt, wt, w_all, w_gate, w_up, w_down)
    out = call_return(hid, tgt, y, sh)
    return out, cache.reshape(8, PAGE, 1024), log_totals


def solution(mesh):
    tok = P(("req", "exp"), None)
    ex = P("exp", None, None)
    sh = P("exp", "req")
    return jax.shard_map(
        on_device,
        mesh=mesh,
        in_specs=(tok, tok, tok, P(), P("req", None), tok, tok, ex, ex, ex, sh, sh, sh, P()),
        out_specs=(tok, P(("req", "exp"), None, None), P(None, ("req", "exp"))),
        check_vma=False,
    )
```

```python
import functools

import jax
import jax.numpy as jnp
from jax import lax
from jax.experimental import pallas as pl
from jax.experimental.pallas import tpu as pltpu
from jax.sharding import PartitionSpec as P

D = 2048
QUERY_HEADS = 16
KEY_VALUE_HEADS = 4
HEAD_SIZE = 128
FF = 1408
TOPK = 6
PAGE = 16
CAP = 36
TOK = 128
SPAD = 768
MAXLEN = 3072
eps_norm = 1e-06
MESH = pl.DeviceIdType.MESH
CODES = (0, 1, -1, 2)
ANY = pl.BlockSpec(memory_space=pl.ANY)
VM = pl.BlockSpec(memory_space=pltpu.VMEM)
SM = pl.BlockSpec(memory_space=pltpu.SMEM)
F32 = jnp.float32
BF16 = jnp.bfloat16
VMEM_LIMIT = 62 * 1024 * 1024


class Place:
    def __init__(self):
        c = lax.axis_index("exp")
        self.c = c
        self.r = lax.axis_index("req")
        self.z = c // 8
        self.x = lax.rem(c // 2, 4)
        self.k = lax.rem(c, 2)
        self.partner = c + 1 - 2 * self.k

    def at(self, dx, dz):
        return lax.rem(self.z + dz + 4, 4) * 8 + lax.rem(self.x + dx + 4, 4) * 2 + self.k

    def step(self, dim, s):
        return self.at(s, 0) if dim == "x" else self.at(0, s)

    def up(self, s):
        return lax.rem(self.r + s + 4, 4)

    def barrier(self, along_y):
        sem = pltpu.get_barrier_semaphore()
        peers = [self.at(1, 0), self.at(-1, 0), self.at(0, 1), self.at(0, -1), self.partner]
        for p in peers:
            pl.semaphore_signal(sem, inc=1, device_id={"exp": p}, device_id_type=MESH)
        for s in along_y:
            pl.semaphore_signal(sem, inc=1, device_id={"req": self.up(s)}, device_id_type=MESH)
        pl.semaphore_wait(sem, len(peers) + len(along_y))


def route(q):
    first, second = ("x", "z") if q < 2 else ("z", "x")
    return first, second, (1 if q % 2 == 0 else -1)


def shift(q, a, b):
    first, _, t = route(q)
    u, v = CODES[a] * t, CODES[b] * t
    return (u, v) if first == "x" else (v, u)


def hop(code, t):
    return -t if code == 2 else t


def depth(a, b):
    return abs(CODES[a]) + abs(CODES[b])


def children(q, a, b):
    first, second, t = route(q)
    out = []
    if b == 0:
        if a == 0:
            out += [(first, t, 1, 0), (first, -t, 2, 0)]
        elif a == 1:
            out += [(first, t, 3, 0)]
        out += [(second, t, a, 1), (second, -t, a, 2)]
    elif b == 1:
        out += [(second, t, a, 3)]
    return out


NEAR = (
    ((0, 0), (1, 0), (3, 0), (0, 1), (0, 3)),
    ((1, 1), (1, 3), (3, 1), (3, 3), (2, 0), (0, 2)),
    ((2, 1), (2, 3), (1, 2), (3, 2), (2, 2)),
)
CHUNKS = (NEAR[0][:1], NEAR[0][1:], NEAR[1], NEAR[2])
BASE = (0, 80, 368, 800)
SPAN = (80, 288, 432, 368)
Y_ROWS = 1168


def parts_of(i):
    return [CHUNKS[i][k:k + 2] for k in range(0, len(CHUNKS[i]), 2)]


class Gather:
    def __init__(self, place, own, every, rows, pieces, send_sem, recv_sem, pair_sem, groups=None):
        self.groups = groups or (tuple((i, j) for i in range(4) for j in range(4)),)
        self.p, self.own, self.every, self.rows, self.pieces = place, own, every, rows, pieces
        self.rq = rows // pieces
        self.send_sem, self.recv_sem, self.pair_sem = send_sem, recv_sem, pair_sem

    def slot(self, src, q):
        return self.every.at[pl.ds(pl.multiple_of(src * self.rows + q * self.rq, self.rq), self.rq)]

    def block(self, src):
        return self.every.at[pl.ds(pl.multiple_of(src * self.rows, self.rows), self.rows)]

    def source(self, q, a, b):
        dx, dz = shift(q, a, b)
        return self.p.at(-dx, -dz)

    def recv_of(self, q, a, b):
        return self.recv_sem.at[q * 15 + a * 4 + b - 1]

    def pass_on(self, q, a, b):
        src = self.source(q, a, b)
        ref = self.own.at[pl.ds(q * self.rq, self.rq)] if a == 0 and b == 0 else self.slot(src, q)
        for dim, s, na, nb in children(q, a, b):
            pltpu.make_async_remote_copy(
                ref, self.slot(src, q), self.send_sem, self.recv_of(q, na, nb),
                device_id={"exp": self.p.step(dim, s)}, device_id_type=MESH,
            ).start()

    def group(self, q, a, b):
        dx, dz = shift(q, a, b)
        return [i for i, g in enumerate(self.groups) if (-dx % 4, -dz % 4) in g][0]

    def to_pair(self, ref, dst, group):
        pltpu.make_async_remote_copy(
            ref, dst, self.send_sem, self.pair_sem.at[group],
            device_id={"exp": self.p.partner}, device_id_type=MESH,
        ).start()

    def start(self):
        for q in range(self.pieces):
            self.pass_on(q, 0, 0)
        self.to_pair(self.own, self.block(self.p.c), 0)

    def events(self):
        out = []
        for q in range(self.pieces):
            for a in range(4):
                for b in range(4):
                    if a or b:
                        out.append((self.group(q, a, b), depth(a, b), b, a, q))
        return sorted(out)

    def take(self, ev):
        _, _, b, a, q = ev
        ref = self.slot(self.source(q, a, b), q)
        pltpu.make_async_remote_copy(
            ref, ref, self.send_sem, self.recv_of(q, a, b),
            device_id={"exp": self.p.partner}, device_id_type=MESH,
        ).wait_recv()
        self.pass_on(q, a, b)
        self.to_pair(ref, ref, self.group(q, a, b))

    def wait_pair(self, group=0):
        ref = self.every.at[pl.ds(0, len(self.groups[group]) * self.rows)]
        pltpu.make_async_remote_copy(
            ref, ref, self.send_sem, self.pair_sem.at[group],
            device_id={"exp": self.p.partner}, device_id_type=MESH,
        ).wait_recv()

    def drain(self):
        ref = self.every.at[pl.ds(0, 31 * self.rows)]
        pltpu.make_async_copy(ref, ref, self.send_sem).wait()


class RingY:
    def __init__(self, place, own, every, rows, send_sem, recv_sem):
        self.p, self.own, self.every, self.rows = place, own, every, rows
        self.h = rows // 2
        self.send_sem, self.recv_sem = send_sem, recv_sem

    def slot(self, src, q):
        return self.every.at[pl.ds(pl.multiple_of(src * self.rows + q * self.h, self.h), self.h)]

    def send(self, ref, src, q, s, code):
        pltpu.make_async_remote_copy(
            ref, self.slot(src, q), self.send_sem, self.recv_sem.at[q * 3 + code - 1],
            device_id={"req": self.p.up(s)}, device_id_type=MESH,
        ).start()

    def start(self):
        for q, t in ((0, 1), (1, -1)):
            ref = self.own.at[pl.ds(q * self.h, self.h)]
            self.send(ref, self.p.r, q, t, 1)
            self.send(ref, self.p.r, q, -t, 2)

    def finish(self, codes=(1, 2, 3)):
        for code in codes:
            for q, t in ((0, 1), (1, -1)):
                src = self.p.up(-CODES[code] * t)
                ref = self.slot(src, q)
                pltpu.make_async_remote_copy(
                    ref, ref, self.send_sem, self.recv_sem.at[q * 3 + code - 1],
                    device_id={"req": self.p.up(1)}, device_id_type=MESH,
                ).wait_recv()
                if code == 1:
                    self.send(ref, src, q, t, 3)

    def drain(self):
        ref = self.every.at[pl.ds(0, 3 * self.rows)]
        pltpu.make_async_copy(ref, ref, self.send_sem).wait()


def attend_start(c, q_ref, len_ref, qs, m_s, l_s, acc_s, lt_s, beg_s):
    for h in range(QUERY_HEADS):
        qs[pl.ds(h * TOK, TOK), :] = q_ref[:, h * HEAD_SIZE:(h + 1) * HEAD_SIZE]
    qpos = c * TOK + lax.broadcasted_iota(jnp.int32, (TOK, 1), 0)
    begin = jnp.zeros((TOK, 1), jnp.int32)
    end = len_ref[0, 0]
    for j in range(16):
        begin = jnp.where(qpos >= end, end, begin)
        if j < 15:
            end = end + len_ref[0, j + 1]
    beg_s[...] = begin
    m_s[...] = jnp.full_like(m_s, -5e29)
    l_s[...] = jnp.zeros_like(l_s)
    acc_s[...] = jnp.zeros_like(acc_s)
    lt_s[...] = jnp.zeros_like(lt_s)


def near_offset(group, i):
    odd = 1 + 2 * lax.rem(i, 2)
    if group == 1:
        h = i // 4
        v = 1 + 2 * lax.rem(i // 2, 2)
        return (1 - h) * v + h * 2 * (1 - lax.rem(i, 2)), (1 - h) * odd + h * 2 * lax.rem(i, 2)
    h, k = i // 4, lax.rem(i // 2, 2)
    if group == 0:
        return (1 - h) * (1 - k) * odd, (1 - h) * k * odd
    return (1 - h) * ((1 - k) * 2 + k * odd) + 2 * h, (1 - h) * ((1 - k) * odd + k * 2) + 2 * h


def attend_chunks(p, group, kv_ref, qs, m_s, l_s, acc_s, beg_s):
    rows = 4 * TOK
    c = p.c
    first = jnp.maximum(c * TOK - MAXLEN, 0) // 256
    last = c // 2

    def chunk(i, _):
        dx, dz = near_offset(group, i)
        chip = lax.rem(p.z + dz, 4) * 4 + lax.rem(p.x + dx, 4)

        @pl.when((chip >= first) & (chip <= last))
        def _():
            k0 = pl.multiple_of(chip * 256, 256)
            kpos = k0 + lax.broadcasted_iota(jnp.int32, (TOK, 256), 1)
            qp = c * TOK + lax.broadcasted_iota(jnp.int32, (TOK, 256), 0)
            seen = (kpos >= beg_s[...]) & (kpos <= qp)
            bias = jnp.where(seen, 0.0, -1e30).astype(F32)
            bias = jnp.concatenate([bias] * 4, axis=0)
            for g in range(KEY_VALUE_HEADS):
                at = pl.ds(g * rows, rows)
                keys = kv_ref[pl.ds(k0, 256), g * HEAD_SIZE:(g + 1) * HEAD_SIZE]
                values = kv_ref[pl.ds(k0, 256), 512 + g * HEAD_SIZE:512 + (g + 1) * HEAD_SIZE]
                s = lax.dot_general(qs[at, :], keys, (((1,), (1,)), ((), ())), preferred_element_type=F32)
                s = s * HEAD_SIZE ** (-0.5) + bias
                old = m_s[at, :]
                new = jnp.maximum(old, jnp.max(s, axis=1, keepdims=True))
                e = jnp.exp(s - jnp.concatenate([new, new], axis=1))
                alpha = jnp.exp(old - new)
                m_s[at, :] = new
                l_s[at, :] = l_s[at, :] * alpha + jnp.sum(e, axis=1, keepdims=True)
                acc_s[at, :] = acc_s[at, :] * alpha + jnp.dot(e.astype(BF16), values, preferred_element_type=F32)

        return 0

    lax.fori_loop(0, len(NEAR[group]), chunk, 0)


def place_pages(p, table_ref, pg_all, cache_ref):
    block = lax.broadcasted_iota(jnp.int32, (1, 512), 1) // PAGE
    slot = jnp.full((1, 512), -1, jnp.int32)
    for g in range(4):
        for j in range(8):
            slot = jnp.where(block == g * 8 + j, table_ref[g, p.c * 8 + j] - (p.r * 256 + p.c * 8), slot)
    i0 = lax.broadcasted_iota(jnp.int32, (TOK, 512), 0)
    i1 = lax.broadcasted_iota(jnp.int32, (TOK, 512), 1)
    hit = (slot == i0 // PAGE) & (lax.rem(i0, PAGE) == lax.rem(i1, PAGE))
    one = jnp.where(hit, 1.0, 0.0).astype(BF16)
    cache_ref[...] = jnp.dot(one, pg_all[...], preferred_element_type=F32).astype(BF16)


def attend_end(res_ref, gain_ref, hid_ref, normed_ref, lt_ref, m_s, l_s, acc_s, lt_s):
    total = jnp.zeros((TOK, 1), F32)
    for h in range(QUERY_HEADS):
        at = pl.ds(h * TOK, TOK)
        cols = slice(h * HEAD_SIZE, (h + 1) * HEAD_SIZE)
        att = (acc_s[at, :] / l_s[at, :]).astype(BF16)
        lane = lax.broadcasted_iota(jnp.int32, (TOK, 128), 1)
        lt_s[...] = jnp.where(lane == h, m_s[at, :] + jnp.log(l_s[at, :]), lt_s[...])
        hid = res_ref[:, cols].astype(F32) + att.astype(F32)
        hid_ref[:, cols] = hid
        total = total + jnp.sum(hid * hid, axis=1, keepdims=True)
    scale = lax.rsqrt(total * (1.0 / D) + eps_norm)
    for h in range(QUERY_HEADS):
        cols = slice(h * HEAD_SIZE, (h + 1) * HEAD_SIZE)
        normed_ref[:, cols] = (hid_ref[:, cols] * scale * gain_ref[:, cols].astype(F32)).astype(BF16)
    lt_ref[...] = jnp.transpose(lt_s[...])[:QUERY_HEADS, :]


def kernel_attend(len_ref, table_ref, kv_ref, w_ref, meta_ref, q_ref, res_ref, gain_ref,
                  w_all, hid_ref, normed_ref, lt_ref, cache_ref, tgt_ref, wt_ref,
                  kv_all, w_s, meta_all, pg_all, qs, m_s, l_s, acc_s, lt_s, beg_s,
                  kv_r, w_r, meta_r, pg_r, send, kv_pair, pair, local):
    p = Place()
    c = p.c
    p.barrier((1, -1))
    kv = Gather(p, kv_ref, kv_all, TOK, 4, send.at[0], kv_r, kv_pair, NEAR)
    w = Gather(p, w_ref, w_s, 64, 4, send.at[1], w_r, pair.at[pl.ds(0, 1)], None)
    meta = Gather(p, meta_ref, meta_all, 16, 1, send.at[2], meta_r, pair.at[pl.ds(1, 1)], None)
    pages = RingY(p, kv_ref, pg_all, TOK, send.at[3], pg_r)
    meta.start()
    kv.start()
    pages.start()
    w_s[pl.ds(pl.multiple_of(c * 64, 64), 64), :] = w_ref[...]
    kv_all[pl.ds(pl.multiple_of(c * TOK, TOK), TOK), :] = kv_ref[...]
    meta_all[pl.ds(pl.multiple_of(c * 16, 16), 16), :] = meta_ref[...]
    pg_all[pl.ds(pl.multiple_of(p.r * TOK, TOK), TOK), :] = kv_ref[...]
    def run(g, d):
        for ev in sorted(g.events(), key=lambda ev: ev[1:]):
            if ev[1] in d:
                g.take(ev)

    attention = (kv_all, qs, m_s, l_s, acc_s, beg_s)
    attend_start(c, q_ref, len_ref, qs, m_s, l_s, acc_s, lt_s, beg_s)
    run(kv, (1,))
    run(meta, (1,))
    pages.finish((1,))
    run(meta, (2,))
    run(kv, (2,))
    w.start()
    kv.wait_pair(0)
    attend_chunks(p, 0, *attention)
    run(kv, (3, 4))
    run(w, (1,))
    run(meta, (3, 4))
    pages.finish((2, 3))
    kv.wait_pair(1)
    attend_chunks(p, 1, *attention)
    run(w, (2,))
    kv.wait_pair(2)
    attend_chunks(p, 2, *attention)
    run(w, (3,))
    meta.wait_pair()
    plan_rows(c.astype(F32), meta_all, tgt_ref, wt_ref)
    run(w, (4,))
    w.wait_pair()
    w_out = pltpu.make_async_copy(w_s, w_all, local)
    w_out.start()
    attend_end(res_ref, gain_ref, hid_ref, normed_ref, lt_ref, m_s, l_s, acc_s, lt_s)
    place_pages(p, table_ref, pg_all, cache_ref)
    for g in (kv, w, meta):
        g.drain()
    pages.drain()
    w_out.wait()


def call_attend(lengths, table, kv, wcat, meta, q, res, gain):
    n = QUERY_HEADS * TOK
    return pl.pallas_call(
        kernel_attend,
        out_shape=(
            jax.ShapeDtypeStruct((D, 2 * SPAD), BF16),
            jax.ShapeDtypeStruct((TOK, D), F32),
            jax.ShapeDtypeStruct((TOK, D), BF16),
            jax.ShapeDtypeStruct((QUERY_HEADS, TOK), F32),
            jax.ShapeDtypeStruct((TOK, 1024), BF16),
            jax.ShapeDtypeStruct((32, 128), F32),
            jax.ShapeDtypeStruct((32, 128), F32),
        ),
        in_specs=[SM, SM] + [VM] * 6,
        out_specs=(ANY,) + (VM,) * 6,
        scratch_shapes=[
            pltpu.VMEM((32 * TOK, 1024), BF16),
            pltpu.VMEM((D, 2 * SPAD), BF16),
            pltpu.VMEM((512, 128), F32),
            pltpu.VMEM((512, 1024), BF16),
            pltpu.VMEM((n, HEAD_SIZE), BF16),
            pltpu.VMEM((n, HEAD_SIZE), F32),
            pltpu.VMEM((n, HEAD_SIZE), F32),
            pltpu.VMEM((n, HEAD_SIZE), F32),
            pltpu.VMEM((TOK, 128), F32),
            pltpu.VMEM((TOK, 1), jnp.int32),
            pltpu.SemaphoreType.DMA((60,)),
            pltpu.SemaphoreType.DMA((60,)),
            pltpu.SemaphoreType.DMA((15,)),
            pltpu.SemaphoreType.DMA((6,)),
            pltpu.SemaphoreType.DMA((4,)),
            pltpu.SemaphoreType.DMA((3,)),
            pltpu.SemaphoreType.DMA((2,)),
            pltpu.SemaphoreType.DMA,
        ],
        compiler_params=pltpu.CompilerParams(collective_id=0, has_side_effects=True, vmem_limit_bytes=VMEM_LIMIT),
        name="attend",
    )(lengths, table, kv, wcat, meta, q, res, gain)


def silu_mul(g, u):
    return (g / (1.0 + jnp.exp(-g)) * u).astype(BF16)


def shared_up(rows_ref, w_ref, act_s):
    def up(j, _):
        col = pl.multiple_of(j * 256, 256)
        g = jnp.dot(rows_ref[...], w_ref[:, pl.ds(col, 256)], preferred_element_type=F32)
        u = jnp.dot(rows_ref[...], w_ref[:, pl.ds(SPAD + col, 256)], preferred_element_type=F32)
        act_s[:, pl.ds(col, 256)] = silu_mul(g, u)
        return 0

    lax.fori_loop(0, 3, up, 0)


def shared_down(w_ref, act_s, out_ref):
    def down(j, _):
        col = pl.multiple_of(j * 256, 256)
        o = lax.dot_general(act_s[...], w_ref[pl.ds(col, 256), :], (((1,), (1,)), ((), ())),
                            preferred_element_type=F32)
        out_ref[:, pl.ds(col, 256)] = o.astype(BF16)
        return 0

    lax.fori_loop(0, 8, down, 0)


def plan_rows(e, meta_ref, tgt_s, wt_s):
    tgt_s[...] = jnp.zeros_like(tgt_s)
    for s in range(32):
        ids = meta_ref[pl.ds(s * 16, 8), :]
        logits = meta_ref[pl.ds(s * 16 + 8, 8), :]
        wts = jnp.exp(logits - jnp.max(logits, axis=0, keepdims=True))
        wts = wts / jnp.sum(wts, axis=0, keepdims=True)
        hit = jnp.where(ids == e, 1.0, 0.0).astype(F32)
        tgt_s[s:s + 1, :] = jnp.sum(hit, axis=0, keepdims=True)
        wt_s[s:s + 1, :] = jnp.sum(hit * wts, axis=0, keepdims=True)
    sel = tgt_s[...]
    i0 = lax.broadcasted_iota(jnp.int32, (128, 128), 0)
    i1 = lax.broadcasted_iota(jnp.int32, (128, 128), 1)
    tri = jnp.where(i0 <= i1, 1.0, 0.0).astype(BF16)
    rank = jnp.dot(sel.astype(BF16), tri, preferred_element_type=F32)
    core = lax.rem(lax.broadcasted_iota(jnp.int32, (32, 128), 0), 2).astype(F32)
    tgt_s[...] = jnp.where(sel > 0.5, core * CAP + rank - 1.0, -1000.0)


def join_rows(ref, devs, step):
    rows = []
    for k, d in enumerate(devs):
        t = ref[pl.ds(d, 2), :] + k * step
        rows += [t[0:1, :], t[1:2, :]]
    return jnp.concatenate(rows, axis=1)


def pick(tgt_ref, devs):
    n = len(devs)
    trow = join_rows(tgt_ref, devs, 2.0 * CAP)
    return lax.broadcasted_iota(jnp.int32, (2 * CAP * n, 256 * n), 0).astype(F32) == trow


def chip_of(p, o):
    return pl.multiple_of(p.at(o[0], o[1]) - p.k, 2)


def kernel_moe(n_ref, tgt_ref, wt_ref, w2_ref, w_hbm, wg_h, wu_h, wd_h, y_out, sh_out,
               n_all, y_all, w_s, w2_s, wg, wu, wd, x_s, act_s, y_s, sact, sho,
               n_r, y_r, w2_r, send, pair, w2_pair, w_sem, out_sem):
    p = Place()
    p.barrier((1, -1))
    g = Gather(p, n_ref, n_all, TOK, 4, send.at[0], n_r, pair, CHUNKS)
    y = RingY(p, n_ref, y_all, TOK, send.at[1], y_r)
    g.start()
    y.start()
    ws = [pltpu.make_async_copy(a, b, w_sem.at[i]) for i, (a, b) in enumerate(
        ((wg_h.at[0], wg), (wu_h.at[0], wu), (wd_h.at[0], wd), (w_hbm, w_s)))]
    for w in ws:
        w.start()
    n_all[pl.ds(pl.multiple_of(p.c * TOK, TOK), TOK), :] = n_ref[...]
    y_all[pl.ds(pl.multiple_of(p.r * TOK, TOK), TOK), :] = n_ref[...]
    evs = g.events()
    state = {"at": 0}
    last = {ev[0]: i for i, ev in enumerate(evs)}

    w2 = Gather(p, w2_ref, w2_s, 64, 4, send.at[2], w2_r, w2_pair)
    w2_s[pl.ds(pl.multiple_of(p.c * 64, 64), 64), :] = w2_ref[...]

    def level(d):
        for ev in w2.events():
            if ev[1] == d:
                w2.take(ev)

    def tick(n):
        for ev in evs[state["at"]:state["at"] + n]:
            g.take(ev)
        state["at"] = min(len(evs), state["at"] + n)

    def chunk(i, ticks):
        tick(max(0, last.get(i, -1) + 1 - state["at"]))
        if i == 3:
            w2.start()
        g.wait_pair(i)
        m = 2 * CAP * len(CHUNKS[i])
        wcols = []
        for j, part in enumerate(parts_of(i)):
            devs = [chip_of(p, o) for o in part]
            hit = pick(tgt_ref, devs)
            wcols.append(jnp.sum(jnp.where(hit, join_rows(wt_ref, devs, 0.0), 0.0), axis=1, keepdims=True))
            one = jnp.where(hit, 1.0, 0.0).astype(BF16)
            starts = [pl.multiple_of(d * TOK, 256) for d in devs]

            def fetch(n, _, j=j, one=one, starts=starts):
                col = pl.multiple_of(n * 512, 512)
                v = 0.0
                for k, r in enumerate(starts):
                    v = v + jnp.dot(one[:, k * 256:(k + 1) * 256], n_all[pl.ds(r, 256), pl.ds(col, 512)],
                                    preferred_element_type=F32)
                x_s[pl.ds(j * 144, 72 * len(starts)), pl.ds(col, 512)] = v.astype(BF16)
                return 0

            lax.fori_loop(0, 4, fetch, 0)
            tick(ticks[0])
            if i == 3 and j == 2:
                level(1)
        wcol = jnp.concatenate(wcols, axis=0) if len(wcols) > 1 else wcols[0]
        if i == 0:
            ws[0].wait()
            ws[1].wait()

        def up(col, n):
            gv = jnp.dot(x_s[:m, :], wg[:, pl.ds(col, n)], preferred_element_type=F32)
            uv = jnp.dot(x_s[:m, :], wu[:, pl.ds(col, n)], preferred_element_type=F32)
            act_s[:m, pl.ds(col, n)] = silu_mul(gv, uv)

        def up_body(j, _):
            up(pl.multiple_of(j * 512, 512), 512)
            return 0

        lax.fori_loop(0, 2, up_body, 0)
        tick(ticks[1])
        if i == 3:
            level(2)
        up(1024, 384)
        tick(ticks[2])
        if i == 0:
            ws[2].wait()

        def down(j, _):
            col = pl.multiple_of(j * 512, 512)
            o = jnp.dot(act_s[:m, :], wd[:, pl.ds(col, 512)], preferred_element_type=F32)
            y_s[pl.ds(BASE[i], m), pl.ds(col, 512)] = (o * wcol).astype(BF16)
            return 0

        lax.fori_loop(0, 4, down, 0)
        tick(ticks[3])
        if i == 3:
            level(3)
        rows = pl.ds(BASE[i], SPAN[i])
        out = pltpu.make_async_copy(y_s.at[rows], y_out.at[rows], out_sem.at[i])
        out.start()
        return out

    outs = [chunk(0, (0, 0, 0, 4))]
    y.finish((1,))
    outs.append(chunk(1, (2, 4, 2, 3)))
    y.finish((2, 3))
    ws[3].wait()
    shared_up(y_all, w_s, sact)
    tick(6)
    outs.append(chunk(2, (2, 5, 3, 4)))
    outs.append(chunk(3, (0, 0, 0, 0)))
    level(4)
    w2.wait_pair()
    shared_down(w2_s, sact, sho)
    outs.append(pltpu.make_async_copy(sho, sh_out, out_sem.at[4]))
    outs[-1].start()
    w2.drain()
    g.drain()
    y.drain()
    for o in outs:
        o.wait()


def call_moe(normed, tgt, wt, w2, w_all, wg, wu, wd):
    return pl.pallas_call(
        kernel_moe,
        out_shape=(
            jax.ShapeDtypeStruct((Y_ROWS, D), BF16),
            jax.ShapeDtypeStruct((512, D), BF16),
        ),
        in_specs=[VM, VM, VM, VM, ANY, ANY, ANY, ANY],
        out_specs=(ANY, ANY),
        scratch_shapes=[
            pltpu.VMEM((32 * TOK, D), BF16),
            pltpu.VMEM((512, D), BF16),
            pltpu.VMEM((D, 2 * SPAD), BF16),
            pltpu.VMEM((D, SPAD), BF16),
            pltpu.VMEM((D, FF), BF16),
            pltpu.VMEM((D, FF), BF16),
            pltpu.VMEM((FF, D), BF16),
            pltpu.VMEM((12 * CAP, D), BF16),
            pltpu.VMEM((12 * CAP, FF), BF16),
            pltpu.VMEM((Y_ROWS, D), BF16),
            pltpu.VMEM((512, SPAD), BF16),
            pltpu.VMEM((512, D), BF16),
            pltpu.SemaphoreType.DMA((60,)),
            pltpu.SemaphoreType.DMA((6,)),
            pltpu.SemaphoreType.DMA((60,)),
            pltpu.SemaphoreType.DMA((3,)),
            pltpu.SemaphoreType.DMA((4,)),
            pltpu.SemaphoreType.DMA((1,)),
            pltpu.SemaphoreType.DMA((4,)),
            pltpu.SemaphoreType.DMA((5,)),
        ],
        compiler_params=pltpu.CompilerParams(collective_id=1, has_side_effects=True, vmem_limit_bytes=VMEM_LIMIT),
        name="moe",
    )(normed, tgt, wt, w2, w_all, wg, wu, wd)


def kernel_return(hid_ref, tgt_ref, y_hbm, sh, out_ref, y_ref, mine, pair, rbuf, shbuf, pair_sem, recv_sem,
                  sh_recv, send, y_sem):
    p = Place()
    loads = [pltpu.make_async_copy(y_hbm.at[pl.ds(b, n)], y_ref.at[pl.ds(b, n)], y_sem.at[i])
             for i, (b, n) in enumerate(zip(BASE, SPAN))]
    for i in (3, 2, 1, 0):
        loads[i].start()
    p.barrier((1, -1, 2))
    shares = []
    for i, s in enumerate((1, -1, 2)):
        shares.append(pltpu.make_async_remote_copy(
            sh.at[pl.ds(pl.multiple_of(p.up(s) * TOK, TOK), TOK)], shbuf.at[i], send.at[1], sh_recv.at[i],
            device_id={"req": p.up(s)}, device_id_type=MESH))
        shares[-1].start()
    sh_own = pltpu.make_async_copy(sh.at[pl.ds(pl.multiple_of(p.r * TOK, TOK), TOK)], shbuf.at[3], sh_recv.at[3])
    sh_own.start()

    def blk(dev):
        return mine.at[pl.ds(pl.multiple_of(dev * TOK, TOK), TOK)]

    pairs = {}

    def put(i, which):
        for j in which:
            part = parts_of(i)[j]
            devs = [chip_of(p, o) for o in part]
            one = jnp.where(pick(tgt_ref, devs), 1.0, 0.0).astype(BF16)
            starts = [pl.multiple_of(d * TOK, 256) for d in devs]

            def body(n, _, j=j, one=one, starts=starts):
                col = pl.multiple_of(n * 1024, 1024)
                v = lax.dot_general(
                    one, y_ref[pl.ds(BASE[i] + j * 144, 72 * len(starts)), pl.ds(col, 1024)],
                    (((0,), (0,)), ((), ())), preferred_element_type=F32).astype(BF16)
                for k, r in enumerate(starts):
                    mine[pl.ds(r, 256), pl.ds(col, 1024)] = v[k * 256:(k + 1) * 256]
                return 0

            lax.fori_loop(0, 2, body, 0)
            for o in part:
                k = o[0] * 4 + o[1]
                pairs[o] = pltpu.make_async_remote_copy(
                    blk(p.at(o[0], o[1]) + 1 - 2 * p.k), pair.at[k], send.at[0], pair_sem.at[k],
                    device_id={"exp": p.partner}, device_id_type=MESH)
                pairs[o].start()

    done = set()

    def node(q, a, b):
        dx, dz = shift(q, a, b)
        o = (-dx % 4, -dz % 4)
        j = o[0] * 4 + o[1]
        if o not in done:
            done.add(o)
            pairs[o].wait_recv()
        kids = []
        for _, _, na, nb in children(q, a, b):
            i = q * 15 + na * 4 + nb - 1
            kids.append(i)
            pltpu.make_async_remote_copy(
                rbuf.at[i], rbuf.at[i], send.at[2], recv_sem.at[i],
                device_id={"exp": p.partner}, device_id_type=MESH).wait_recv()
        dest = p.at(-dx, -dz)
        rows = pl.ds(q * 32, 32)
        drows = pl.ds(pl.multiple_of(dest * TOK + q * 32, 32), 32)
        root = a == 0 and b == 0

        def add(n, _):
            cols = pl.ds(pl.multiple_of(n * 512, 512), 512)
            v = mine[drows, cols].astype(F32) + pair[j, rows, cols].astype(F32)
            for i in kids:
                v = v + rbuf[i, :, cols].astype(F32)
            if root:
                t = shbuf[3, rows, cols].astype(F32)
                for i in range(3):
                    t = t + shbuf[i, rows, cols].astype(F32)
                out_ref[rows, cols] = (hid_ref[rows, cols] + v + t).astype(BF16)
            else:
                mine[drows, cols] = v.astype(BF16)
            return 0

        lax.fori_loop(0, 4, add, 0)
        if not root:
            first, second, t = route(q)
            dim, code = (second, b) if b else (first, a)
            i = q * 15 + a * 4 + b - 1
            pltpu.make_async_remote_copy(
                mine.at[drows], rbuf.at[i], send.at[2], recv_sem.at[i],
                device_id={"exp": p.step(dim, -hop(code, t))}, device_id_type=MESH).start()

    todo = sorted((-depth(a, b), b, a, q) for q in range(4) for a in range(4) for b in range(4))

    def nodes(d):
        for dist, b, a, q in todo:
            if -dist == d:
                node(q, a, b)

    loads[3].wait()
    put(3, (2, 1, 0))
    nodes(4)
    loads[2].wait()
    put(2, (0,))
    nodes(3)
    put(2, (1, 2))
    loads[1].wait()
    put(1, (0, 1))
    nodes(2)
    loads[0].wait()
    put(0, (0,))
    nodes(1)
    for s in shares:
        s.wait_recv()
    sh_own.wait()
    for q in range(4):
        node(q, 0, 0)
    ref = pair
    pltpu.make_async_copy(ref, ref, send.at[0]).wait()
    ref = shbuf.at[pl.ds(0, 3)]
    pltpu.make_async_copy(ref, ref, send.at[1]).wait()
    pltpu.make_async_copy(rbuf, rbuf, send.at[2]).wait()


def call_return(hid, tgt, y, sh):
    return pl.pallas_call(
        kernel_return,
        out_shape=jax.ShapeDtypeStruct((TOK, D), BF16),
        in_specs=[VM, VM, ANY, ANY],
        out_specs=VM,
        scratch_shapes=[
            pltpu.VMEM((Y_ROWS, D), BF16),
            pltpu.VMEM((32 * TOK, D), BF16),
            pltpu.VMEM((16, TOK, D), BF16),
            pltpu.VMEM((60, 32, D), BF16),
            pltpu.VMEM((4, TOK, D), BF16),
            pltpu.SemaphoreType.DMA((16,)),
            pltpu.SemaphoreType.DMA((60,)),
            pltpu.SemaphoreType.DMA((4,)),
            pltpu.SemaphoreType.DMA((3,)),
            pltpu.SemaphoreType.DMA((4,)),
        ],
        compiler_params=pltpu.CompilerParams(collective_id=2, has_side_effects=True, vmem_limit_bytes=VMEM_LIMIT),
        name="give_back",
    )(hid, tgt, y, sh)


def on_device(queries, keys_then_values, residual, norm_gain, prompt_lengths, expert_ids, router_logits,
              w_gate, w_up, w_down, w_shared_gate, w_shared_up, w_shared_down, page_table):
    pad = ((0, 0), (0, SPAD - 704))
    w1 = jnp.concatenate([jnp.pad(w, pad) for w in (w_shared_gate, w_shared_up)], axis=1)
    w2 = jnp.pad(w_shared_down, pad)
    two = ((0, 0), (0, 2))
    meta = jnp.concatenate([
        jnp.pad(expert_ids.astype(F32), two, constant_values=-1.0),
        jnp.pad(router_logits, two, constant_values=-1e30)], axis=1).T
    w_all, hid, normed, log_totals, cache, tgt, wt = call_attend(
        prompt_lengths, page_table, keys_then_values, w1, meta, queries, residual, norm_gain.reshape(1, D))
    y, sh = call_moe(normed, tgt, wt, w2, w_all, w_gate, w_up, w_down)
    out = call_return(hid, tgt, y, sh)
    return out, cache.reshape(8, PAGE, 1024), log_totals


def solution(mesh):
    tok = P(("req", "exp"), None)
    ex = P("exp", None, None)
    sh = P("exp", "req")
    return jax.shard_map(
        on_device,
        mesh=mesh,
        in_specs=(tok, tok, tok, P(), P("req", None), tok, tok, ex, ex, ex, sh, sh, sh, P()),
        out_specs=(tok, P(("req", "exp"), None, None), P(None, ("req", "exp"))),
        check_vma=False,
    )
```
